32 devices in a mesh: dp: 8 (over z, x), tensor: 4 (over y, core).
Axes of the slice: x: 2, y: 2, z: 4, core: 2. Of those that a mesh axis runs over, the one named last changes fastest.
Arguments:
- patches: bfloat16 [192, 50, 1024], P(('dp', 'tensor')), may hold values from -6 to 6
- keep_index: int32 [192, 50], P(('dp', 'tensor')), may hold values from 0 to 49, each once within a row
- kept_count: int32 [192], P(('dp', 'tensor')), may hold values from 25 to 50, as said below
- norm_gain: float32 [2, 2, 1024], replicated, may hold values from 0.5 to 1.5
- shifts: float32 [2, 4, 1024], replicated, may hold values from -3 to 3
- w_qkv: bfloat16 [2, 1024, 3, 1024], P(None, None, None, 'tensor'), may hold values from -0.1875 to 0.1875
- bias_qv: float32 [2, 2, 1024], P(None, None, 'tensor'), may hold values from -3 to 3
- w_out: bfloat16 [2, 1024, 1024], P(None, 'tensor'), may hold values from -1 to 1
- w_fc1: bfloat16 [2, 1024, 4096], P(None, None, 'tensor'), may hold values from -0.1875 to 0.1875
- bias_fc1: float32 [2, 4096], P(None, 'tensor'), may hold values from -3 to 3
- w_fc2: bfloat16 [2, 4096, 1024], P(None, 'tensor'), may hold values from -0.09375 to 0.09375
- cotangent: bfloat16 [192, 50, 1024], P(('dp', 'tensor')), may hold values from -6 to 6
Outputs:
- layer_out: float32 [192, 50, 1024], P(('dp', 'tensor'))
- grad_patches: float32 [192, 50, 1024], P(('dp', 'tensor'))
- grad_gain: float32 [2, 2, 1024], replicated
- grad_shifts: float32 [2, 4, 1024], replicated
- grad_qkv: float32 [2, 1024, 3, 1024], P(None, 'dp', None, 'tensor')
- grad_bias_qv: float32 [2, 2, 1024], replicated
- grad_out: float32 [2, 1024, 1024], P(None, 'tensor', 'dp')
- grad_fc1: float32 [2, 1024, 4096], P(None, 'dp', 'tensor')
- grad_bias_fc1: float32 [2, 4096], replicated
- grad_fc2: float32 [2, 4096, 1024], P(None, 'tensor', 'dp')
The draws below stay inside these ranges and needn't reach their ends.
Inputs may be any that keep to these rules, and one draw needn't show every extreme that they name: Each row of keep_index holds every patch index once. `kept_count`: some image keeps all 50 slots and some keeps 25.
All inputs are finite; a program needn't handle non-finite values.
Results may differ from the reference program's by a relative error of at most 0.039.
Values may be sent and summed in bfloat16 or wider, within the bound.
A program may use at most 192 MiB of HBM per device.

```python
from functools import partial
import jax
import jax.numpy as jnp
from jax import lax

D = 1024
HEADS = 16
HEAD = 64
FF = 4096
LAYERS = 2
PATCHES = 50
KEEP_MIN = 25
IMG_DEV = 24
IMAGES = 192


def draw_kept_count(key, part):
    counts = jax.random.randint(key, (IMAGES,), KEEP_MIN, PATCHES + 1).astype(jnp.int32)
    counts = counts.at[0].set(PATCHES)
    return counts.at[1].set(KEEP_MIN)


def spiked(drawn, stream_key, source, target, shards_of, factor):
    def block_of(axis_at):
        return (jnp.arange(drawn.shape[axis_at]) // (drawn.shape[axis_at] // shards_of)).reshape((-1,) + (1,) * (drawn.ndim - 1 - axis_at))

    one_side = jax.random.permutation(stream_key, shards_of)[block_of(target)]
    second = (block_of(target) + shards_of // 2) % shards_of
    return jnp.where((block_of(source) == one_side) | (block_of(source) == second), factor * drawn, drawn)


def steps_of(own_key, dims, pieces, smallest, high):
    gain, own = 1.0, jax.random.fold_in(own_key, 6)
    for dim, parts in pieces:
        steps = jnp.exp(jax.random.uniform(jax.random.fold_in(own, dim), (parts,), jnp.float32, smallest / len(pieces), high / len(pieces)))
        gain = gain * jnp.repeat(steps, dims[dim] // parts).reshape([-1 if axis == dim else 1 for axis in range(len(dims))])
    return gain


def bell_draw(key, dims, width, limit, cuts=(), held_as=jnp.bfloat16):
    loudness = steps_of(key, dims, cuts, -0.22, 0.18) if cuts else 1.0
    array = jax.random.normal(key, dims, jnp.float32) * width * loudness
    return jnp.minimum(jnp.maximum(array, -limit), limit).astype(held_as)


def heavy_noise(rng, shape, scale, reach, pieces, heavy, held_as=jnp.bfloat16):
    values = scale * jax.random.normal(rng, shape, jnp.float32)
    if pieces:
        values = values * steps_of(rng, shape, pieces, -0.22, 0.18)
    return jnp.clip(spiked(values, jax.random.fold_in(rng, 3), *heavy), -reach, reach).astype(held_as)


def setup_inputs(seed: int = 0) -> dict:
    key_of = jax.random.split(jax.random.key(seed), 13)
    return {
        "patches": bell_draw(key_of[0], (IMAGES, PATCHES, D), 1.0, 6.0, ((0, 32),)),
        "keep_index": jax.vmap(lambda own: jax.random.permutation(own, PATCHES))(jax.random.split(key_of[1], IMAGES)).reshape((IMAGES, PATCHES)).astype(jnp.int32),
        "kept_count": draw_kept_count(jax.random.fold_in(key_of[12], 71), 0),
        "norm_gain": jnp.clip(1.0 + 0.1 * jax.random.normal(key_of[3], (LAYERS, 2, D), jnp.float32), 0.5, 1.5),
        "shifts": bell_draw(key_of[4], (LAYERS, 4, D), 0.5, 3.0, (), jnp.float32),
        "w_qkv": bell_draw(key_of[5], (LAYERS, D, 3, D), D ** -0.5, 0.1875, ((3, 4),)),
        "bias_qv": bell_draw(key_of[6], (LAYERS, 2, D), 0.5, 3.0, ((2, 4),), jnp.float32),
        "w_out": bell_draw(key_of[7], (LAYERS, D, D), (D // 32) ** -0.5, 1.0, ((1, 4),)),
        "w_fc1": bell_draw(key_of[8], (LAYERS, D, FF), D ** -0.5, 0.1875, ((2, 4),)),
        "bias_fc1": bell_draw(key_of[9], (LAYERS, FF), 0.5, 3.0, ((1, 4),), jnp.float32),
        "w_fc2": bell_draw(key_of[10], (LAYERS, FF, D), FF ** -0.5, 0.09375, ((1, 4),)),
        "cotangent": heavy_noise(key_of[11], (IMAGES, PATCHES, D), 1.0, 6.0, ((0, 32),), (0, 2, 32, 2.75)),
    }


@jax.custom_vjp
def low(v):
    return lax.optimization_barrier(v.astype(jnp.bfloat16)).astype(jnp.float32)

@jax.custom_vjp
def low_back(v):
    return v

def low_keep(v):
    return (low(v), None)

def low_pass(kept, grad):
    return (grad,)

def back_keep(v):
    return (v, None)

def back_low(kept, grad):
    return (low(grad),)
low.defvjp(low_keep, low_pass)
low_back.defvjp(back_keep, back_low)
EPS = 1e-06
HIGHEST = lax.Precision.HIGHEST

def norm_rows(values, scaling, offset):
    average = lax.optimization_barrier(jnp.mean(values, axis=-1, keepdims=True))
    centred = values - average
    variance = lax.optimization_barrier(jnp.mean(centred * centred, axis=-1, keepdims=True))
    return centred * lax.rsqrt(variance + EPS) * scaling + offset

def attend(queries, key_rows, value_rows, visible):
    scores = jnp.einsum('bqhe,bkhe->bhqk', queries, key_rows, precision=HIGHEST) * HEAD ** (-0.5)
    scores = low_back(scores)
    scores = jnp.where(visible[:, None, None, :], scores, -1e+30)
    probability = jax.nn.softmax(scores, axis=-1)
    return jnp.einsum('bhqk,bkhe->bqhe', low(probability), value_rows, precision=HIGHEST)

def group_forward(params, images, keep_rows, kept_rows):
    norm_gain, shifts, w_qkv, bias_qv, w_out, w_fc1, bias_fc1, w_fc2 = params
    image_total = images.shape[0]
    slot_ids = jnp.arange(PATCHES, dtype=jnp.int32)
    selector = (keep_rows[:, :, None] == slot_ids[None, None, :]).astype(jnp.float32)
    residual = jnp.einsum('bsp,bpd->bsd', selector, images, precision=HIGHEST)
    visible = slot_ids[None, :] < kept_rows[:, None]
    shape_heads = (image_total, PATCHES, HEADS, HEAD)
    for layer_no in range(LAYERS):
        normed = low(norm_rows(residual, norm_gain[layer_no, 0], shifts[layer_no, 0]))
        triple = jnp.einsum('bsd,dce->bsce', normed, w_qkv[layer_no], precision=HIGHEST)
        queries = low(low_back(triple[:, :, 0] + bias_qv[layer_no, 0]))
        key_rows = low(low_back(triple[:, :, 1]))
        value_rows = low(low_back(triple[:, :, 2] + bias_qv[layer_no, 1]))
        attended = attend(queries.reshape(shape_heads), key_rows.reshape(shape_heads), value_rows.reshape(shape_heads), visible)
        attended = low(low_back(attended.reshape(image_total, PATCHES, D)))
        branch = low_back(jnp.einsum('bse,ed->bsd', attended, w_out[layer_no], precision=HIGHEST) + shifts[layer_no, 2])
        residual = residual + branch
        normed_mlp = low(norm_rows(residual, norm_gain[layer_no, 1], shifts[layer_no, 1]))
        pre_act = low_back(jnp.einsum('bsd,df->bsf', normed_mlp, w_fc1[layer_no], precision=HIGHEST) + bias_fc1[layer_no])
        activated = low(jax.nn.gelu(pre_act, approximate=False))
        branch = low_back(jnp.einsum('bsf,fd->bsd', activated, w_fc2[layer_no], precision=HIGHEST) + shifts[layer_no, 3])
        residual = residual + branch
    return residual * visible[:, :, None].astype(residual.dtype)

def reference(patches, keep_index, kept_count, norm_gain, shifts, w_qkv, bias_qv, w_out, w_fc1, bias_fc1, w_fc2, cotangent):
    params = (norm_gain.astype(jnp.float32), shifts.astype(jnp.float32), w_qkv.astype(jnp.float32), bias_qv.astype(jnp.float32), w_out.astype(jnp.float32), w_fc1.astype(jnp.float32), bias_fc1.astype(jnp.float32), w_fc2.astype(jnp.float32))
    groups = IMAGES // IMG_DEV

    def forward(weights_in, images):
        stacked = images.reshape(groups, IMG_DEV, PATCHES, D)
        keep_groups = keep_index.reshape(groups, IMG_DEV, PATCHES)
        counts = kept_count.reshape(groups, IMG_DEV)
        runner = jax.checkpoint(partial(group_forward, weights_in))

        def advance(carried, group_item):
            return (carried, runner(group_item[0], group_item[1], group_item[2]))
        unused, outputs = lax.scan(advance, jnp.zeros((), jnp.float32), (stacked, keep_groups, counts))
        return outputs.reshape(IMAGES, PATCHES, D)
    layer_out, pullback = jax.vjp(forward, params, patches.astype(jnp.float32))
    grad_params, grad_patches = pullback(cotangent.astype(jnp.float32))
    return (layer_out, grad_patches, grad_params[0], grad_params[1], grad_params[2], grad_params[3], grad_params[4], grad_params[5], grad_params[6], grad_params[7])
```

```python
from functools import partial

import jax
import jax.numpy as jnp
from jax import lax
from jax.sharding import PartitionSpec as P

D = 1024
HEAD = 64
FF = 4096
LAYERS = 2
PATCHES = 50


EPS = 1e-06
HIGHEST = lax.Precision.HIGHEST


def norm_rows(values, scaling, offset):
    average = jnp.mean(values, axis=-1, keepdims=True)
    centred = values - average
    variance = jnp.mean(centred * centred, axis=-1, keepdims=True)
    return centred * lax.rsqrt(variance + EPS) * scaling + offset


def spread(rows, counts):
    return (
        lax.all_gather(rows, "tensor", axis=0, tiled=True),
        lax.all_gather(counts, "tensor", axis=0, tiled=True),
    )


def collect(partial_rows):
    return lax.psum_scatter(
        partial_rows.astype(jnp.bfloat16), "tensor", scatter_dimension=0, tiled=True
    ).astype(jnp.float32)


def spread_grad(rows):
    return lax.all_gather(rows, "tensor", axis=0, tiled=True)


def collect_grad(partial_rows):
    return lax.psum_scatter(
        partial_rows.astype(jnp.bfloat16), "tensor", scatter_dimension=0, tiled=True
    ).astype(jnp.float32)


def collect_weight(partial_grad, split_dim):
    return lax.psum_scatter(
        partial_grad.astype(jnp.bfloat16), "dp", scatter_dimension=split_dim, tiled=True
    ).astype(jnp.float32)


def score_block(queries, key_rows, visible, score_scale):
    scores = (
        jnp.einsum("bqhe,bkhe->bhqk", queries, key_rows, preferred_element_type=jnp.float32)
        * score_scale
    )
    return jnp.where(visible[:, None, None, :], scores, -1e30)


def local(
    patches,
    keep_index,
    kept_count,
    norm_gain,
    shifts,
    w_qkv,
    bias_qv,
    w_out,
    w_fc1,
    bias_fc1,
    w_fc2,
    cotangent,
):
    width_local = w_qkv.shape[-1]
    hidden_local = w_fc1.shape[-1]
    heads_local = width_local // HEAD
    score_scale = HEAD ** (-0.5)
    slot_ids = jnp.arange(PATCHES, dtype=jnp.int32)
    selector = (keep_index[:, :, None] == slot_ids[None, None, :]).astype(jnp.bfloat16)
    residual = jnp.einsum("bsp,bpd->bsd", selector, patches, preferred_element_type=jnp.float32)
    stored = []
    visible = None
    shape_heads = None
    image_total = 0
    for layer_no in range(LAYERS):
        normed_own = norm_rows(residual, norm_gain[layer_no, 0], shifts[layer_no, 0]).astype(
            jnp.bfloat16
        )
        normed, counts_all = spread(normed_own, kept_count)
        visible = slot_ids[None, :] < counts_all[:, None]
        image_total = normed.shape[0]
        shape_heads = (image_total, PATCHES, heads_local, HEAD)
        triple = jnp.einsum(
            "bsd,dce->bsce", normed, w_qkv[layer_no], preferred_element_type=jnp.float32
        )
        queries = (triple[:, :, 0] + bias_qv[layer_no, 0]).astype(jnp.bfloat16).reshape(shape_heads)
        key_rows = triple[:, :, 1].astype(jnp.bfloat16).reshape(shape_heads)
        value_rows = (
            (triple[:, :, 2] + bias_qv[layer_no, 1]).astype(jnp.bfloat16).reshape(shape_heads)
        )
        scores = score_block(queries, key_rows, visible, score_scale)
        log_total = jax.nn.logsumexp(scores, axis=-1, keepdims=True)
        attn_weights = jnp.exp(scores - log_total).astype(jnp.bfloat16)
        attended = jnp.einsum(
            "bhqk,bkhe->bqhe", attn_weights, value_rows, preferred_element_type=jnp.float32
        )
        attended = attended.reshape(image_total, PATCHES, width_local).astype(jnp.bfloat16)
        mixed = collect(
            jnp.einsum("bse,ed->bsd", attended, w_out[layer_no], preferred_element_type=jnp.float32)
        )
        middle = residual + mixed + shifts[layer_no, 2]
        normed_mid = norm_rows(middle, norm_gain[layer_no, 1], shifts[layer_no, 1]).astype(
            jnp.bfloat16
        )
        normed_mlp, counts_again = spread(normed_mid, kept_count)
        pre_act = (
            jnp.einsum(
                "bsd,df->bsf", normed_mlp, w_fc1[layer_no], preferred_element_type=jnp.float32
            )
            + bias_fc1[layer_no]
        )
        activated = jax.nn.gelu(pre_act, approximate=False).astype(jnp.bfloat16)
        stored.append(
            (
                residual,
                normed,
                queries,
                key_rows,
                value_rows,
                log_total,
                attended,
                middle,
                normed_mlp,
                pre_act,
                activated,
            )
        )
        mlp_part = collect(
            jnp.einsum(
                "bsf,fd->bsd", activated, w_fc2[layer_no], preferred_element_type=jnp.float32
            )
        )
        residual = middle + mlp_part + shifts[layer_no, 3]
    own_mask = (slot_ids[None, :] < kept_count[:, None]).astype(jnp.float32)[:, :, None]
    layer_out = residual * own_mask
    gradient = cotangent.astype(jnp.float32) * own_mask
    offset_at = lax.axis_index("tensor") * width_local
    hidden_at = lax.axis_index("tensor") * hidden_local
    gain_terms = []
    shift_terms = []
    bias_qv_terms = []
    bias_fc1_terms = []
    weight_terms = []
    for layer_no in reversed(range(LAYERS)):
        (
            residual_in,
            normed,
            queries,
            key_rows,
            value_rows,
            log_total,
            attended,
            middle,
            normed_mlp,
            pre_act,
            activated,
        ) = stored[layer_no]
        grad_mlp = gradient.astype(jnp.bfloat16)
        shift_fc2 = jnp.sum(grad_mlp.astype(jnp.float32), axis=(0, 1))
        grad_rows = spread_grad(grad_mlp)
        d_fc2 = jnp.einsum("bsf,bsd->fd", activated, grad_rows, preferred_element_type=jnp.float32)
        d_act = jnp.einsum(
            "bsd,fd->bsf", grad_rows, w_fc2[layer_no], preferred_element_type=jnp.float32
        )
        gelu_pull = jax.vjp(partial(jax.nn.gelu, approximate=False), pre_act)[1]
        d_pre = gelu_pull(d_act)[0].astype(jnp.bfloat16)
        d_bias_fc1 = jnp.sum(d_pre.astype(jnp.float32), axis=(0, 1))
        d_fc1 = jnp.einsum("bsd,bsf->df", normed_mlp, d_pre, preferred_element_type=jnp.float32)
        d_normed = collect_grad(
            jnp.einsum("bsf,df->bsd", d_pre, w_fc1[layer_no], preferred_element_type=jnp.float32)
        )
        norm_pull = jax.vjp(norm_rows, middle, norm_gain[layer_no, 1], shifts[layer_no, 1])[1]
        d_middle, d_gain_mlp, d_shift_mlp = norm_pull(d_normed)
        gradient = gradient + d_middle
        grad_attn = gradient.astype(jnp.bfloat16)
        shift_attn = jnp.sum(grad_attn.astype(jnp.float32), axis=(0, 1))
        grad_rows = spread_grad(grad_attn)
        d_out = jnp.einsum("bse,bsd->ed", attended, grad_rows, preferred_element_type=jnp.float32)
        d_attended = jnp.einsum(
            "bsd,ed->bse", grad_rows, w_out[layer_no], preferred_element_type=jnp.float32
        )
        d_attended = d_attended.astype(jnp.bfloat16).reshape(shape_heads)
        scores = score_block(queries, key_rows, visible, score_scale)
        probability = jnp.exp(scores - log_total)
        d_values = jnp.einsum(
            "bhqk,bqhe->bkhe",
            probability.astype(jnp.bfloat16),
            d_attended,
            preferred_element_type=jnp.float32,
        )
        d_prob = jnp.einsum(
            "bqhe,bkhe->bhqk", d_attended, value_rows, preferred_element_type=jnp.float32
        )
        centre_term = jnp.sum(probability * d_prob, axis=-1, keepdims=True)
        d_scores = (probability * (d_prob - centre_term)).astype(jnp.bfloat16)
        d_queries = (
            jnp.einsum("bhqk,bkhe->bqhe", d_scores, key_rows, preferred_element_type=jnp.float32)
            * score_scale
        )
        d_keys = (
            jnp.einsum("bhqk,bqhe->bkhe", d_scores, queries, preferred_element_type=jnp.float32)
            * score_scale
        )
        d_triple = jnp.stack([d_queries, d_keys, d_values], axis=2)
        d_triple = d_triple.reshape(image_total, PATCHES, 3, width_local).astype(jnp.bfloat16)
        d_bias_qv = jnp.sum(d_triple[:, :, 0::2].astype(jnp.float32), axis=(0, 1))
        d_qkv = jnp.einsum("bsd,bsce->dce", normed, d_triple, preferred_element_type=jnp.float32)
        d_normed = collect_grad(
            jnp.einsum(
                "bsce,dce->bsd", d_triple, w_qkv[layer_no], preferred_element_type=jnp.float32
            )
        )
        norm_pull = jax.vjp(norm_rows, residual_in, norm_gain[layer_no, 0], shifts[layer_no, 0])[1]
        d_input, d_gain_attn, d_shift_attn = norm_pull(d_normed)
        gradient = gradient + d_input
        gain_terms.insert(0, jnp.stack([d_gain_attn, d_gain_mlp]))
        shift_terms.insert(0, jnp.stack([d_shift_attn, d_shift_mlp, shift_attn, shift_fc2]))
        bias_qv_terms.insert(0, d_bias_qv)
        bias_fc1_terms.insert(0, d_bias_fc1)
        weight_terms.insert(
            0,
            (
                collect_weight(d_qkv, 0),
                collect_weight(d_out, 1),
                collect_weight(d_fc1, 0),
                collect_weight(d_fc2, 1),
            ),
        )
    grad_qkv, grad_out, grad_fc1, grad_fc2 = (
        jnp.stack([entry[k] for entry in weight_terms]) for k in range(4)
    )
    zero_at = offset_at * 0
    qv_full = lax.dynamic_update_slice(
        jnp.zeros((LAYERS, 2, D), jnp.float32),
        jnp.stack(bias_qv_terms),
        (zero_at, zero_at, offset_at),
    )
    fc1_full = lax.dynamic_update_slice(
        jnp.zeros((LAYERS, FF), jnp.float32), jnp.stack(bias_fc1_terms), (zero_at, hidden_at)
    )
    grad_gain, grad_shifts, grad_bias_qv, grad_bias_fc1 = lax.psum(
        (jnp.stack(gain_terms), jnp.stack(shift_terms), qv_full, fc1_full), ("dp", "tensor")
    )
    grad_patches = jnp.einsum(
        "bsp,bsd->bpd", selector.astype(jnp.float32), gradient, precision=HIGHEST
    )
    return (
        layer_out,
        grad_patches,
        grad_gain,
        grad_shifts,
        grad_qkv,
        grad_bias_qv,
        grad_out,
        grad_fc1,
        grad_bias_fc1,
        grad_fc2,
    )


def solution(mesh):
    in_specs = (
        P(("dp", "tensor"), None, None),
        P(("dp", "tensor"), None),
        P(("dp", "tensor")),
        P(),
        P(),
        P(None, None, None, "tensor"),
        P(None, None, "tensor"),
        P(None, "tensor", None),
        P(None, None, "tensor"),
        P(None, "tensor"),
        P(None, "tensor", None),
        P(("dp", "tensor"), None, None),
    )
    out_specs = (
        P(("dp", "tensor"), None, None),
        P(("dp", "tensor"), None, None),
        P(),
        P(),
        P(None, "dp", None, "tensor"),
        P(),
        P(None, "tensor", "dp"),
        P(None, "dp", "tensor"),
        P(),
        P(None, "tensor", "dp"),
    )
    return jax.shard_map(local, mesh=mesh, in_specs=in_specs, out_specs=out_specs, check_vma=False)
```

```python
from functools import partial

import jax
import jax.numpy as jnp
from jax import lax
from jax.experimental import pallas as pl
from jax.experimental.pallas import tpu as pltpu
from jax.sharding import PartitionSpec as P

D = 1024
HEAD = 64
FF = 4096
LAYERS = 2
PATCHES = 50
EPS = 1e-06
HIGHEST = lax.Precision.HIGHEST
F32 = jnp.float32
BF16 = jnp.bfloat16

GROUPS = 2
ROWS = 160
LIVE = 150
COLS = 128
SCALE = HEAD ** (-0.5)


def dot(a, b, lhs=1, rhs=0):
    return lax.dot_general(a, b, (((lhs,), (rhs,)), ((), ())), preferred_element_type=F32)


def remote(src, dst, send, recv, peer):
    return pltpu.make_async_remote_copy(
        src_ref=src,
        dst_ref=dst,
        send_sem=send,
        recv_sem=recv,
        device_id={"tensor": peer},
        device_id_type=pl.DeviceIdType.MESH,
    )


def norm_parts(values):
    average = jnp.mean(values, axis=-1, keepdims=True)
    centred = values - average
    variance = jnp.mean(centred * centred, axis=-1, keepdims=True)
    scale = lax.rsqrt(variance + EPS)
    return centred * scale, scale


def head_mask(h, width):
    lane = lax.broadcasted_iota(jnp.int32, (1, width), 1)
    return (lane // HEAD == h).astype(F32).astype(BF16)


class Exchange:
    def __init__(self, x_own, gath, part, bufs, sems):
        self.x_own, self.gath, self.part = x_own, gath, part
        self.out_po, self.out_pd, self.out_y, self.in_po, self.in_pd, self.in_y = bufs
        self.sem = sems
        me = lax.axis_index("tensor")
        self.me = me
        self.mate = me + 1 - 2 * (me % 2)
        self.far = (me + 2) % 4
        self.diag = (self.mate + 2) % 4

    def barrier(self):
        sem = pltpu.get_barrier_semaphore()
        for peer in (self.mate, self.far):
            pl.semaphore_signal(
                sem, inc=1, device_id={"tensor": peer}, device_id_type=pl.DeviceIdType.MESH
            )
        pl.semaphore_wait(sem, 2)

    def copy(self, kind, g):
        s = self.sem
        own = GROUPS * self.me + g
        if kind == 0:
            src, dst, peer = self.x_own.at[g], self.gath.at[own], self.far
        elif kind == 1:
            src, dst, peer = self.x_own.at[g], self.gath.at[own], self.mate
        elif kind == 2:
            slot = GROUPS * self.far + g
            src, dst, peer = self.gath.at[slot], self.gath.at[slot], self.mate
        elif kind == 3:
            src, dst, peer = self.out_po.at[g], self.in_po.at[g], self.mate
        elif kind == 4:
            src, dst, peer = self.out_pd.at[g], self.in_pd.at[g], self.mate
        else:
            src, dst, peer = self.out_y.at[g], self.in_y.at[g], self.far
        return remote(src, dst, s.at[0, kind, g], s.at[1, kind, g], peer)

    def local(self, g):
        return pltpu.make_async_copy(
            self.x_own.at[g], self.gath.at[GROUPS * self.me + g], self.sem.at[0, 6, g]
        )

    def begin(self):
        self.barrier()
        for g in range(GROUPS):
            self.copy(0, g).start()
            self.copy(1, g).start()
            self.local(g).start()

    def slot(self, i):
        owner = jnp.where(
            i < 2, self.me, jnp.where(i < 4, self.mate, jnp.where(i % 2 == 0, self.far, self.diag))
        )
        g = jnp.where(i < 4, i % 2, (i - 4) // 2)
        return GROUPS * owner + g

    def before(self, i):
        for g in range(GROUPS):

            @pl.when(i == g)
            def _():
                self.local(g).wait()

            @pl.when(i == 2 + g)
            def _():
                self.copy(1, g).wait_recv()

            @pl.when(i == 4 + 2 * g)
            def _():
                self.copy(0, g).wait_recv()
                self.copy(2, g).start()

            @pl.when(i == 5 + 2 * g)
            def _():
                self.copy(2, g).wait_recv()

    def after(self, i):
        for g in range(GROUPS):

            @pl.when(i == 2 + g)
            def _():
                self.out_po[g] = self.part[2 + g].astype(BF16)
                self.copy(3, g).start()

            @pl.when(i == 5 + 2 * g)
            def _():
                self.out_pd[g] = self.part[5 + 2 * g].astype(BF16)
                self.copy(4, g).start()
                self.copy(4, g).wait_recv()
                self.out_y[g] = (self.part[4 + 2 * g] + self.in_pd[g].astype(F32)).astype(BF16)
                self.copy(5, g).start()

    def total(self, g):
        self.copy(3, g).wait_recv()
        self.copy(5, g).wait_recv()
        return self.part[g] + self.in_po[g].astype(F32) + self.in_y[g].astype(F32)

    def end(self):
        for g in range(GROUPS):
            for kind in range(6):
                self.copy(kind, g).wait_send()


def exchange_scratch():
    return [
        pltpu.VMEM((8, ROWS, D), BF16),
        pltpu.VMEM((8, ROWS, D), F32),
    ] + [pltpu.VMEM((GROUPS, ROWS, D), BF16)] * 6 + [pltpu.SemaphoreType.DMA((2, 7, GROUPS))]


class Moves:
    def __init__(self, sems):
        self.sems = sems

    def load(self, n, src, dst):
        return pltpu.make_async_copy(src, dst, self.sems.at[n])


def keep_pad(old, new):
    row = lax.broadcasted_iota(jnp.int32, (ROWS, D), 0)
    return jnp.where(row >= LIVE, old.astype(F32), new)


def attend_kernel(
    x_own, norm2, shift_a, shift_n, bias, resid_h, wqkv_h, wout_h,
    gath_h, qkv_h, prob_h, att_h, middle, next_own,
    gath, part, out_po, out_pd, out_y, in_po, in_pd, in_y, ex_sem,
    resid, wqkv, wout, qkv, prob, att, load_sem, save_sem,
):
    ex = Exchange(x_own, gath, part, (out_po, out_pd, out_y, in_po, in_pd, in_y), ex_sem)
    width = wout.shape[0]
    loads = Moves(load_sem)
    for n, pair in enumerate(((wqkv_h, wqkv), (wout_h, wout), (resid_h, resid))):
        loads.load(n, *pair).start()
    ex.begin()
    loads.load(0, wqkv_h, wqkv).wait()
    loads.load(1, wout_h, wout).wait()
    pairs = ((gath, gath_h), (qkv, qkv_h), (prob, prob_h), (att, att_h))

    def saves(slot):
        return [
            pltpu.make_async_copy(a.at[slot], b.at[slot], save_sem.at[n, slot])
            for n, (a, b) in enumerate(pairs)
        ]

    def step(i, _):
        ex.before(i)
        slot = ex.slot(i)
        x = gath[slot]
        triple = dot(x, wqkv[...])
        q = (triple[:, :width] + bias[0:1]).astype(BF16)
        k = triple[:, width : 2 * width].astype(BF16)
        v = (triple[:, 2 * width :] + bias[1:2]).astype(BF16)
        qkv[slot, :, 0:width] = q
        qkv[slot, :, width : 2 * width] = k
        qkv[slot, :, 2 * width :] = v
        counts = gath[slot, ROWS - 16 : ROWS, 0:256][:, 0:ROWS].astype(F32)
        lane = lax.broadcasted_iota(jnp.int32, (1, ROWS), 1)
        image = lane // PATCHES
        count = jnp.where(
            image == 0, counts[6:7], jnp.where(image == 1, counts[7:8], counts[8:9])
        )
        fits = (lane - image * PATCHES).astype(F32) < count
        row = lax.broadcasted_iota(jnp.int32, (ROWS, ROWS), 0)
        col = lax.broadcasted_iota(jnp.int32, (ROWS, ROWS), 1)
        same = jnp.minimum(row // PATCHES, 2) == col // PATCHES
        veil = jnp.where(same, 0.0, -1e30) + jnp.where(fits, 0.0, -1e30)
        mixed = jnp.zeros((ROWS, width), F32)
        for h in range(width // HEAD):
            mask = head_mask(h, width)
            scores = dot(q * mask, k, 1, 1) * SCALE + veil
            peak = jnp.max(scores, axis=-1, keepdims=True)
            raised = jnp.exp(scores - peak)
            weight = raised * (1.0 / jnp.sum(raised, axis=-1, keepdims=True))
            rounded = weight.astype(BF16)
            prob[slot, h * ROWS : (h + 1) * ROWS] = rounded
            mixed = mixed + dot(rounded, v * mask)
        mixed = mixed.astype(BF16)
        att[slot] = mixed
        part[i] = dot(mixed, wout[...])
        for copy in saves(slot):
            copy.start()
        ex.after(i)
        return 0

    lax.fori_loop(0, 8, step, 0)
    loads.load(2, resid_h, resid).wait()
    for g in range(GROUPS):
        mid = resid[g] + ex.total(g) + shift_a[...]
        middle[g] = mid
        unit, _ = norm_parts(mid)
        next_own[g] = keep_pad(x_own[g], unit * norm2[...] + shift_n[...]).astype(BF16)
    ex.end()

    def drain(slot, _):
        for copy in saves(slot):
            copy.wait()
        return 0

    lax.fori_loop(0, 8, drain, 0)


def erf_parts(pre):
    cdf = 0.5 * (1.0 + lax.erf(pre * (0.5 ** 0.5)))
    pdf = jnp.exp(-0.5 * pre * pre) * 0.3989422804014327
    return cdf, pdf


def mlp_kernel(
    x_own, gain_n, shift_a, shift_n, bias, middle_h, w1_h, w2_h,
    gath_h, act_h, slope_h, resid_out, next_own,
    gath, part, out_po, out_pd, out_y, in_po, in_pd, in_y, ex_sem,
    middle, w1, w2, act, slope, load_sem, save_sem,
):
    ex = Exchange(x_own, gath, part, (out_po, out_pd, out_y, in_po, in_pd, in_y), ex_sem)
    hidden = w1.shape[1]
    loads = Moves(load_sem)
    for n, pair in enumerate(((w1_h, w1), (w2_h, w2), (middle_h, middle))):
        loads.load(n, *pair).start()
    ex.begin()
    loads.load(0, w1_h, w1).wait()
    loads.load(1, w2_h, w2).wait()
    pairs = ((gath, gath_h), (act, act_h), (slope, slope_h))

    def saves(slot):
        return [
            pltpu.make_async_copy(a.at[slot], b.at[slot], save_sem.at[n, slot])
            for n, (a, b) in enumerate(pairs)
        ]

    def step(i, _):
        ex.before(i)
        slot = ex.slot(i)
        x = gath[slot]
        for block in range(hidden // 256):
            at = slice(block * 256, block * 256 + 256)
            pre = dot(x, w1[:, at]) + bias[:, at]
            cdf, pdf = erf_parts(pre)
            act[slot, :, at] = (pre * cdf).astype(BF16)
            slope[slot, :, at] = (cdf + pre * pdf).astype(BF16)
        part[i] = dot(act[slot], w2[...])
        for copy in saves(slot):
            copy.start()
        ex.after(i)
        return 0

    lax.fori_loop(0, 8, step, 0)
    loads.load(2, middle_h, middle).wait()
    for g in range(GROUPS):
        res = middle[g] + ex.total(g) + shift_a[...]
        resid_out[g] = res
        unit, _ = norm_parts(res)
        next_own[g] = keep_pad(x_own[g], unit * gain_n[...] + shift_n[...]).astype(BF16)
    ex.end()

    def drain(slot, _):
        for copy in saves(slot):
            copy.wait()
        return 0

    lax.fori_loop(0, 8, drain, 0)


VM = pl.BlockSpec(memory_space=pltpu.VMEM)
HB = pl.BlockSpec(memory_space=pl.ANY)


def sds(shape, dtype):
    return jax.ShapeDtypeStruct(shape, dtype)


def params(n):
    return pltpu.CompilerParams(
        collective_id=n, has_side_effects=True, vmem_limit_bytes=60 * 1024 * 1024
    )


def attend_half(x_own, gain, shift_a, shift_n, bias, resid, wqkv, wout):
    width = wout.shape[0]
    heads = width // HEAD
    return pl.pallas_call(
        attend_kernel,
        out_shape=(
            sds((8, ROWS, D), BF16),
            sds((8, ROWS, 3 * width), BF16),
            sds((8, heads * ROWS, ROWS), BF16),
            sds((8, ROWS, width), BF16),
            sds((GROUPS, ROWS, D), F32),
            sds((GROUPS, ROWS, D), BF16),
        ),
        in_specs=[VM] * 5 + [HB] * 3,
        out_specs=(HB, HB, HB, HB, VM, VM),
        scratch_shapes=exchange_scratch()
        + [
            pltpu.VMEM((GROUPS, ROWS, D), F32),
            pltpu.VMEM((D, 3 * width), BF16),
            pltpu.VMEM((width, D), BF16),
            pltpu.VMEM((8, ROWS, 3 * width), BF16),
            pltpu.VMEM((8, heads * ROWS, ROWS), BF16),
            pltpu.VMEM((8, ROWS, width), BF16),
            pltpu.SemaphoreType.DMA((3,)),
            pltpu.SemaphoreType.DMA((4, 8)),
        ],
        compiler_params=params(1),
    )(x_own, gain, shift_a, shift_n, bias, resid, wqkv, wout)


def mlp_half(x_own, gain, shift_a, shift_n, bias, middle, w1, w2):
    hidden = w1.shape[1]
    return pl.pallas_call(
        mlp_kernel,
        out_shape=(
            sds((8, ROWS, D), BF16),
            sds((8, ROWS, hidden), BF16),
            sds((8, ROWS, hidden), BF16),
            sds((GROUPS, ROWS, D), F32),
            sds((GROUPS, ROWS, D), BF16),
        ),
        in_specs=[VM] * 5 + [HB] * 3,
        out_specs=(HB, HB, HB, VM, VM),
        scratch_shapes=exchange_scratch()
        + [
            pltpu.VMEM((GROUPS, ROWS, D), F32),
            pltpu.VMEM((D, hidden), BF16),
            pltpu.VMEM((hidden, D), BF16),
            pltpu.VMEM((8, ROWS, hidden), BF16),
            pltpu.VMEM((8, ROWS, hidden), BF16),
            pltpu.SemaphoreType.DMA((3,)),
            pltpu.SemaphoreType.DMA((3, 8)),
        ],
        compiler_params=params(2),
    )(x_own, gain, shift_a, shift_n, bias, middle, w1, w2)


def column_sums(values):
    return jnp.sum(values, axis=0, keepdims=True)


def back_through_norm(ex, g, gradient, source, gain, grad_out, next_own, sums):
    moved = ex.total(g)
    unit, scale = norm_parts(source[g])
    scaled = moved * gain[...]
    lean = jnp.mean(scaled, axis=-1, keepdims=True)
    tilt = jnp.mean(scaled * unit, axis=-1, keepdims=True)
    grad = gradient[g] + scale * (scaled - lean - unit * tilt)
    rounded = grad.astype(BF16)
    grad_out[g] = grad
    next_own[g] = rounded
    rows = (column_sums(moved * unit), column_sums(moved), column_sums(rounded.astype(F32)))
    for n, row in enumerate(rows):
        sums[n : n + 1] = row if g == 0 else sums[n : n + 1] + row


def weight_blocks(left, right, rows_out, cols_left, cols_right, cols_out, copies):
    flat = 8 * ROWS

    def block(n, _):
        at = pl.ds(pl.multiple_of(n * 256, 256), 256)
        some = left[:, :, at].reshape(flat, 256)
        rows_out[at, :] = dot(some, right[...].reshape(flat, right.shape[-1]), 0, 0).astype(BF16)
        some = cols_right[:, :, at].reshape(flat, 256)
        wide = dot(cols_left[...].reshape(flat, cols_left.shape[-1]), some, 0, 0).astype(BF16)
        cols_out[2 * n] = wide[:, :COLS]
        cols_out[2 * n + 1] = wide[:, COLS:]
        for copy in copies(n):
            copy.start()
        return 0

    lax.fori_loop(0, D // 256, block, 0)


def weight_copies(rows_out, rows_h, cols_out, cols_h, sems):
    def copies(n):
        at = pl.ds(pl.multiple_of(n * 256, 256), 256)
        two = pl.ds(2 * n, 2)
        return (
            pltpu.make_async_copy(rows_out.at[at], rows_h.at[at], sems.at[0, n]),
            pltpu.make_async_copy(cols_out.at[two], cols_h.at[two], sems.at[1, n]),
        )

    return copies


def drain_weights(copies):
    def drain(n, _):
        for copy in copies(n):
            copy.wait()
        return 0

    lax.fori_loop(0, D // 256, drain, 0)


def mlp_back_kernel(
    x_own, gain, gradient_h, middle_h, w1_h, w2_h, act_h, slope_h, norm_h,
    grad_out, next_own, sums, bias_sum, rows_h, cols_h,
    gath, part, out_po, out_pd, out_y, in_po, in_pd, in_y, ex_sem,
    gradient, middle, w1, w2, act, slope, norm, pre, rows_out, cols_out, load_sem, save_sem,
):
    ex = Exchange(x_own, gath, part, (out_po, out_pd, out_y, in_po, in_pd, in_y), ex_sem)
    hidden = w1.shape[1]
    loads = [
        pltpu.make_async_copy(a, b, load_sem.at[n])
        for n, (a, b) in enumerate(
            (
                (w2_h, w2),
                (slope_h, slope),
                (w1_h, w1),
                (act_h, act),
                (norm_h, norm),
                (gradient_h, gradient),
                (middle_h, middle),
            )
        )
    ]
    for copy in loads:
        copy.start()
    ex.begin()
    for copy in loads[:3]:
        copy.wait()

    def step(i, _):
        ex.before(i)
        slot = ex.slot(i)
        grad = gath[slot]
        for block in range(hidden // 256):
            at = slice(block * 256, block * 256 + 256)
            d_act = dot(grad, w2[at, :], 1, 1)
            pre[slot, :, at] = (d_act * slope[slot, :, at].astype(F32)).astype(BF16)
        part[i] = dot(pre[slot], w1[...], 1, 1)
        ex.after(i)
        return 0

    lax.fori_loop(0, 8, step, 0)
    for copy in loads[3:]:
        copy.wait()
    copies = weight_copies(rows_out, rows_h, cols_out, cols_h, save_sem)
    weight_blocks(norm, pre, rows_out, act, gath, cols_out, copies)
    ones = jnp.ones((8, 8 * ROWS), BF16)
    bias_sum[...] = dot(ones, pre[...].reshape(8 * ROWS, hidden))
    for g in range(GROUPS):
        back_through_norm(ex, g, gradient, middle, gain, grad_out, next_own, sums)
    ex.end()
    drain_weights(copies)


def attend_back_kernel(
    x_own, gain, gradient_h, resid_h, wqkv_h, wout_h, qkv_h, prob_h, att_h, norm_h,
    grad_out, next_own, sums, bias_sum, rows_h, cols_h,
    gath, part, out_po, out_pd, out_y, in_po, in_pd, in_y, ex_sem,
    gradient, resid, wqkv, wout, qkv, prob, att, norm, triple, rows_out, cols_out,
    load_sem, save_sem,
):
    ex = Exchange(x_own, gath, part, (out_po, out_pd, out_y, in_po, in_pd, in_y), ex_sem)
    width = wout.shape[0]
    loads = [
        pltpu.make_async_copy(a, b, load_sem.at[n])
        for n, (a, b) in enumerate(
            (
                (wout_h, wout),
                (qkv_h, qkv),
                (prob_h, prob),
                (wqkv_h, wqkv),
                (att_h, att),
                (norm_h, norm),
                (gradient_h, gradient),
                (resid_h, resid),
            )
        )
    ]
    for copy in loads:
        copy.start()
    ex.begin()
    for copy in loads[:4]:
        copy.wait()

    def step(i, _):
        ex.before(i)
        slot = ex.slot(i)
        grad = gath[slot]
        d_att = dot(grad, wout[...], 1, 1).astype(BF16)
        q = qkv[slot, :, 0:width]
        k = qkv[slot, :, width : 2 * width]
        v = qkv[slot, :, 2 * width :]
        d_q = jnp.zeros((ROWS, width), F32)
        d_k = jnp.zeros((ROWS, width), F32)
        d_v = jnp.zeros((ROWS, width), F32)
        for h in range(width // HEAD):
            mask = head_mask(h, width)
            d_one = d_att * mask
            rounded = prob[slot, h * ROWS : (h + 1) * ROWS]
            weight = rounded.astype(F32)
            d_prob = dot(d_one, v, 1, 1)
            centre = jnp.sum(weight * d_prob, axis=-1, keepdims=True)
            d_scores = (weight * (d_prob - centre)).astype(BF16)
            d_q = d_q + dot(d_scores, k * mask)
            d_k = d_k + dot(d_scores, q * mask, 0, 0)
            d_v = d_v + dot(rounded, d_one, 0, 0)
        triple[slot, :, 0:width] = (d_q * SCALE).astype(BF16)
        triple[slot, :, width : 2 * width] = (d_k * SCALE).astype(BF16)
        triple[slot, :, 2 * width :] = d_v.astype(BF16)
        part[i] = dot(triple[slot], wqkv[...], 1, 1)
        ex.after(i)
        return 0

    lax.fori_loop(0, 8, step, 0)
    for copy in loads[4:]:
        copy.wait()
    copies = weight_copies(rows_out, rows_h, cols_out, cols_h, save_sem)
    weight_blocks(norm, triple, rows_out, att, gath, cols_out, copies)
    ones = jnp.ones((8, 8 * ROWS), BF16)
    bias_sum[...] = dot(ones, triple[...].reshape(8 * ROWS, 3 * width))
    for g in range(GROUPS):
        back_through_norm(ex, g, gradient, resid, gain, grad_out, next_own, sums)
    ex.end()
    drain_weights(copies)


def back_outs(rows, cols):
    return (
        sds((GROUPS, ROWS, D), F32),
        sds((GROUPS, ROWS, D), BF16),
        sds((8, D), F32),
        sds((8, rows), F32),
        sds((D, rows), BF16),
        sds((D // COLS, cols, COLS), BF16),
    )


def back_scratch(rows, cols, loads):
    return [
        pltpu.VMEM((D, rows), BF16),
        pltpu.VMEM((D // COLS, cols, COLS), BF16),
        pltpu.SemaphoreType.DMA((loads,)),
        pltpu.SemaphoreType.DMA((2, D // 256)),
    ]


def mlp_back(x_own, gain, gradient, middle, w1, w2, act, slope, norm):
    hidden = w1.shape[1]
    wide = pltpu.VMEM((8, ROWS, hidden), BF16)
    return pl.pallas_call(
        mlp_back_kernel,
        out_shape=back_outs(hidden, hidden),
        in_specs=[VM] * 2 + [HB] * 7,
        out_specs=(VM, VM, VM, VM, HB, HB),
        scratch_shapes=exchange_scratch()
        + [
            pltpu.VMEM((GROUPS, ROWS, D), F32),
            pltpu.VMEM((GROUPS, ROWS, D), F32),
            pltpu.VMEM((D, hidden), BF16),
            pltpu.VMEM((hidden, D), BF16),
            wide,
            wide,
            pltpu.VMEM((8, ROWS, D), BF16),
            wide,
        ]
        + back_scratch(hidden, hidden, 7),
        compiler_params=params(3),
    )(x_own, gain, gradient, middle, w1, w2, act, slope, norm)


def attend_back(x_own, gain, gradient, resid, wqkv, wout, qkv, prob, att, norm):
    width = wout.shape[0]
    heads = width // HEAD
    return pl.pallas_call(
        attend_back_kernel,
        out_shape=back_outs(3 * width, width),
        in_specs=[VM] * 2 + [HB] * 8,
        out_specs=(VM, VM, VM, VM, HB, HB),
        scratch_shapes=exchange_scratch()
        + [
            pltpu.VMEM((GROUPS, ROWS, D), F32),
            pltpu.VMEM((GROUPS, ROWS, D), F32),
            pltpu.VMEM((D, 3 * width), BF16),
            pltpu.VMEM((width, D), BF16),
            pltpu.VMEM((8, ROWS, 3 * width), BF16),
            pltpu.VMEM((8, heads * ROWS, ROWS), BF16),
            pltpu.VMEM((8, ROWS, width), BF16),
            pltpu.VMEM((8, ROWS, D), BF16),
            pltpu.VMEM((8, ROWS, 3 * width), BF16),
        ]
        + back_scratch(3 * width, width, 8),
        compiler_params=params(4),
    )(x_own, gain, gradient, resid, wqkv, wout, qkv, prob, att, norm)


def to_groups(array, dtype):
    images = array.shape[0] // GROUPS
    rows = array.reshape(GROUPS, images * PATCHES, D)
    return jnp.pad(rows, ((0, 0), (0, ROWS - images * PATCHES), (0, 0))).astype(dtype)


def from_groups(array):
    return array[:, :LIVE].reshape(GROUPS * (LIVE // PATCHES), PATCHES, D)


def collect_weight(partial_grad, split_dim):
    return lax.psum_scatter(
        partial_grad, "dp", scatter_dimension=split_dim, tiled=True
    ).astype(F32)


def join_columns(blocks):
    return jnp.transpose(blocks, (1, 0, 2)).reshape(blocks.shape[1], -1)


def local(
    patches,
    keep_index,
    kept_count,
    norm_gain,
    shifts,
    w_qkv,
    bias_qv,
    w_out,
    w_fc1,
    bias_fc1,
    w_fc2,
    cotangent,
):
    width = w_qkv.shape[-1]
    hidden = w_fc1.shape[-1]
    slot_ids = jnp.arange(PATCHES, dtype=jnp.int32)
    selector = (keep_index[:, :, None] == slot_ids[None, None, :]).astype(BF16)
    tokens = jnp.einsum("bsp,bpd->bsd", selector, patches, preferred_element_type=F32)
    resid = to_groups(tokens, F32)
    unit, _ = norm_parts(resid)
    own = unit * norm_gain[0, 0] + shifts[0, 0]
    per = kept_count.shape[0] // GROUPS
    pad_row = jnp.arange(ROWS) - LIVE
    counts = kept_count.reshape(GROUPS, per).astype(F32)
    counts = jnp.pad(counts, ((0, 0), (LIVE, ROWS - LIVE - per)))
    own = jnp.where(pad_row[None, :, None] >= 0, counts[:, :, None], own).astype(BF16)

    def row(array):
        return array.reshape(1, -1)

    stored = []
    for n in range(LAYERS):
        wqkv = w_qkv[n].reshape(D, 3 * width)
        gath, qkv, prob, att, middle, own = attend_half(
            own, row(norm_gain[n, 1]), row(shifts[n, 2]), row(shifts[n, 1]),
            bias_qv[n], resid, wqkv, w_out[n],
        )
        after = min(n + 1, LAYERS - 1)
        gath_mlp, act, slope, resid_out, own = mlp_half(
            own, row(norm_gain[after, 0]), row(shifts[n, 3]), row(shifts[after, 0]),
            row(bias_fc1[n]), middle, w_fc1[n], w_fc2[n],
        )
        stored.append((resid, wqkv, gath, qkv, prob, att, middle, gath_mlp, act, slope))
        resid = resid_out
    own_mask = (slot_ids[None, :] < kept_count[:, None]).astype(F32)[:, :, None]
    layer_out = from_groups(resid) * own_mask
    start = cotangent.astype(F32) * own_mask
    gradient = to_groups(start, F32)
    own = gradient.astype(BF16)
    shift_last = jnp.sum(start, axis=(0, 1))
    gain_terms, shift_terms, bias_qv_terms, bias_fc1_terms, weight_terms = [], [], [], [], []
    for n in reversed(range(LAYERS)):
        resid, wqkv, gath, qkv, prob, att, middle, gath_mlp, act, slope = stored[n]
        gradient, own, sums, fc1_sum, d_fc1, d_fc2 = mlp_back(
            own, row(norm_gain[n, 1]), gradient, middle, w_fc1[n], w_fc2[n], act, slope, gath_mlp
        )
        gradient, own, sums_a, qkv_sum, d_qkv, d_out = attend_back(
            own, row(norm_gain[n, 0]), gradient, resid, wqkv, w_out[n], qkv, prob, att, gath
        )
        gain_terms.insert(0, jnp.stack([sums_a[0], sums[0]]))
        shift_terms.insert(0, jnp.stack([sums_a[1], sums[1], sums[2], shift_last]))
        shift_last = sums_a[2]
        bias_fc1_terms.insert(0, fc1_sum[0])
        bias_qv_terms.insert(0, jnp.stack([qkv_sum[0, :width], qkv_sum[0, 2 * width :]]))
        weight_terms.insert(
            0,
            (
                collect_weight(d_qkv.reshape(D, 3, width), 0),
                collect_weight(join_columns(d_out), 1),
                collect_weight(d_fc1, 0),
                collect_weight(join_columns(d_fc2), 1),
            ),
        )
    grad_qkv, grad_out, grad_fc1, grad_fc2 = (
        jnp.stack([entry[k] for entry in weight_terms]) for k in range(4)
    )
    offset_at = lax.axis_index("tensor") * width
    hidden_at = lax.axis_index("tensor") * hidden
    zero_at = offset_at * 0
    qv_full = lax.dynamic_update_slice(
        jnp.zeros((LAYERS, 2, D), F32), jnp.stack(bias_qv_terms), (zero_at, zero_at, offset_at)
    )
    fc1_full = lax.dynamic_update_slice(
        jnp.zeros((LAYERS, FF), F32), jnp.stack(bias_fc1_terms), (zero_at, hidden_at)
    )
    grad_gain, grad_shifts, grad_bias_qv, grad_bias_fc1 = lax.psum(
        (jnp.stack(gain_terms), jnp.stack(shift_terms), qv_full, fc1_full), ("dp", "tensor")
    )
    grad_patches = jnp.einsum(
        "bsp,bsd->bpd", selector.astype(F32), from_groups(gradient), precision=HIGHEST
    )
    return (
        layer_out,
        grad_patches,
        grad_gain,
        grad_shifts,
        grad_qkv,
        grad_bias_qv,
        grad_out,
        grad_fc1,
        grad_bias_fc1,
        grad_fc2,
    )


def solution(mesh):
    in_specs = (
        P(("dp", "tensor"), None, None),
        P(("dp", "tensor"), None),
        P(("dp", "tensor")),
        P(),
        P(),
        P(None, None, None, "tensor"),
        P(None, None, "tensor"),
        P(None, "tensor", None),
        P(None, None, "tensor"),
        P(None, "tensor"),
        P(None, "tensor", None),
        P(("dp", "tensor"), None, None),
    )
    out_specs = (
        P(("dp", "tensor"), None, None),
        P(("dp", "tensor"), None, None),
        P(),
        P(),
        P(None, "dp", None, "tensor"),
        P(),
        P(None, "tensor", "dp"),
        P(None, "dp", "tensor"),
        P(),
        P(None, "tensor", "dp"),
    )
    return jax.shard_map(local, mesh=mesh, in_specs=in_specs, out_specs=out_specs, check_vma=False)
```

```python
from functools import partial

import jax
import jax.numpy as jnp
from jax import lax
from jax.experimental import pallas as pl
from jax.experimental.pallas import tpu as pltpu
from jax.sharding import PartitionSpec as P

D = 1024
HEAD = 64
FF = 4096
LAYERS = 2
PATCHES = 50
EPS = 1e-06
HIGHEST = lax.Precision.HIGHEST
F32 = jnp.float32
BF16 = jnp.bfloat16

GROUPS = 2
ROWS = 160
LIVE = 150
COLS = 128
SCALE = HEAD ** (-0.5)


def dot(a, b, lhs=1, rhs=0):
    return lax.dot_general(a, b, (((lhs,), (rhs,)), ((), ())), preferred_element_type=F32)


def remote(src, dst, send, recv, peer):
    return pltpu.make_async_remote_copy(
        src_ref=src,
        dst_ref=dst,
        send_sem=send,
        recv_sem=recv,
        device_id={"tensor": peer},
        device_id_type=pl.DeviceIdType.MESH,
    )


def norm_parts(values):
    average = jnp.mean(values, axis=-1, keepdims=True)
    centred = values - average
    variance = jnp.mean(centred * centred, axis=-1, keepdims=True)
    scale = lax.rsqrt(variance + EPS)
    return centred * scale, scale


def head_mask(h, width):
    lane = lax.broadcasted_iota(jnp.int32, (1, width), 1)
    return (lane // HEAD == h).astype(F32).astype(BF16)


class Exchange:
    def __init__(self, x_own, gath, part, bufs, sems):
        self.x_own, self.gath, self.part = x_own, gath, part
        self.out_po, self.out_pd, self.out_y, self.in_po, self.in_pd, self.in_y = bufs
        self.sem = sems
        me = lax.axis_index("tensor")
        self.me = me
        self.mate = me + 1 - 2 * (me % 2)
        self.far = (me + 2) % 4
        self.diag = (self.mate + 2) % 4

    def barrier(self):
        sem = pltpu.get_barrier_semaphore()
        for peer in (self.mate, self.far):
            pl.semaphore_signal(
                sem, inc=1, device_id={"tensor": peer}, device_id_type=pl.DeviceIdType.MESH
            )
        pl.semaphore_wait(sem, 2)

    def copy(self, kind, g):
        s = self.sem
        own = GROUPS * self.me + g
        if kind == 0:
            src, dst, peer = self.x_own.at[g], self.gath.at[own], self.far
        elif kind == 1:
            src, dst, peer = self.x_own.at[g], self.gath.at[own], self.mate
        elif kind == 2:
            slot = GROUPS * self.far + g
            src, dst, peer = self.gath.at[slot], self.gath.at[slot], self.mate
        elif kind == 3:
            src, dst, peer = self.out_po.at[g], self.in_po.at[g], self.mate
        elif kind == 4:
            src, dst, peer = self.out_pd.at[g], self.in_pd.at[g], self.mate
        else:
            src, dst, peer = self.out_y.at[g], self.in_y.at[g], self.far
        return remote(src, dst, s.at[0, kind, g], s.at[1, kind, g], peer)

    def local(self, g):
        return pltpu.make_async_copy(
            self.x_own.at[g], self.gath.at[GROUPS * self.me + g], self.sem.at[0, 6, g]
        )

    def begin(self):
        self.barrier()
        for g in range(GROUPS):
            self.copy(0, g).start()
            self.copy(1, g).start()
            self.local(g).start()

    def slot(self, i):
        owner = jnp.where(
            i < 2, self.me, jnp.where(i < 4, self.mate, jnp.where(i % 2 == 0, self.far, self.diag))
        )
        g = jnp.where(i < 4, i % 2, (i - 4) // 2)
        return GROUPS * owner + g

    def before(self, i):
        for g in range(GROUPS):

            @pl.when(i == g)
            def _():
                self.local(g).wait()

            @pl.when(i == 2 + g)
            def _():
                self.copy(1, g).wait_recv()

            @pl.when(i == 4 + 2 * g)
            def _():
                self.copy(0, g).wait_recv()
                self.copy(2, g).start()

            @pl.when(i == 5 + 2 * g)
            def _():
                self.copy(2, g).wait_recv()

    def after(self, i):
        for g in range(GROUPS):

            @pl.when(i == 2 + g)
            def _():
                self.out_po[g] = self.part[2 + g].astype(BF16)
                self.copy(3, g).start()

            @pl.when(i == 5 + 2 * g)
            def _():
                self.out_pd[g] = self.part[5 + 2 * g].astype(BF16)
                self.copy(4, g).start()
                self.copy(4, g).wait_recv()
                self.out_y[g] = (self.part[4 + 2 * g] + self.in_pd[g].astype(F32)).astype(BF16)
                self.copy(5, g).start()

    def total(self, g):
        self.copy(3, g).wait_recv()
        self.copy(5, g).wait_recv()
        return self.part[g] + self.in_po[g].astype(F32) + self.in_y[g].astype(F32)

    def end(self):
        for g in range(GROUPS):
            for kind in range(6):
                self.copy(kind, g).wait_send()


def exchange_scratch():
    return [
        pltpu.VMEM((8, ROWS, D), BF16),
        pltpu.VMEM((8, ROWS, D), F32),
    ] + [pltpu.VMEM((GROUPS, ROWS, D), BF16)] * 6 + [pltpu.SemaphoreType.DMA((2, 7, GROUPS))]


class Moves:
    def __init__(self, sems):
        self.sems = sems

    def load(self, n, src, dst):
        return pltpu.make_async_copy(src, dst, self.sems.at[n])


def keep_pad(old, new):
    row = lax.broadcasted_iota(jnp.int32, (ROWS, D), 0)
    return jnp.where(row >= LIVE, old.astype(F32), new)


def attend_kernel(
    x_own, norm2, shift_a, shift_n, bias, resid_h, wqkv_h, wout_h,
    gath_h, qkv_h, prob_h, att_h, middle, next_own,
    gath, part, out_po, out_pd, out_y, in_po, in_pd, in_y, ex_sem,
    resid, wqkv, wout, qkv, prob, att, load_sem, save_sem,
):
    ex = Exchange(x_own, gath, part, (out_po, out_pd, out_y, in_po, in_pd, in_y), ex_sem)
    width = wout.shape[0]
    loads = Moves(load_sem)
    for n, pair in enumerate(((wqkv_h, wqkv), (wout_h, wout), (resid_h, resid))):
        loads.load(n, *pair).start()
    ex.begin()
    loads.load(0, wqkv_h, wqkv).wait()
    loads.load(1, wout_h, wout).wait()
    pairs = ((gath, gath_h), (qkv, qkv_h), (prob, prob_h), (att, att_h))

    def saves(slot):
        return [
            pltpu.make_async_copy(a.at[slot], b.at[slot], save_sem.at[n, slot])
            for n, (a, b) in enumerate(pairs)
        ]

    def step(i, _):
        ex.before(i)
        slot = ex.slot(i)
        x = gath[slot]
        triple = dot(x, wqkv[...])
        q = (triple[:, :width] + bias[0:1]).astype(BF16)
        k = triple[:, width : 2 * width].astype(BF16)
        v = (triple[:, 2 * width :] + bias[1:2]).astype(BF16)
        qkv[slot, :, 0:width] = q
        qkv[slot, :, width : 2 * width] = k
        qkv[slot, :, 2 * width :] = v
        counts = gath[slot, ROWS - 16 : ROWS, 0:256][:, 0:ROWS].astype(F32)
        lane = lax.broadcasted_iota(jnp.int32, (1, ROWS), 1)
        image = lane // PATCHES
        count = jnp.where(
            image == 0, counts[6:7], jnp.where(image == 1, counts[7:8], counts[8:9])
        )
        fits = (lane - image * PATCHES).astype(F32) < count
        row = lax.broadcasted_iota(jnp.int32, (ROWS, ROWS), 0)
        col = lax.broadcasted_iota(jnp.int32, (ROWS, ROWS), 1)
        same = jnp.minimum(row // PATCHES, 2) == col // PATCHES
        veil = jnp.where(same, 0.0, -1e30) + jnp.where(fits, 0.0, -1e30)
        mixed = jnp.zeros((ROWS, width), F32)
        for h in range(width // HEAD):
            mask = head_mask(h, width)
            scores = dot(q * mask, k, 1, 1) * SCALE + veil
            peak = jnp.max(scores, axis=-1, keepdims=True)
            raised = jnp.exp(scores - peak)
            weight = raised * (1.0 / jnp.sum(raised, axis=-1, keepdims=True))
            rounded = weight.astype(BF16)
            prob[slot, h * ROWS : (h + 1) * ROWS] = rounded
            mixed = mixed + dot(rounded, v * mask)
        mixed = mixed.astype(BF16)
        att[slot] = mixed
        part[i] = dot(mixed, wout[...])
        for copy in saves(slot):
            copy.start()
        ex.after(i)
        return 0

    lax.fori_loop(0, 8, step, 0)
    loads.load(2, resid_h, resid).wait()
    for g in range(GROUPS):
        mid = resid[g] + ex.total(g) + shift_a[...]
        middle[g] = mid
        unit, _ = norm_parts(mid)
        next_own[g] = keep_pad(x_own[g], unit * norm2[...] + shift_n[...]).astype(BF16)
    ex.end()

    def drain(slot, _):
        for copy in saves(slot):
            copy.wait()
        return 0

    lax.fori_loop(0, 8, drain, 0)


def erf_parts(pre):
    cdf = 0.5 * (1.0 + lax.erf(pre * (0.5 ** 0.5)))
    pdf = jnp.exp(-0.5 * pre * pre) * 0.3989422804014327
    return cdf, pdf


def mlp_kernel(
    x_own, gain_n, shift_a, shift_n, bias, middle_h, w1_h, w2_h,
    gath_h, act_h, slope_h, resid_out, next_own,
    gath, part, out_po, out_pd, out_y, in_po, in_pd, in_y, ex_sem,
    middle, w1, w2, act, slope, load_sem, save_sem,
):
    ex = Exchange(x_own, gath, part, (out_po, out_pd, out_y, in_po, in_pd, in_y), ex_sem)
    hidden = w1.shape[1]
    loads = Moves(load_sem)
    for n, pair in enumerate(((w1_h, w1), (w2_h, w2), (middle_h, middle))):
        loads.load(n, *pair).start()
    ex.begin()
    loads.load(0, w1_h, w1).wait()
    loads.load(1, w2_h, w2).wait()
    pairs = ((gath, gath_h), (act, act_h), (slope, slope_h))

    def saves(slot):
        return [
            pltpu.make_async_copy(a.at[slot], b.at[slot], save_sem.at[n, slot])
            for n, (a, b) in enumerate(pairs)
        ]

    def step(i, _):
        ex.before(i)
        slot = ex.slot(i)
        x = gath[slot]
        for block in range(hidden // 256):
            at = slice(block * 256, block * 256 + 256)
            pre = dot(x, w1[:, at]) + bias[:, at]
            cdf, pdf = erf_parts(pre)
            act[slot, :, at] = (pre * cdf).astype(BF16)
            slope[slot, :, at] = (cdf + pre * pdf).astype(BF16)
        part[i] = dot(act[slot], w2[...])
        for copy in saves(slot):
            copy.start()
        ex.after(i)
        return 0

    lax.fori_loop(0, 8, step, 0)
    loads.load(2, middle_h, middle).wait()
    for g in range(GROUPS):
        res = middle[g] + ex.total(g) + shift_a[...]
        resid_out[g] = res
        unit, _ = norm_parts(res)
        next_own[g] = keep_pad(x_own[g], unit * gain_n[...] + shift_n[...]).astype(BF16)
    ex.end()

    def drain(slot, _):
        for copy in saves(slot):
            copy.wait()
        return 0

    lax.fori_loop(0, 8, drain, 0)


VM = pl.BlockSpec(memory_space=pltpu.VMEM)
HB = pl.BlockSpec(memory_space=pl.ANY)


def sds(shape, dtype):
    return jax.ShapeDtypeStruct(shape, dtype)


def params(n):
    return pltpu.CompilerParams(
        collective_id=n, has_side_effects=True, vmem_limit_bytes=60 * 1024 * 1024
    )


def attend_half(x_own, gain, shift_a, shift_n, bias, resid, wqkv, wout):
    width = wout.shape[0]
    heads = width // HEAD
    return pl.pallas_call(
        attend_kernel,
        out_shape=(
            sds((8, ROWS, D), BF16),
            sds((8, ROWS, 3 * width), BF16),
            sds((8, heads * ROWS, ROWS), BF16),
            sds((8, ROWS, width), BF16),
            sds((GROUPS, ROWS, D), F32),
            sds((GROUPS, ROWS, D), BF16),
        ),
        in_specs=[VM] * 5 + [HB] * 3,
        out_specs=(HB, HB, HB, HB, VM, VM),
        scratch_shapes=exchange_scratch()
        + [
            pltpu.VMEM((GROUPS, ROWS, D), F32),
            pltpu.VMEM((D, 3 * width), BF16),
            pltpu.VMEM((width, D), BF16),
            pltpu.VMEM((8, ROWS, 3 * width), BF16),
            pltpu.VMEM((8, heads * ROWS, ROWS), BF16),
            pltpu.VMEM((8, ROWS, width), BF16),
            pltpu.SemaphoreType.DMA((3,)),
            pltpu.SemaphoreType.DMA((4, 8)),
        ],
        compiler_params=params(1),
    )(x_own, gain, shift_a, shift_n, bias, resid, wqkv, wout)


def mlp_half(x_own, gain, shift_a, shift_n, bias, middle, w1, w2):
    hidden = w1.shape[1]
    return pl.pallas_call(
        mlp_kernel,
        out_shape=(
            sds((8, ROWS, D), BF16),
            sds((8, ROWS, hidden), BF16),
            sds((8, ROWS, hidden), BF16),
            sds((GROUPS, ROWS, D), F32),
            sds((GROUPS, ROWS, D), BF16),
        ),
        in_specs=[VM] * 5 + [HB] * 3,
        out_specs=(HB, HB, HB, VM, VM),
        scratch_shapes=exchange_scratch()
        + [
            pltpu.VMEM((GROUPS, ROWS, D), F32),
            pltpu.VMEM((D, hidden), BF16),
            pltpu.VMEM((hidden, D), BF16),
            pltpu.VMEM((8, ROWS, hidden), BF16),
            pltpu.VMEM((8, ROWS, hidden), BF16),
            pltpu.SemaphoreType.DMA((3,)),
            pltpu.SemaphoreType.DMA((3, 8)),
        ],
        compiler_params=params(2),
    )(x_own, gain, shift_a, shift_n, bias, middle, w1, w2)


def column_sums(values):
    return jnp.sum(values, axis=0, keepdims=True)


def back_through_norm(ex, g, gradient, source, gain, grad_out, next_own, sums):
    moved = ex.total(g)
    unit, scale = norm_parts(source[g])
    scaled = moved * gain[...]
    lean = jnp.mean(scaled, axis=-1, keepdims=True)
    tilt = jnp.mean(scaled * unit, axis=-1, keepdims=True)
    grad = gradient[g] + scale * (scaled - lean - unit * tilt)
    rounded = grad.astype(BF16)
    grad_out[g] = grad
    next_own[g] = rounded
    rows = (column_sums(moved * unit), column_sums(moved), column_sums(rounded.astype(F32)))
    for n, row in enumerate(rows):
        sums[n : n + 1] = row if g == 0 else sums[n : n + 1] + row


def weight_blocks(left, right, rows_out, cols_left, cols_right, cols_out, copies):
    flat = 8 * ROWS

    def block(n, _):
        at = pl.ds(pl.multiple_of(n * 256, 256), 256)
        some = left[:, :, at].reshape(flat, 256)
        tall = dot(some, right[...].reshape(flat, right.shape[-1]), 0, 0).astype(BF16)
        rows_out[0, n] = tall[:COLS]
        rows_out[1, n] = tall[COLS:]
        some = cols_right[:, :, at].reshape(flat, 256)
        wide = dot(cols_left[...].reshape(flat, cols_left.shape[-1]), some, 0, 0).astype(BF16)
        cols_out[0, n] = wide[:, :COLS]
        cols_out[1, n] = wide[:, COLS:]
        for copy in copies(n):
            copy.start()
        return 0

    lax.fori_loop(0, D // 256, block, 0)


def weight_copies(rows_out, rows_h, cols_out, cols_h, sems):
    def copies(n):
        return [
            pltpu.make_async_copy(a.at[half, n], b.at[half, n], sems.at[2 * kind + half, n])
            for kind, (a, b) in enumerate(((rows_out, rows_h), (cols_out, cols_h)))
            for half in range(2)
        ]

    return copies


def drain_weights(copies):
    def drain(n, _):
        for copy in copies(n):
            copy.wait()
        return 0

    lax.fori_loop(0, D // 256, drain, 0)


def mlp_back_kernel(
    x_own, gain, gradient_h, middle_h, w1_h, w2_h, act_h, slope_h, norm_h,
    grad_out, next_own, sums, bias_sum, rows_h, cols_h,
    gath, part, out_po, out_pd, out_y, in_po, in_pd, in_y, ex_sem,
    gradient, middle, w1, w2, act, slope, norm, pre, rows_out, cols_out, load_sem, save_sem,
):
    ex = Exchange(x_own, gath, part, (out_po, out_pd, out_y, in_po, in_pd, in_y), ex_sem)
    hidden = w1.shape[1]
    loads = [
        pltpu.make_async_copy(a, b, load_sem.at[n])
        for n, (a, b) in enumerate(
            (
                (w2_h, w2),
                (slope_h, slope),
                (w1_h, w1),
                (act_h, act),
                (norm_h, norm),
                (gradient_h, gradient),
                (middle_h, middle),
            )
        )
    ]
    for copy in loads:
        copy.start()
    ex.begin()
    for copy in loads[:3]:
        copy.wait()

    def step(i, _):
        ex.before(i)
        slot = ex.slot(i)
        grad = gath[slot]
        for block in range(hidden // 256):
            at = slice(block * 256, block * 256 + 256)
            d_act = dot(grad, w2[at, :], 1, 1)
            pre[slot, :, at] = (d_act * slope[slot, :, at].astype(F32)).astype(BF16)
        part[i] = dot(pre[slot], w1[...], 1, 1)
        ex.after(i)
        return 0

    lax.fori_loop(0, 8, step, 0)
    for copy in loads[3:]:
        copy.wait()
    copies = weight_copies(rows_out, rows_h, cols_out, cols_h, save_sem)
    weight_blocks(norm, pre, rows_out, act, gath, cols_out, copies)
    ones = jnp.ones((8, 8 * ROWS), BF16)
    bias_sum[...] = dot(ones, pre[...].reshape(8 * ROWS, hidden))
    for g in range(GROUPS):
        back_through_norm(ex, g, gradient, middle, gain, grad_out, next_own, sums)
    ex.end()
    drain_weights(copies)


def attend_back_kernel(
    x_own, gain, gradient_h, resid_h, wqkv_h, wout_h, qkv_h, prob_h, att_h, norm_h,
    grad_out, next_own, sums, bias_sum, rows_h, cols_h,
    gath, part, out_po, out_pd, out_y, in_po, in_pd, in_y, ex_sem,
    gradient, resid, wqkv, wout, qkv, prob, att, norm, triple, rows_out, cols_out,
    load_sem, save_sem,
):
    ex = Exchange(x_own, gath, part, (out_po, out_pd, out_y, in_po, in_pd, in_y), ex_sem)
    width = wout.shape[0]
    loads = [
        pltpu.make_async_copy(a, b, load_sem.at[n])
        for n, (a, b) in enumerate(
            (
                (wout_h, wout),
                (qkv_h, qkv),
                (prob_h, prob),
                (wqkv_h, wqkv),
                (att_h, att),
                (norm_h, norm),
                (gradient_h, gradient),
                (resid_h, resid),
            )
        )
    ]
    for copy in loads:
        copy.start()
    ex.begin()
    for copy in loads[:4]:
        copy.wait()

    def step(i, _):
        ex.before(i)
        slot = ex.slot(i)
        grad = gath[slot]
        d_att = dot(grad, wout[...], 1, 1).astype(BF16)
        q = qkv[slot, :, 0:width]
        k = qkv[slot, :, width : 2 * width]
        v = qkv[slot, :, 2 * width :]
        d_q = jnp.zeros((ROWS, width), F32)
        d_k = jnp.zeros((ROWS, width), F32)
        d_v = jnp.zeros((ROWS, width), F32)
        for h in range(width // HEAD):
            mask = head_mask(h, width)
            d_one = d_att * mask
            rounded = prob[slot, h * ROWS : (h + 1) * ROWS]
            weight = rounded.astype(F32)
            d_prob = dot(d_one, v, 1, 1)
            centre = jnp.sum(weight * d_prob, axis=-1, keepdims=True)
            d_scores = (weight * (d_prob - centre)).astype(BF16)
            d_q = d_q + dot(d_scores, k * mask)
            d_k = d_k + dot(d_scores, q * mask, 0, 0)
            d_v = d_v + dot(rounded, d_one, 0, 0)
        triple[slot, :, 0:width] = (d_q * SCALE).astype(BF16)
        triple[slot, :, width : 2 * width] = (d_k * SCALE).astype(BF16)
        triple[slot, :, 2 * width :] = d_v.astype(BF16)
        part[i] = dot(triple[slot], wqkv[...], 1, 1)
        ex.after(i)
        return 0

    lax.fori_loop(0, 8, step, 0)
    for copy in loads[4:]:
        copy.wait()
    copies = weight_copies(rows_out, rows_h, cols_out, cols_h, save_sem)
    weight_blocks(norm, triple, rows_out, att, gath, cols_out, copies)
    ones = jnp.ones((8, 8 * ROWS), BF16)
    bias_sum[...] = dot(ones, triple[...].reshape(8 * ROWS, 3 * width))
    for g in range(GROUPS):
        back_through_norm(ex, g, gradient, resid, gain, grad_out, next_own, sums)
    ex.end()
    drain_weights(copies)


def back_outs(rows, cols):
    return (
        sds((GROUPS, ROWS, D), F32),
        sds((GROUPS, ROWS, D), BF16),
        sds((8, D), F32),
        sds((8, rows), F32),
        sds((2, D // 256, COLS, rows), BF16),
        sds((2, D // 256, cols, COLS), BF16),
    )


def back_scratch(rows, cols, loads):
    return [
        pltpu.VMEM((2, D // 256, COLS, rows), BF16),
        pltpu.VMEM((2, D // 256, cols, COLS), BF16),
        pltpu.SemaphoreType.DMA((loads,)),
        pltpu.SemaphoreType.DMA((4, D // 256)),
    ]


def mlp_back(x_own, gain, gradient, middle, w1, w2, act, slope, norm):
    hidden = w1.shape[1]
    wide = pltpu.VMEM((8, ROWS, hidden), BF16)
    return pl.pallas_call(
        mlp_back_kernel,
        out_shape=back_outs(hidden, hidden),
        in_specs=[VM] * 2 + [HB] * 7,
        out_specs=(VM, VM, VM, VM, HB, HB),
        scratch_shapes=exchange_scratch()
        + [
            pltpu.VMEM((GROUPS, ROWS, D), F32),
            pltpu.VMEM((GROUPS, ROWS, D), F32),
            pltpu.VMEM((D, hidden), BF16),
            pltpu.VMEM((hidden, D), BF16),
            wide,
            wide,
            pltpu.VMEM((8, ROWS, D), BF16),
            wide,
        ]
        + back_scratch(hidden, hidden, 7),
        compiler_params=params(3),
    )(x_own, gain, gradient, middle, w1, w2, act, slope, norm)


def attend_back(x_own, gain, gradient, resid, wqkv, wout, qkv, prob, att, norm):
    width = wout.shape[0]
    heads = width // HEAD
    return pl.pallas_call(
        attend_back_kernel,
        out_shape=back_outs(3 * width, width),
        in_specs=[VM] * 2 + [HB] * 8,
        out_specs=(VM, VM, VM, VM, HB, HB),
        scratch_shapes=exchange_scratch()
        + [
            pltpu.VMEM((GROUPS, ROWS, D), F32),
            pltpu.VMEM((GROUPS, ROWS, D), F32),
            pltpu.VMEM((D, 3 * width), BF16),
            pltpu.VMEM((width, D), BF16),
            pltpu.VMEM((8, ROWS, 3 * width), BF16),
            pltpu.VMEM((8, heads * ROWS, ROWS), BF16),
            pltpu.VMEM((8, ROWS, width), BF16),
            pltpu.VMEM((8, ROWS, D), BF16),
            pltpu.VMEM((8, ROWS, 3 * width), BF16),
        ]
        + back_scratch(3 * width, width, 8),
        compiler_params=params(4),
    )(x_own, gain, gradient, resid, wqkv, wout, qkv, prob, att, norm)


def to_groups(array, dtype):
    images = array.shape[0] // GROUPS
    rows = array.reshape(GROUPS, images * PATCHES, D)
    return jnp.pad(rows, ((0, 0), (0, ROWS - images * PATCHES), (0, 0))).astype(dtype)


def from_groups(array):
    return array[:, :LIVE].reshape(GROUPS * (LIVE // PATCHES), PATCHES, D)


def collect_weight(partial_grad, split_dim):
    return lax.psum_scatter(
        partial_grad, "dp", scatter_dimension=split_dim, tiled=True
    ).astype(F32)


def join_rows(blocks):
    return jnp.transpose(blocks, (1, 0, 2, 3)).reshape(D, -1)


def join_columns(blocks):
    return jnp.transpose(blocks, (2, 1, 0, 3)).reshape(blocks.shape[2], -1)


def to_peer(axis, src, dst, sems, n, peer):
    return pltpu.make_async_remote_copy(
        src_ref=src,
        dst_ref=dst,
        send_sem=sems.at[0, n],
        recv_sem=sems.at[1, n],
        device_id={axis: peer},
        device_id_type=pl.DeviceIdType.MESH,
    )


def reduce_kernel(*refs):
    count = 2 * 4
    grads, small = refs[:count], refs[count]
    outs, small_out = refs[count + 1 : 2 * count + 1], refs[2 * count + 1]
    rest = refs[2 * count + 2 :]
    keeps, halves = rest[:count], rest[count : 2 * count]
    arrivals = rest[2 * count : 3 * count]
    totals = rest[3 * count : 4 * count]
    small_sum, small_in, small_z = rest[4 * count : 4 * count + 3]
    load_sem, half_sem, z_sem, out_sem, small_sem = rest[4 * count + 3 :]
    me = lax.axis_index("dp")
    x, z = me % 2, me // 2
    across = me + 1 - 2 * x
    mine = lax.axis_index("tensor")

    barrier = pltpu.get_barrier_semaphore()

    def greet(axis, peer):
        pl.semaphore_signal(
            barrier, inc=1, device_id={axis: peer}, device_id_type=pl.DeviceIdType.MESH
        )

    greet("dp", across)
    for d in range(1, 4):
        greet("dp", 2 * ((z + d) % 4) + x)
        greet("tensor", (mine + d) % 4)
    pl.semaphore_wait(barrier, 7)

    def half(n):
        return to_peer("dp", grads[n].at[1 - x], halves[n], half_sem, n, across)

    def keep(n):
        return pltpu.make_async_copy(grads[n].at[x], keeps[n], load_sem.at[n])

    def shard(n, d):
        there = (z + d) % 4
        return to_peer(
            "dp", keeps[n].at[there], arrivals[n].at[d - 1], z_sem.at[n], d - 1, 2 * there + x
        )

    def store(n):
        return pltpu.make_async_copy(totals[n], outs[n], out_sem.at[n])

    small_x = to_peer("dp", small, small_in, small_sem, 0, across)
    small_x.start()
    for n in range(count):
        half(n).start()
        keep(n).start()

    def small_over_z(d):
        return to_peer(
            "dp", small_sum, small_z.at[z], small_sem, d, 2 * ((z + d) % 4) + x
        )

    def small_over_tensor(d):
        return to_peer(
            "tensor", small_out.at[mine], small_out.at[mine], small_sem, 3 + d, (mine + d) % 4
        )

    small_x.wait_recv()
    small_sum[...] = small[...] + small_in[...]
    for d in range(1, 4):
        small_over_z(d).start()
    small_z[z] = small_sum[...]
    for d in range(1, 4):
        small_over_z(d).wait_recv()
    small_out[mine] = small_z[0] + small_z[1] + small_z[2] + small_z[3]
    for d in range(1, 4):
        small_over_tensor(d).start()

    for n in range(count):
        keep(n).wait()
        half(n).wait_recv()
        rows = keeps[n].shape[1]

        def fold(i, _, n=n, rows=rows):
            at = pl.ds(pl.multiple_of(i * 128, 128), 128)
            for j in range(4):
                keeps[n][j, at, :] = (
                    keeps[n][j, at, :].astype(F32) + halves[n][j, at, :].astype(F32)
                ).astype(BF16)
            return 0

        lax.fori_loop(0, rows // 128, fold, 0)
        for d in range(1, 4):
            shard(n, d).start()
    for n in range(count):
        for d in range(1, 4):
            shard(n, d).wait_recv()
        rows = keeps[n].shape[1]

        def add(i, _, n=n, rows=rows):
            at = pl.ds(pl.multiple_of(i * 128, 128), 128)
            total = keeps[n][z, at, :].astype(F32)
            for j in range(3):
                total = total + arrivals[n][j, at, :].astype(F32)
            totals[n][at, :] = total
            return 0

        lax.fori_loop(0, rows // 128, add, 0)
        store(n).start()
    for d in range(1, 4):
        small_over_tensor(d).wait_recv()
    small_x.wait_send()
    for d in range(1, 4):
        small_over_z(d).wait_send()
        small_over_tensor(d).wait_send()
    for n in range(count):
        half(n).wait_send()
        for d in range(1, 4):
            shard(n, d).wait_send()
        store(n).wait()


def reduce_all(grads, small):
    shapes = [g.shape[2:] for g in grads]
    count = len(grads)
    small_shape = small.shape
    dma = pltpu.SemaphoreType.DMA
    results = pl.pallas_call(
        reduce_kernel,
        out_shape=[sds(s, F32) for s in shapes] + [sds((4,) + small_shape, F32)],
        in_specs=[HB] * count + [VM],
        out_specs=[HB] * count + [VM],
        scratch_shapes=[pltpu.VMEM((4,) + s, BF16) for s in shapes]
        + [pltpu.VMEM((4,) + s, BF16) for s in shapes]
        + [pltpu.VMEM((3,) + s, BF16) for s in shapes]
        + [pltpu.VMEM(s, F32) for s in shapes]
        + [
            pltpu.VMEM(small_shape, F32),
            pltpu.VMEM(small_shape, F32),
            pltpu.VMEM((4,) + small_shape, F32),
            dma((count,)),
            dma((2, count)),
            dma((count, 2, 3)),
            dma((count,)),
            dma((2, 7)),
        ],
        compiler_params=params(5),
    )(*grads, small)
    return results[:-1], results[-1]


def local(
    patches,
    keep_index,
    kept_count,
    norm_gain,
    shifts,
    w_qkv,
    bias_qv,
    w_out,
    w_fc1,
    bias_fc1,
    w_fc2,
    cotangent,
):
    width = w_qkv.shape[-1]
    hidden = w_fc1.shape[-1]
    dp_size = lax.axis_size("dp")
    slot_ids = jnp.arange(PATCHES, dtype=jnp.int32)
    selector = (keep_index[:, :, None] == slot_ids[None, None, :]).astype(BF16)
    tokens = jnp.einsum("bsp,bpd->bsd", selector, patches, preferred_element_type=F32)
    resid = to_groups(tokens, F32)
    unit, _ = norm_parts(resid)
    own = unit * norm_gain[0, 0] + shifts[0, 0]
    per = kept_count.shape[0] // GROUPS
    pad_row = jnp.arange(ROWS) - LIVE
    counts = kept_count.reshape(GROUPS, per).astype(F32)
    counts = jnp.pad(counts, ((0, 0), (LIVE, ROWS - LIVE - per)))
    own = jnp.where(pad_row[None, :, None] >= 0, counts[:, :, None], own).astype(BF16)

    def row(array):
        return array.reshape(1, -1)

    stored = []
    for n in range(LAYERS):
        wqkv = w_qkv[n].reshape(D, 3 * width)
        gath, qkv, prob, att, middle, own = attend_half(
            own, row(norm_gain[n, 1]), row(shifts[n, 2]), row(shifts[n, 1]),
            bias_qv[n], resid, wqkv, w_out[n],
        )
        after = min(n + 1, LAYERS - 1)
        gath_mlp, act, slope, resid_out, own = mlp_half(
            own, row(norm_gain[after, 0]), row(shifts[n, 3]), row(shifts[after, 0]),
            row(bias_fc1[n]), middle, w_fc1[n], w_fc2[n],
        )
        stored.append((resid, wqkv, gath, qkv, prob, att, middle, gath_mlp, act, slope))
        resid = resid_out
    own_mask = (slot_ids[None, :] < kept_count[:, None]).astype(F32)[:, :, None]
    layer_out = from_groups(resid) * own_mask
    start = cotangent.astype(F32) * own_mask
    gradient = to_groups(start, F32)
    own = gradient.astype(BF16)
    shift_last = jnp.sum(start, axis=(0, 1))
    gain_terms, shift_terms, bias_qv_terms, bias_fc1_terms, weight_terms = [], [], [], [], []
    for n in reversed(range(LAYERS)):
        resid, wqkv, gath, qkv, prob, att, middle, gath_mlp, act, slope = stored[n]
        gradient, own, sums, fc1_sum, d_fc1, d_fc2 = mlp_back(
            own, row(norm_gain[n, 1]), gradient, middle, w_fc1[n], w_fc2[n], act, slope, gath_mlp
        )
        gradient, own, sums_a, qkv_sum, d_qkv, d_out = attend_back(
            own, row(norm_gain[n, 0]), gradient, resid, wqkv, w_out[n], qkv, prob, att, gath
        )
        gain_terms.insert(0, jnp.stack([sums_a[0], sums[0]]))
        shift_terms.insert(0, jnp.stack([sums_a[1], sums[1], sums[2], shift_last]))
        shift_last = sums_a[2]
        bias_fc1_terms.insert(0, fc1_sum[0])
        bias_qv_terms.insert(0, jnp.stack([qkv_sum[0, :width], qkv_sum[0, 2 * width :]]))
        weight_terms.insert(0, (d_qkv, d_out, d_fc1, d_fc2))
    if dp_size == 8 and lax.axis_size("tensor") == 4 and 4 * width == D and hidden == D:
        flat = [entry[k] for k in range(4) for entry in weight_terms]
        lines = gain_terms + shift_terms + [row(line) for line in bias_fc1_terms]
        lines = lines + [jnp.stack(bias_qv_terms).reshape(1, D), jnp.zeros((1, D), F32)]
        totals, small = reduce_all(flat, jnp.concatenate(lines))
        grad_qkv, grad_out, grad_fc1, grad_fc2 = (
            jnp.stack([totals[LAYERS * k + n] for n in range(LAYERS)]) for k in range(4)
        )
        grad_qkv = grad_qkv.reshape(LAYERS, -1, 3, width)
        summed = jnp.sum(small[:, :12], axis=0)
        grad_gain = summed[:4].reshape(LAYERS, 2, D)
        grad_shifts = summed[4:].reshape(LAYERS, 4, D)
        grad_bias_fc1 = jnp.transpose(small[:, 12:14], (1, 0, 2)).reshape(LAYERS, FF)
        quarters = small[:, 14].reshape(4, LAYERS, 2, width)
        grad_bias_qv = jnp.transpose(quarters, (1, 2, 0, 3)).reshape(LAYERS, 2, D)
    else:
        grad_qkv, grad_out, grad_fc1, grad_fc2 = (
            jnp.stack(
                [
                    collect_weight(join(entry[k]), split)
                    for entry in weight_terms
                ]
            )
            for k, (join, split) in enumerate(
                ((join_rows, 0), (join_columns, 1), (join_rows, 0), (join_columns, 1))
            )
        )
        grad_qkv = grad_qkv.reshape(LAYERS, -1, 3, width)
        offset_at = lax.axis_index("tensor") * width
        hidden_at = lax.axis_index("tensor") * hidden
        zero_at = offset_at * 0
        qv_full = lax.dynamic_update_slice(
            jnp.zeros((LAYERS, 2, D), F32), jnp.stack(bias_qv_terms), (zero_at, zero_at, offset_at)
        )
        fc1_full = lax.dynamic_update_slice(
            jnp.zeros((LAYERS, FF), F32), jnp.stack(bias_fc1_terms), (zero_at, hidden_at)
        )
        grad_gain, grad_shifts, grad_bias_qv, grad_bias_fc1 = lax.psum(
            (jnp.stack(gain_terms), jnp.stack(shift_terms), qv_full, fc1_full), ("dp", "tensor")
        )
    grad_patches = jnp.einsum(
        "bsp,bsd->bpd", selector.astype(F32), from_groups(gradient), precision=HIGHEST
    )
    return (
        layer_out,
        grad_patches,
        grad_gain,
        grad_shifts,
        grad_qkv,
        grad_bias_qv,
        grad_out,
        grad_fc1,
        grad_bias_fc1,
        grad_fc2,
    )


def solution(mesh):
    in_specs = (
        P(("dp", "tensor"), None, None),
        P(("dp", "tensor"), None),
        P(("dp", "tensor")),
        P(),
        P(),
        P(None, None, None, "tensor"),
        P(None, None, "tensor"),
        P(None, "tensor", None),
        P(None, None, "tensor"),
        P(None, "tensor"),
        P(None, "tensor", None),
        P(("dp", "tensor"), None, None),
    )
    out_specs = (
        P(("dp", "tensor"), None, None),
        P(("dp", "tensor"), None, None),
        P(),
        P(),
        P(None, "dp", None, "tensor"),
        P(),
        P(None, "tensor", "dp"),
        P(None, "dp", "tensor"),
        P(),
        P(None, "tensor", "dp"),
    )
    return jax.shard_map(local, mesh=mesh, in_specs=in_specs, out_specs=out_specs, check_vma=False)
```

```python
from functools import partial

import jax
import jax.numpy as jnp
from jax import lax
from jax.experimental import pallas as pl
from jax.experimental.pallas import tpu as pltpu
from jax.sharding import PartitionSpec as P

D = 1024
HEAD = 64
FF = 4096
LAYERS = 2
PATCHES = 50
EPS = 1e-06
HIGHEST = lax.Precision.HIGHEST
F32 = jnp.float32
BF16 = jnp.bfloat16

GROUPS = 2
ROWS = 160
LIVE = 150
COLS = 128
SCALE = HEAD ** (-0.5)


def dot(a, b, lhs=1, rhs=0):
    return lax.dot_general(a, b, (((lhs,), (rhs,)), ((), ())), preferred_element_type=F32)


def remote(src, dst, send, recv, peer):
    return pltpu.make_async_remote_copy(
        src_ref=src,
        dst_ref=dst,
        send_sem=send,
        recv_sem=recv,
        device_id={"tensor": peer},
        device_id_type=pl.DeviceIdType.MESH,
    )


def norm_parts(values):
    average = jnp.mean(values, axis=-1, keepdims=True)
    centred = values - average
    variance = jnp.mean(centred * centred, axis=-1, keepdims=True)
    scale = lax.rsqrt(variance + EPS)
    return centred * scale, scale


def head_mask(h, width):
    lane = lax.broadcasted_iota(jnp.int32, (1, width), 1)
    return (lane // HEAD == h).astype(F32).astype(BF16)


class Exchange:
    def __init__(self, gath, part, bufs, sems):
        self.gath, self.part = gath, part
        self.out_po, self.out_pd, self.out_y, self.in_po, self.in_pd, self.in_y = bufs
        self.sem = sems
        me = lax.axis_index("tensor")
        self.me = me
        self.mate = me + 1 - 2 * (me % 2)
        self.far = (me + 2) % 4
        self.diag = (self.mate + 2) % 4
        self.stage = 0

    def barrier(self):
        sem = pltpu.get_barrier_semaphore()
        for peer in (self.mate, self.far):
            pl.semaphore_signal(
                sem, inc=1, device_id={"tensor": peer}, device_id_type=pl.DeviceIdType.MESH
            )
        pl.semaphore_wait(sem, 2)

    def own(self, g):
        return GROUPS * self.me + g

    def rows(self, slot):
        return self.gath.at[self.stage % 2, slot]

    def copy(self, kind, g):
        s = self.sem
        own, slot = self.rows(self.own(g)), self.rows(GROUPS * self.far + g)
        src, dst, peer = (
            (own, own, self.far),
            (own, own, self.mate),
            (slot, slot, self.mate),
            (self.out_po.at[g], self.in_po.at[g], self.mate),
            (self.out_pd.at[g], self.in_pd.at[g], self.mate),
            (self.out_y.at[g], self.in_y.at[g], self.far),
        )[kind]
        return remote(src, dst, s.at[0, kind, g], s.at[1, kind, g], peer)

    def again(self, kind, g):
        if self.stage:
            self.copy(kind, g).wait_send()

    def send(self, kind, g):
        self.copy(kind, g).start()

    def share(self, g):
        for kind in range(2):
            self.again(kind, g)
            self.send(kind, g)

    def slot(self, i):
        even = i % 2 == 0
        owner = jnp.where(
            i < 4,
            jnp.where(even, self.me, self.mate),
            jnp.where(even, self.far, self.diag),
        )
        return GROUPS * owner + (i // 2) % 2

    def before(self, i):
        for g in range(GROUPS):

            @pl.when(i == 1 + 2 * g)
            def _():
                self.copy(1, g).wait_recv()

            @pl.when(i == 4 + 2 * g)
            def _():
                self.copy(0, g).wait_recv()
                self.again(2, g)
                self.send(2, g)

            @pl.when(i == 5 + 2 * g)
            def _():
                self.copy(2, g).wait_recv()

    def after(self, i):
        for g in range(GROUPS):

            @pl.when(i == 1 + 2 * g)
            def _():
                self.again(3, g)
                self.out_po[g] = self.part[1 + 2 * g].astype(BF16)
                self.send(3, g)

            @pl.when(i == 5 + 2 * g)
            def _():
                self.again(4, g)
                self.out_pd[g] = self.part[5 + 2 * g].astype(BF16)
                self.send(4, g)
                self.copy(4, g).wait_recv()
                self.again(5, g)
                self.out_y[g] = (self.part[4 + 2 * g] + self.in_pd[g].astype(F32)).astype(BF16)
                self.send(5, g)

    def total(self, g):
        self.copy(3, g).wait_recv()
        self.copy(5, g).wait_recv()
        return self.part[2 * g] + self.in_po[g].astype(F32) + self.in_y[g].astype(F32)

    def end(self):
        for g in range(GROUPS):
            for kind in range(6):
                self.copy(kind, g).wait_send()


def exchange_scratch():
    return [
        pltpu.VMEM((2, 8, ROWS, D), BF16),
        pltpu.VMEM((8, ROWS, D), F32),
    ] + [pltpu.VMEM((GROUPS, ROWS, D), BF16)] * 6 + [pltpu.SemaphoreType.DMA((2, 6, GROUPS))]


def picker(keep, g):
    patch = lax.broadcasted_iota(jnp.int32, (ROWS, ROWS), 0)
    return (keep[g] == patch).astype(F32).astype(BF16)


def attend(x, q_bias, v_bias, wqkv, wout, counts, keep_parts):
    width = wout.shape[0]
    triple = dot(x, wqkv[...])
    q = (triple[:, :width] + q_bias).astype(BF16)
    k = triple[:, width : 2 * width].astype(BF16)
    v = (triple[:, 2 * width :] + v_bias).astype(BF16)
    keep_parts(0, q, k, v)
    lane = lax.broadcasted_iota(jnp.int32, (1, ROWS), 1)
    image = lane // PATCHES
    count = jnp.where(image == 0, counts[6:7], jnp.where(image == 1, counts[7:8], counts[8:9]))
    fits = (lane - image * PATCHES).astype(F32) < count
    row = lax.broadcasted_iota(jnp.int32, (ROWS, ROWS), 0)
    col = lax.broadcasted_iota(jnp.int32, (ROWS, ROWS), 1)
    same = jnp.minimum(row // PATCHES, 2) == col // PATCHES
    veil = jnp.where(same, 0.0, -1e30) + jnp.where(fits, 0.0, -1e30)
    mixed = jnp.zeros((ROWS, width), F32)
    for h in range(width // HEAD):
        mask = head_mask(h, width)
        scores = dot(q * mask, k, 1, 1) * SCALE + veil
        peak = jnp.max(scores, axis=-1, keepdims=True)
        raised = jnp.exp(scores - peak)
        weight = raised * (1.0 / jnp.sum(raised, axis=-1, keepdims=True))
        rounded = weight.astype(BF16)
        keep_parts(1 + h, rounded)
        mixed = mixed + dot(rounded, v * mask)
    return mixed.astype(BF16)


def erf_parts(pre):
    cdf = 0.5 * (1.0 + lax.erf(pre * (0.5 ** 0.5)))
    pdf = jnp.exp(-0.5 * pre * pre) * 0.3989422804014327
    return cdf, pdf


def forward_kernel(
    patches, keep, counts, gains, shifts, bias_qv, bias_fc1, wqkv_h, wout_h, w1_h, w2_h,
    flow_h, gath_h, qkv_h, prob_h, att_h, gmlp_h, act_h, slope_h,
    gath, part, out_po, out_pd, out_y, in_po, in_pd, in_y, ex_sem,
    flow, wqkv, wout, w1, w2, qkv, prob, att, act, slope, load_sem, save_sem, flow_sem,
):
    ex = Exchange(gath, part, (out_po, out_pd, out_y, in_po, in_pd, in_y), ex_sem)
    width, hidden = wout.shape[1], w1.shape[2]
    stages = 2 * LAYERS
    loads = []
    for n in range(LAYERS):
        pieces = [
            (wqkv_h.at[n, c], wqkv.at[n, :, pl.ds(c * width, width)]) for c in range(3)
        ] + [(wout_h.at[n], wout.at[n])]
        loads.append([pltpu.make_async_copy(*p, load_sem.at[6 * n + m]) for m, p in enumerate(pieces)])
        pieces = [(w1_h.at[n], w1.at[n]), (w2_h.at[n], w2.at[n])]
        loads.append(
            [pltpu.make_async_copy(*p, load_sem.at[6 * n + 4 + m]) for m, p in enumerate(pieces)]
        )
    for group in loads:
        for copy in group:
            copy.start()
    ex.barrier()

    def save_flow(s, g):
        return pltpu.make_async_copy(flow.at[s, g], flow_h.at[s, g], flow_sem.at[s, g])

    def produce(s, g):
        n = s // 2
        if s == 0:
            value = dot(picker(keep, g), patches[g], 0, 0)
        else:
            before = (s - 1) // 2
            shift = shifts[before, 2 + (s - 1) % 2].reshape(1, D)
            value = flow[s - 1, g] + ex_last.total(g) + shift
        flow[s, g] = value
        save_flow(s, g).start()
        if s == stages:
            return
        unit, _ = norm_parts(value)
        gain, shift = gains[n, s % 2].reshape(1, D), shifts[n, s % 2].reshape(1, D)
        own = ex.own(g)
        gath[s % 2, own] = (unit * gain + shift).astype(BF16)
        tail = gath[s % 2, own, ROWS - 16 : ROWS, 0:256].astype(F32)
        row = lax.broadcasted_iota(jnp.int32, (16, 256), 0)
        tail = jnp.where(row >= LIVE - ROWS + 16, counts[g], tail)
        gath[s % 2, own, ROWS - 16 : ROWS, 0:256] = tail.astype(BF16)
        ex.share(g)

    def saves(s, slot):
        n = s // 2
        if s % 2 == 0:
            pairs = ((gath.at[0], gath_h), (qkv, qkv_h), (prob, prob_h), (att, att_h))
        else:
            pairs = ((gath.at[1], gmlp_h), (act, act_h), (slope, slope_h))
        return [
            pltpu.make_async_copy(a.at[slot], b.at[n, slot], save_sem.at[m, slot])
            for m, (a, b) in enumerate(pairs)
        ]

    def drain(s):
        def one(slot, _):
            for copy in saves(s, slot):
                copy.wait()
            return 0

        lax.fori_loop(0, 8, one, 0)

    ex_last = ex
    for s in range(stages):
        n = s // 2
        ex.stage = s
        produce(s, 0)
        if s == 0:
            produce(s, 1)
        else:
            drain(s - 1)
        for copy in loads[s]:
            copy.wait()

        def step(i, _, s=s, n=n):
            if s:

                @pl.when(i == 2)
                def _():
                    produce(s, 1)

            ex.before(i)
            slot = ex.slot(i)
            x = gath[s % 2, slot]
            if s % 2 == 0:

                def keep_parts(kind, *values):
                    if kind == 0:
                        for c, value in enumerate(values):
                            qkv[slot, :, c * width : (c + 1) * width] = value
                    else:
                        prob[slot, (kind - 1) * ROWS : kind * ROWS] = values[0]

                tail = gath[0, slot, ROWS - 16 : ROWS, 0:256][:, 0:ROWS].astype(F32)
                mixed = attend(
                    x, bias_qv[n, 0:1], bias_qv[n, 1:2], wqkv.at[n], wout.at[n], tail, keep_parts
                )
                att[slot] = mixed
                part[i] = dot(mixed, wout[n])
            else:
                for block in range(hidden // 256):
                    at = slice(block * 256, block * 256 + 256)
                    pre = dot(x, w1[n, :, at]) + bias_fc1[n : n + 1, at]
                    cdf, pdf = erf_parts(pre)
                    act[slot, :, at] = (pre * cdf).astype(BF16)
                    slope[slot, :, at] = (cdf + pre * pdf).astype(BF16)
                part[i] = dot(act[slot], w2[n])
            for copy in saves(s, slot):
                copy.start()
            ex.after(i)
            return 0

        lax.fori_loop(0, 8, step, 0)
    for g in range(GROUPS):
        produce(stages, g)
    drain(stages - 1)
    ex.end()
    for s in range(stages + 1):
        for g in range(GROUPS):
            save_flow(s, g).wait()


VM = pl.BlockSpec(memory_space=pltpu.VMEM)
HB = pl.BlockSpec(memory_space=pl.ANY)


def sds(shape, dtype):
    return jax.ShapeDtypeStruct(shape, dtype)


def params(n):
    return pltpu.CompilerParams(
        collective_id=n, has_side_effects=True, vmem_limit_bytes=67043328
    )


def forward(patches, keep, counts, gains, shifts, bias_qv, bias_fc1, wqkv, wout, w1, w2):
    width, hidden = wout.shape[1], w1.shape[2]
    heads = width // HEAD
    wide = (8, ROWS, D)
    inner = ((8, ROWS, 3 * width), (8, heads * ROWS, ROWS), (8, ROWS, width))
    mlp = ((8, ROWS, hidden), (8, ROWS, hidden))
    kept = (wide,) + inner + (wide,) + mlp
    steps = (2 * LAYERS + 1, GROUPS, ROWS, D)
    dma = pltpu.SemaphoreType.DMA
    return pl.pallas_call(
        forward_kernel,
        out_shape=(sds(steps, F32),) + tuple(sds((LAYERS,) + k, BF16) for k in kept),
        in_specs=[VM] * 7 + [HB] * 4,
        out_specs=(HB,) * 8,
        scratch_shapes=exchange_scratch()
        + [
            pltpu.VMEM(steps, F32),
            pltpu.VMEM((LAYERS, D, 3 * width), BF16),
            pltpu.VMEM((LAYERS, width, D), BF16),
            pltpu.VMEM((LAYERS, D, hidden), BF16),
            pltpu.VMEM((LAYERS, hidden, D), BF16),
        ]
        + [pltpu.VMEM(k, BF16) for k in inner + mlp]
        + [dma((6 * LAYERS,)), dma((4, 8)), dma((2 * LAYERS + 1, GROUPS))],
        compiler_params=params(1),
    )(patches, keep, counts, gains, shifts, bias_qv, bias_fc1, wqkv, wout, w1, w2)


def column_sums(values):
    return jnp.sum(values, axis=0, keepdims=True)


class Scatter:
    def __init__(self, made, halves, arrivals, totals, outs, sems):
        self.made, self.halves, self.arrivals = made, halves, arrivals
        self.totals, self.outs = totals, outs
        self.x_sem, self.z_sem, self.out_sem, self.x_free, self.z_free = sems
        me = lax.axis_index("dp")
        self.x, self.z = me % 2, me // 2
        self.across = me + 1 - 2 * self.x

    def peer(self, k):
        return 2 * ((self.z + k) % 4) + self.x

    def shard(self, k):
        return (self.z + k) % 4

    def over_x(self, kind, part, k):
        n = self.shard(k)
        return to_peer(
            "dp",
            self.made[kind][part].at[1 - self.x, n],
            self.halves[kind][part].at[n],
            self.x_sem.at[kind, part, k, 0],
            self.x_sem.at[kind, part, k, 1],
            self.across,
        )

    def over_z(self, kind, part, k):
        return to_peer(
            "dp",
            self.made[kind][part].at[self.x, self.shard(k)],
            self.arrivals[kind][part].at[k - 1],
            self.z_sem.at[kind, part, k, 0],
            self.z_sem.at[kind, part, k, 1],
            self.peer(k),
        )

    def ready(self, s, part):
        if s >= 2:
            for k in range(4):
                self.over_x(s % 2, part, k).wait_send()
                if k:
                    self.over_z(s % 2, part, k).wait_send()

    def send(self, s, part, k):
        if s >= 2:
            pl.semaphore_wait(self.x_free.at[s % 2, part], 1)
        self.over_x(s % 2, part, k).start()

    def fold(self, s, part, k):
        kind = s % 2
        made, half = self.made[kind][part], self.halves[kind][part]
        total = self.totals[kind][part]
        n = self.shard(k)
        self.over_x(kind, part, k).wait_recv()
        last = isinstance(k, int) and k == 0
        if last and s >= 2:
            self.store(s - 2, part, wait=True)

        def add(i, _):
            at = pl.ds(pl.multiple_of(i * COLS, COLS), COLS)
            both = made[self.x, n, at, :].astype(F32) + half[n, at, :].astype(F32)
            if last:
                total[at, :] = both
            else:
                made[self.x, n, at, :] = both.astype(BF16)
            return 0

        lax.fori_loop(0, half.shape[1] // COLS, add, 0)
        if s < 2:
            pl.semaphore_signal(
                self.x_free.at[kind, part],
                inc=1,
                device_id={"dp": self.across},
                device_id_type=pl.DeviceIdType.MESH,
            )
        if not last:
            if s >= 2:
                pl.semaphore_wait(self.z_free.at[kind, part, k], 1)
            self.over_z(kind, part, k).start()

    def store(self, s, part, wait=False):
        kind, n = s % 2, LAYERS - 1 - s // 2
        total, out = self.totals[kind][part], self.outs[kind][part]
        if kind == 1 and part == 1:
            width = out.shape[-1]
            pairs = [(total.at[:, pl.ds(c * width, width)], out.at[n, c]) for c in range(3)]
        else:
            pairs = [(total, out.at[n])]
        for c, pair in enumerate(pairs):
            copy = pltpu.make_async_copy(*pair, self.out_sem.at[kind, part, c])
            if wait:
                copy.wait()
            else:
                copy.start()

    def finish(self, s, part):
        kind = s % 2
        total, arrivals = self.totals[kind][part], self.arrivals[kind][part]
        for k in range(1, 4):
            self.over_z(kind, part, k).wait_recv()

        def add(i, _):
            at = pl.ds(pl.multiple_of(i * COLS, COLS), COLS)
            value = total[at, :]
            for k in range(3):
                value = value + arrivals[k, at, :].astype(F32)
            total[at, :] = value
            return 0

        lax.fori_loop(0, total.shape[0] // COLS, add, 0)
        self.store(s, part)
        if s < 2:
            for k in range(1, 4):
                pl.semaphore_signal(
                    self.z_free.at[kind, part, k],
                    inc=1,
                    device_id={"dp": self.peer(4 - k)},
                    device_id_type=pl.DeviceIdType.MESH,
                )

    def end(self):
        for s in (2, 3):
            for part in range(2):
                self.ready(s, part)
                self.store(s, part, wait=True)


def to_peer(axis, src, dst, send, recv, peer):
    return pltpu.make_async_remote_copy(
        src_ref=src,
        dst_ref=dst,
        send_sem=send,
        recv_sem=recv,
        device_id={axis: peer},
        device_id_type=pl.DeviceIdType.MESH,
    )


def sum_small(lines, arrived, over_z, out, sem, sc, mine):
    across = to_peer("dp", lines, arrived, sem.at[0, 0], sem.at[1, 0], sc.across)
    across.start()
    across.wait_recv()
    across.wait_send()
    over_z[sc.z] = lines[...] + arrived[...]

    def along(k):
        part = over_z.at[sc.z]
        return to_peer("dp", part, part, sem.at[0, k], sem.at[1, k], sc.peer(k))

    for k in range(1, 4):
        along(k).start()
    for k in range(1, 4):
        along(k).wait_recv()
    out[mine] = over_z[0] + over_z[1] + over_z[2] + over_z[3]

    def around(k):
        part = out.at[mine]
        return to_peer("tensor", part, part, sem.at[0, 3 + k], sem.at[1, 3 + k], (mine + k) % 4)

    for k in range(1, 4):
        around(k).start()
    for k in range(1, 4):
        along(k).wait_send()
        around(k).wait()


def backward_kernel(
    fused,
    cot, keep, gains, flow_h, wqkv_h, wout_h, w1_h, w2_h,
    gath_h, qkv_h, prob_h, att_h, gmlp_h, act_h, slope_h,
    patch_grad, small_out, o_fc2, o_fc1, o_out, o_qkv,
    gath, part, out_po, out_pd, out_y, in_po, in_pd, in_y, ex_sem,
    gradient, source, wqkv, wout, w1, w2, qkv, prob, att, norm_a, act, slope, norm_m,
    pre, triple, lines, cols_m, rows_m, cols_a, rows_a, load_sem, *rest,
):
    ex = Exchange(gath, part, (out_po, out_pd, out_y, in_po, in_pd, in_y), ex_sem)
    width, hidden = wout.shape[0], w1.shape[1]
    stages = 2 * LAYERS
    flat = 8 * ROWS
    made = ((cols_m, rows_m), (cols_a, rows_a))
    outs = ((o_fc2, o_fc1), (o_out, o_qkv))
    if fused:
        halves, arrivals, totals = (
            ((rest[4 * n], rest[4 * n + 1]), (rest[4 * n + 2], rest[4 * n + 3])) for n in range(3)
        )
        small_in, small_z, small_sem = rest[12:15]
        sc = Scatter(made, halves, arrivals, totals, outs, rest[15:20])
        z = sc.z
    else:
        sc, z = None, 0
        save_sem = rest[0]

    def layer(s):
        return LAYERS - 1 - s // 2

    def loads(s):
        n = layer(s)
        if s % 2 == 0:
            pairs = (
                (w2_h.at[n], w2),
                (slope_h.at[n], slope),
                (w1_h.at[n], w1),
                (act_h.at[n], act),
                (gmlp_h.at[n], norm_m),
                (flow_h.at[2 * n + 1], source.at[0]),
            )
        else:
            pairs = tuple(
                (wqkv_h.at[n, c], wqkv.at[:, pl.ds(c * width, width)]) for c in range(3)
            ) + (
                (wout_h.at[n], wout),
                (qkv_h.at[n], qkv),
                (prob_h.at[n], prob),
                (att_h.at[n], att),
                (gath_h.at[n], norm_a),
                (flow_h.at[2 * n], source.at[1]),
            )
        return [
            pltpu.make_async_copy(*pair, load_sem.at[s % 2, m]) for m, pair in enumerate(pairs)
        ]

    for s in range(2):
        for copy in loads(s):
            copy.start()
    barrier = pltpu.get_barrier_semaphore()
    peers = [{"tensor": ex.mate}, {"tensor": ex.far}]
    if fused:
        peers += [{"tensor": ex.diag}, {"dp": sc.across}]
        peers += [{"dp": sc.peer(k)} for k in range(1, 4)]
    for peer in peers:
        pl.semaphore_signal(barrier, inc=1, device_id=peer, device_id_type=pl.DeviceIdType.MESH)
    pl.semaphore_wait(barrier, len(peers))

    def note(at, g, row):
        lines[at : at + 1] = row if g == 0 else lines[at : at + 1] + row

    def produce(s, g):
        if s == 0:
            rounded = cot[g]
            gradient[g] = rounded.astype(F32)
        else:
            n, side = layer(s - 1), s % 2
            gain = gains[n, side].reshape(1, D)
            moved = ex.total(g)
            unit, scale = norm_parts(source[1 - side, g])
            note(2 * n + side, g, column_sums(moved * unit))
            note(4 + 4 * n + side, g, column_sums(moved))
            scaled = moved * gain
            lean = jnp.mean(scaled, axis=-1, keepdims=True)
            tilt = jnp.mean(scaled * unit, axis=-1, keepdims=True)
            grad = gradient[g] + scale * (scaled - lean - unit * tilt)
            rounded = grad.astype(BF16)
            if s < stages:
                gradient[g] = grad
            else:
                pick = picker(keep, g)
                rest_of = (grad - rounded.astype(F32)).astype(BF16)
                patch_grad[g] = dot(pick, rounded) + dot(pick, rest_of)
                return
        if s % 2 == 0:
            note(4 + 4 * layer(s) + 3, g, column_sums(rounded.astype(F32)))
        else:
            note(4 + 4 * layer(s) + 2, g, column_sums(rounded.astype(F32)))
        gath[s % 2, ex.own(g)] = rounded
        ex.share(g)

    def spill(s, part, k):
        m = (z + k) % 4
        return [
            pltpu.make_async_copy(
                made[s % 2][part].at[half, m],
                outs[s % 2][part].at[layer(s), half, m],
                save_sem.at[s % 2, part, k, half],
            )
            for half in range(2)
        ]

    def column_block(s, j):
        k = (j + 1) % 4
        n = (z + k) % 4
        at = pl.ds(pl.multiple_of(n * 256, 256), 256)
        some = gath[s % 2, :, :, at].reshape(flat, 256)
        left = (act, att)[s % 2]
        wide = dot(left[...].reshape(flat, left.shape[-1]), some, 0, 0).astype(BF16)
        out = made[s % 2][0]
        out[0, n] = wide[:, :COLS]
        out[1, n] = wide[:, COLS:]
        if fused:
            sc.send(s, 0, k)
        else:
            for copy in spill(s, 0, k):
                copy.start()

    def row_block(s, j):
        k = (j + 1) % 4
        n = (z + k) % 4
        at = pl.ds(pl.multiple_of(n * 256, 256), 256)
        left, right = ((norm_m, pre), (norm_a, triple))[s % 2]
        some = left[:, :, at].reshape(flat, 256)
        tall = dot(some, right[...].reshape(flat, right.shape[-1]), 0, 0).astype(BF16)
        out = made[s % 2][1]
        out[0, n] = tall[:COLS]
        out[1, n] = tall[COLS:]
        if fused:
            sc.send(s, 1, k)
        else:
            for copy in spill(s, 1, k):
                copy.start()

    def settle(s, part):
        if fused:
            sc.ready(s, part)
        elif s >= 2:
            for k in range(4):
                for copy in spill(s - 2, part, k):
                    copy.wait()

    def columns(s):
        settle(s, 0)

        def one(j, _):
            column_block(s, j)
            return 0

        lax.fori_loop(0, 4, one, 0)

    def some_rows(s, start, count):
        def one(j, _):
            row_block(s, start + j)
            return 0

        lax.fori_loop(0, count, one, 0)

    def bias_sums(s):
        n = layer(s)
        ones = jnp.ones((8, flat), BF16)
        if s % 2 == 0:
            lines[12 + n : 13 + n] = dot(ones, pre[...].reshape(flat, hidden))[0:1]
        else:
            sums = dot(ones, triple[...].reshape(flat, 3 * width))[0:1]
            at = 2 * n * width
            lines[14:15, at : at + width] = sums[:, :width]
            lines[14:15, at + width : at + 2 * width] = sums[:, 2 * width :]

    def folds(s, part, first, count):
        if not fused:
            return
        away = min(first + count, 4) - first

        def one(k, _):
            sc.fold(s, part, k)
            return 0

        if away > 0:
            lax.fori_loop(first, first + away, one, 0)
        if first + count > 4:
            sc.fold(s, part, 0)

    def finish(s):
        if fused:
            for part in range(2):
                sc.finish(s, part)

    lines[15:16] = jnp.zeros((1, D), F32)
    plan = {
        (1, 4): lambda: folds(0, 0, 1, 1),
        (1, 6): lambda: folds(0, 0, 2, 2),
        (1, 8): lambda: folds(0, 0, 4, 1),
        (2, 2): lambda: folds(0, 1, 1, 1),
        (2, 4): lambda: folds(0, 1, 2, 1),
        (2, 6): lambda: folds(0, 1, 3, 2),
        (3, 2): lambda: folds(1, 0, 1, 4),
        (3, 4): lambda: folds(1, 1, 1, 2),
        (3, 6): lambda: folds(1, 1, 3, 2),
        (3, 8): lambda: finish(0),
    }

    for s in range(stages):
        ex.stage = s
        if s:
            columns(s - 1)
        produce(s, 0)
        if s == 0:
            produce(s, 1)
        early = (3, 6)[s % 2]
        for copy in loads(s)[:early]:
            copy.wait()

        def step(i, _, s=s):
            if s:

                @pl.when(i == 2)
                def _():
                    settle(s - 1, 1)

                @pl.when((i == 2) | (i == 4))
                def _():
                    some_rows(s - 1, i - 2, 2)

                @pl.when(i == 2)
                def _():
                    produce(s, 1)

                @pl.when(i == 6)
                def _():
                    bias_sums(s - 1)
                    if s + 1 < stages:
                        for copy in loads(s + 1) if s >= 1 else ():
                            copy.start()

            for (stage, at), task in plan.items():
                if stage == s and at < 8:
                    pl.when(i == at)(task)
            ex.before(i)
            slot = ex.slot(i)
            grad = gath[s % 2, slot]
            if s % 2 == 0:
                for block in range(hidden // 256):
                    at = slice(block * 256, block * 256 + 256)
                    d_act = dot(grad, w2[at, :], 1, 1)
                    pre[slot, :, at] = (d_act * slope[slot, :, at].astype(F32)).astype(BF16)
                part[i] = dot(pre[slot], w1[...], 1, 1)
            else:
                d_att = dot(grad, wout[...], 1, 1).astype(BF16)
                q = qkv[slot, :, 0:width]
                k = qkv[slot, :, width : 2 * width]
                v = qkv[slot, :, 2 * width :]
                d_q = jnp.zeros((ROWS, width), F32)
                d_k = jnp.zeros((ROWS, width), F32)
                d_v = jnp.zeros((ROWS, width), F32)
                for h in range(width // HEAD):
                    mask = head_mask(h, width)
                    d_one = d_att * mask
                    rounded = prob[slot, h * ROWS : (h + 1) * ROWS]
                    weight = rounded.astype(F32)
                    d_prob = dot(d_one, v, 1, 1)
                    centre = jnp.sum(weight * d_prob, axis=-1, keepdims=True)
                    d_scores = (weight * (d_prob - centre)).astype(BF16)
                    d_q = d_q + dot(d_scores, k * mask)
                    d_k = d_k + dot(d_scores, q * mask, 0, 0)
                    d_v = d_v + dot(rounded, d_one, 0, 0)
                triple[slot, :, 0:width] = (d_q * SCALE).astype(BF16)
                triple[slot, :, width : 2 * width] = (d_k * SCALE).astype(BF16)
                triple[slot, :, 2 * width :] = d_v.astype(BF16)
                part[i] = dot(triple[slot], wqkv[...], 1, 1)
            ex.after(i)
            return 0

        lax.fori_loop(0, 8, step, 0)
        for copy in loads(s)[early:]:
            copy.wait()
        if (s, 8) in plan:
            plan[s, 8]()
    last = stages - 1
    columns(last)
    settle(last, 1)
    some_rows(last, 0, 4)
    bias_sums(last)
    for g in range(GROUPS):
        produce(stages, g)
    ex.end()
    if fused:
        folds(2, 0, 1, 2)
        sum_small(lines, small_in, small_z, small_out, small_sem, sc, ex.me)
        finish(1)
        folds(2, 0, 3, 2)
        folds(2, 1, 1, 4)
        folds(3, 0, 1, 4)
        sc.finish(2, 0)
        folds(3, 1, 1, 4)
        sc.finish(2, 1)
        finish(3)
        sc.end()
    else:
        small_out[...] = lines[...]
        for s in (2, 3):
            for side in range(2):
                for k in range(4):
                    for copy in spill(s, side, k):
                        copy.wait()


def backward(fused, cot, keep, gains, flow, wqkv, wout, w1, w2, kept):
    width, hidden = wout.shape[1], w1.shape[2]
    heads = width // HEAD
    wide = (8, ROWS, D)
    dma = pltpu.SemaphoreType.DMA
    tall = D // 256
    mine = ((hidden, COLS), (COLS, hidden), (width, COLS), (COLS, 3 * width))
    blocks = [(2, tall) + m for m in mine]
    if fused:
        outs = [
            sds((LAYERS, hidden, COLS), F32),
            sds((LAYERS, COLS, hidden), F32),
            sds((LAYERS, width, COLS), F32),
            sds((LAYERS, 3, COLS, width), F32),
        ]
        small = sds((4, 16, D), F32)
        regular = pltpu.SemaphoreType.REGULAR
        more = (
            [pltpu.VMEM((4,) + m, BF16) for m in mine]
            + [pltpu.VMEM((3,) + m, BF16) for m in mine]
            + [pltpu.VMEM(m, F32) for m in mine]
            + [pltpu.VMEM((16, D), F32), pltpu.VMEM((4, 16, D), F32), dma((2, 7))]
            + [dma((2, 2, 4, 2)), dma((2, 2, 4, 2)), dma((2, 2, 3))]
            + [regular((2, 2)), regular((2, 2, 4))]
        )
    else:
        outs = [sds((LAYERS,) + b, BF16) for b in blocks]
        small = sds((16, D), F32)
        more = [dma((2, 2, 4, 2))]
    kept_shapes = (
        (8, ROWS, 3 * width), (8, heads * ROWS, ROWS), (8, ROWS, width), wide,
        (8, ROWS, hidden), (8, ROWS, hidden), wide, (8, ROWS, hidden), (8, ROWS, 3 * width),
    )
    return pl.pallas_call(
        partial(backward_kernel, fused),
        out_shape=[sds((GROUPS, ROWS, D), F32), small] + outs,
        in_specs=[VM] * 3 + [HB] * 12,
        out_specs=[VM] * 2 + [HB] * 4,
        scratch_shapes=exchange_scratch()
        + [
            pltpu.VMEM((GROUPS, ROWS, D), F32),
            pltpu.VMEM((2, GROUPS, ROWS, D), F32),
            pltpu.VMEM((D, 3 * width), BF16),
            pltpu.VMEM((width, D), BF16),
            pltpu.VMEM((D, hidden), BF16),
            pltpu.VMEM((hidden, D), BF16),
        ]
        + [pltpu.VMEM(k, BF16) for k in kept_shapes]
        + [pltpu.VMEM((16, D), F32)]
        + [pltpu.VMEM(b, BF16) for b in blocks]
        + [dma((2, 9))]
        + more,
        compiler_params=params(2),
    )(cot, keep, gains, flow, wqkv, wout, w1, w2, *kept)


def to_groups(array, dtype):
    images = array.shape[0] // GROUPS
    rows = array.reshape(GROUPS, images * PATCHES, D)
    return jnp.pad(rows, ((0, 0), (0, ROWS - images * PATCHES), (0, 0))).astype(dtype)


def from_groups(array):
    return array[:, :LIVE].reshape(GROUPS * (LIVE // PATCHES), PATCHES, D)


def collect_weight(partial_grad, split_dim):
    return lax.psum_scatter(
        partial_grad, "dp", scatter_dimension=split_dim, tiled=True
    ).astype(F32)


def join_rows(blocks):
    return jnp.transpose(blocks, (1, 0, 2, 3)).reshape(D, -1)


def join_columns(blocks):
    return jnp.transpose(blocks, (2, 1, 0, 3)).reshape(blocks.shape[2], -1)


def local(
    patches,
    keep_index,
    kept_count,
    norm_gain,
    shifts,
    w_qkv,
    bias_qv,
    w_out,
    w_fc1,
    bias_fc1,
    w_fc2,
    cotangent,
):
    width = w_qkv.shape[-1]
    hidden = w_fc1.shape[-1]
    dp_size, ways = lax.axis_size("dp"), lax.axis_size("tensor")
    assert ways == 4
    per = kept_count.shape[0] // GROUPS
    slot_ids = jnp.arange(PATCHES, dtype=jnp.int32)
    counts = kept_count.reshape(GROUPS, per, 1).astype(F32)
    first = LIVE - ROWS + 16
    counts = jnp.broadcast_to(
        jnp.pad(counts, ((0, 0), (first, 16 - first - per), (0, 0))), (GROUPS, 16, 256)
    )
    places = keep_index.reshape(GROUPS, per, PATCHES) + PATCHES * jnp.arange(per)[:, None]
    places = places.reshape(GROUPS, 1, per * PATCHES)
    places = jnp.pad(places, ((0, 0), (0, 0), (0, ROWS - LIVE)), constant_values=-1)
    wqkv = jnp.transpose(w_qkv, (0, 2, 1, 3))
    flow, *kept = forward(
        to_groups(patches, BF16), places, counts, norm_gain, shifts, bias_qv, bias_fc1,
        wqkv, w_out, w_fc1, w_fc2,
    )
    own_mask = (slot_ids[None, :] < kept_count[:, None])[:, :, None]
    layer_out = from_groups(flow[2 * LAYERS]) * own_mask.astype(F32)
    fused = dp_size == 8 and hidden == D and 4 * width == D
    patch_grad, small, g_fc2, g_fc1, g_out, g_qkv = backward(
        fused, to_groups(cotangent * own_mask.astype(BF16), BF16), places, norm_gain, flow,
        wqkv, w_out, w_fc1, w_fc2, kept,
    )
    grad_patches = from_groups(patch_grad)
    if fused:
        grad_qkv, grad_out, grad_fc1, grad_fc2 = g_qkv, g_out, g_fc1, g_fc2
    else:
        grad_qkv, grad_out, grad_fc1, grad_fc2 = (
            jnp.stack([collect_weight(join(array[n]), split) for n in range(LAYERS)])
            for array, join, split in (
                (g_qkv, join_rows, 0),
                (g_out, join_columns, 1),
                (g_fc1, join_rows, 0),
                (g_fc2, join_columns, 1),
            )
        )
        grad_qkv = jnp.transpose(grad_qkv.reshape(LAYERS, -1, 3, width), (0, 2, 1, 3))
        small = lax.all_gather(lax.psum(small, "dp"), "tensor")
    grad_qkv = jnp.transpose(grad_qkv, (0, 2, 1, 3))
    summed = jnp.sum(small[:, :12], axis=0)
    grad_gain = summed[:4].reshape(LAYERS, 2, D)
    grad_shifts = summed[4:].reshape(LAYERS, 4, D)
    grad_bias_fc1 = jnp.transpose(small[:, 12:14], (1, 0, 2)).reshape(LAYERS, ways * hidden)
    quarters = small[:, 14, : 2 * LAYERS * width].reshape(ways, LAYERS, 2, width)
    grad_bias_qv = jnp.transpose(quarters, (1, 2, 0, 3)).reshape(LAYERS, 2, ways * width)
    return (
        layer_out,
        grad_patches,
        grad_gain,
        grad_shifts,
        grad_qkv,
        grad_bias_qv,
        grad_out,
        grad_fc1,
        grad_bias_fc1,
        grad_fc2,
    )


def solution(mesh):
    in_specs = (
        P(("dp", "tensor"), None, None),
        P(("dp", "tensor"), None),
        P(("dp", "tensor")),
        P(),
        P(),
        P(None, None, None, "tensor"),
        P(None, None, "tensor"),
        P(None, "tensor", None),
        P(None, None, "tensor"),
        P(None, "tensor"),
        P(None, "tensor", None),
        P(("dp", "tensor"), None, None),
    )
    out_specs = (
        P(("dp", "tensor"), None, None),
        P(("dp", "tensor"), None, None),
        P(),
        P(),
        P(None, "dp", None, "tensor"),
        P(),
        P(None, "tensor", "dp"),
        P(None, "dp", "tensor"),
        P(),
        P(None, "tensor", "dp"),
    )
    return jax.shard_map(local, mesh=mesh, in_specs=in_specs, out_specs=out_specs, check_vma=False)
```

```python
from functools import partial

import jax
import jax.numpy as jnp
from jax import lax
from jax.experimental import pallas as pl
from jax.experimental.pallas import tpu as pltpu
from jax.sharding import PartitionSpec as P

D = 1024
HEAD = 64
FF = 4096
LAYERS = 2
PATCHES = 50
EPS = 1e-06
HIGHEST = lax.Precision.HIGHEST
F32 = jnp.float32
BF16 = jnp.bfloat16

GROUPS = 2
ROWS = 160
LIVE = 150
COLS = 128
SCALE = HEAD ** (-0.5)


def dot(a, b, lhs=1, rhs=0):
    return lax.dot_general(a, b, (((lhs,), (rhs,)), ((), ())), preferred_element_type=F32)


def remote(src, dst, send, recv, peer):
    return pltpu.make_async_remote_copy(
        src_ref=src,
        dst_ref=dst,
        send_sem=send,
        recv_sem=recv,
        device_id={"tensor": peer},
        device_id_type=pl.DeviceIdType.MESH,
    )


def norm_parts(values):
    average = jnp.mean(values, axis=-1, keepdims=True)
    centred = values - average
    variance = jnp.mean(centred * centred, axis=-1, keepdims=True)
    scale = lax.rsqrt(variance + EPS)
    return centred * scale, scale


def head_mask(h, width):
    lane = lax.broadcasted_iota(jnp.int32, (1, width), 1)
    return (lane // HEAD == h).astype(F32).astype(BF16)


class Exchange:
    def __init__(self, gath, part, bufs, sems):
        self.gath, self.part = gath, part
        self.out_po, self.out_pd, self.out_y, self.in_po, self.in_pd, self.in_y = bufs
        self.sem = sems
        me = lax.axis_index("tensor")
        self.me = me
        self.mate = me + 1 - 2 * (me % 2)
        self.far = (me + 2) % 4
        self.diag = (self.mate + 2) % 4
        self.stage = 0

    def barrier(self):
        sem = pltpu.get_barrier_semaphore()
        for peer in (self.mate, self.far):
            pl.semaphore_signal(
                sem, inc=1, device_id={"tensor": peer}, device_id_type=pl.DeviceIdType.MESH
            )
        pl.semaphore_wait(sem, 2)

    def own(self, g):
        return GROUPS * self.me + g

    def rows(self, slot):
        return self.gath.at[self.stage % 2, slot]

    def copy(self, kind, g):
        s = self.sem
        own, slot = self.rows(self.own(g)), self.rows(GROUPS * self.far + g)
        src, dst, peer = (
            (own, own, self.far),
            (own, own, self.mate),
            (slot, slot, self.mate),
            (self.out_po.at[g], self.in_po.at[g], self.mate),
            (self.out_pd.at[g], self.in_pd.at[g], self.mate),
            (self.out_y.at[g], self.in_y.at[g], self.far),
        )[kind]
        return remote(src, dst, s.at[0, kind, g], s.at[1, kind, g], peer)

    def again(self, kind, g):
        if self.stage:
            self.copy(kind, g).wait_send()

    def send(self, kind, g):
        self.copy(kind, g).start()

    def share(self, g):
        for kind in range(2):
            self.again(kind, g)
            self.send(kind, g)

    def slot(self, i):
        even = i % 2 == 0
        owner = jnp.where(
            i < 4,
            jnp.where(even, self.me, self.mate),
            jnp.where(even, self.far, self.diag),
        )
        return GROUPS * owner + (i // 2) % 2

    def before(self, i):
        for g in range(GROUPS):

            @pl.when(i == 1 + 2 * g)
            def _():
                self.copy(1, g).wait_recv()

            @pl.when(i == 4 + 2 * g)
            def _():
                self.copy(0, g).wait_recv()
                self.again(2, g)
                self.send(2, g)

            @pl.when(i == 5 + 2 * g)
            def _():
                self.copy(2, g).wait_recv()

    def after(self, i):
        for g in range(GROUPS):

            @pl.when(i == 1 + 2 * g)
            def _():
                self.again(3, g)
                self.out_po[g] = self.part[1 + 2 * g].astype(BF16)
                self.send(3, g)

            @pl.when(i == 5 + 2 * g)
            def _():
                self.again(4, g)
                self.out_pd[g] = self.part[5 + 2 * g].astype(BF16)
                self.send(4, g)
                self.copy(4, g).wait_recv()
                self.again(5, g)
                self.out_y[g] = (self.part[4 + 2 * g] + self.in_pd[g].astype(F32)).astype(BF16)
                self.send(5, g)

    def total(self, g):
        self.copy(3, g).wait_recv()
        self.copy(5, g).wait_recv()
        return self.part[2 * g] + self.in_po[g].astype(F32) + self.in_y[g].astype(F32)

    def end(self):
        for g in range(GROUPS):
            for kind in range(6):
                self.copy(kind, g).wait_send()


def exchange_scratch():
    return [
        pltpu.VMEM((2, 8, ROWS, D), BF16),
        pltpu.VMEM((8, ROWS, D), F32),
    ] + [pltpu.VMEM((GROUPS, ROWS, D), BF16)] * 6 + [pltpu.SemaphoreType.DMA((2, 6, GROUPS))]


def picker(keep, g):
    patch = lax.broadcasted_iota(jnp.int32, (ROWS, ROWS), 0)
    return (keep[g] == patch).astype(F32).astype(BF16)


def attend(x, q_bias, v_bias, wqkv, wout, counts, keep_parts):
    width = wout.shape[0]
    triple = dot(x, wqkv[...])
    q = (triple[:, :width] + q_bias).astype(BF16)
    k = triple[:, width : 2 * width].astype(BF16)
    v = (triple[:, 2 * width :] + v_bias).astype(BF16)
    keep_parts(0, q, k, v)
    lane = lax.broadcasted_iota(jnp.int32, (1, ROWS), 1)
    image = lane // PATCHES
    count = jnp.where(image == 0, counts[6:7], jnp.where(image == 1, counts[7:8], counts[8:9]))
    fits = (lane - image * PATCHES).astype(F32) < count
    row = lax.broadcasted_iota(jnp.int32, (ROWS, ROWS), 0)
    col = lax.broadcasted_iota(jnp.int32, (ROWS, ROWS), 1)
    same = jnp.minimum(row // PATCHES, 2) == col // PATCHES
    veil = jnp.where(same, 0.0, -1e30) + jnp.where(fits, 0.0, -1e30)
    mixed = jnp.zeros((ROWS, width), F32)
    for h in range(width // HEAD):
        mask = head_mask(h, width)
        scores = dot(q * mask, k, 1, 1) * SCALE + veil
        peak = jnp.max(scores, axis=-1, keepdims=True)
        raised = jnp.exp(scores - peak)
        weight = raised * (1.0 / jnp.sum(raised, axis=-1, keepdims=True))
        rounded = weight.astype(BF16)
        keep_parts(1 + h, rounded)
        mixed = mixed + dot(rounded, v * mask)
    return mixed.astype(BF16)


def erf_parts(pre):
    cdf = 0.5 * (1.0 + lax.erf(pre * (0.5 ** 0.5)))
    pdf = jnp.exp(-0.5 * pre * pre) * 0.3989422804014327
    return cdf, pdf


def forward_kernel(
    patches, keep, counts, gains, shifts, bias_qv, bias_fc1, wqkv_h, wout_h, w1_h, w2_h,
    flow_h, gath_h, qkv_h, prob_h, att_h, gmlp_h, act_h, slope_h,
    gath, part, out_po, out_pd, out_y, in_po, in_pd, in_y, ex_sem,
    flow, wqkv, wout, w1, w2, qkv, prob, att, act, slope, load_sem, save_sem, flow_sem,
):
    ex = Exchange(gath, part, (out_po, out_pd, out_y, in_po, in_pd, in_y), ex_sem)
    width, hidden = wout.shape[1], w1.shape[2]
    stages = 2 * LAYERS
    loads = []
    for n in range(LAYERS):
        pieces = [
            (wqkv_h.at[n, c], wqkv.at[n, :, pl.ds(c * width, width)]) for c in range(3)
        ] + [(wout_h.at[n], wout.at[n])]
        loads.append([pltpu.make_async_copy(*p, load_sem.at[6 * n + m]) for m, p in enumerate(pieces)])
        pieces = [(w1_h.at[n], w1.at[n]), (w2_h.at[n], w2.at[n])]
        loads.append(
            [pltpu.make_async_copy(*p, load_sem.at[6 * n + 4 + m]) for m, p in enumerate(pieces)]
        )
    for group in loads:
        for copy in group:
            copy.start()
    ex.barrier()

    def save_flow(s, g):
        return pltpu.make_async_copy(flow.at[s, g], flow_h.at[s, g], flow_sem.at[s, g])

    def produce(s, g):
        n = s // 2
        if s == 0:
            value = dot(picker(keep, g), patches[g], 0, 0)
        else:
            before = (s - 1) // 2
            shift = shifts[before, 2 + (s - 1) % 2].reshape(1, D)
            value = flow[s - 1, g] + ex_last.total(g) + shift
        flow[s, g] = value
        save_flow(s, g).start()
        if s == stages:
            return
        unit, _ = norm_parts(value)
        gain, shift = gains[n, s % 2].reshape(1, D), shifts[n, s % 2].reshape(1, D)
        own = ex.own(g)
        gath[s % 2, own] = (unit * gain + shift).astype(BF16)
        tail = gath[s % 2, own, ROWS - 16 : ROWS, 0:256].astype(F32)
        row = lax.broadcasted_iota(jnp.int32, (16, 256), 0)
        tail = jnp.where(row >= LIVE - ROWS + 16, counts[g], tail)
        gath[s % 2, own, ROWS - 16 : ROWS, 0:256] = tail.astype(BF16)
        ex.share(g)

    def saves(s, slot):
        n = s // 2
        if s % 2 == 0:
            pairs = ((gath.at[0], gath_h), (qkv, qkv_h), (prob, prob_h), (att, att_h))
        else:
            pairs = ((gath.at[1], gmlp_h), (act, act_h), (slope, slope_h))
        return [
            pltpu.make_async_copy(a.at[slot], b.at[n, slot], save_sem.at[m, slot])
            for m, (a, b) in enumerate(pairs)
        ]

    def drain(s):
        def one(slot, _):
            for copy in saves(s, slot):
                copy.wait()
            return 0

        lax.fori_loop(0, 8, one, 0)

    ex_last = ex
    for s in range(stages):
        n = s // 2
        ex.stage = s
        produce(s, 0)
        if s == 0:
            produce(s, 1)
        else:
            drain(s - 1)
        for copy in loads[s]:
            copy.wait()

        def step(i, _, s=s, n=n):
            if s:

                @pl.when(i == 2)
                def _():
                    produce(s, 1)

            ex.before(i)
            slot = ex.slot(i)
            x = gath[s % 2, slot]
            if s % 2 == 0:

                def keep_parts(kind, *values):
                    if kind == 0:
                        for c, value in enumerate(values):
                            qkv[slot, :, c * width : (c + 1) * width] = value
                    else:
                        prob[slot, (kind - 1) * ROWS : kind * ROWS] = values[0]

                tail = gath[0, slot, ROWS - 16 : ROWS, 0:256][:, 0:ROWS].astype(F32)
                mixed = attend(
                    x, bias_qv[n, 0:1], bias_qv[n, 1:2], wqkv.at[n], wout.at[n], tail, keep_parts
                )
                att[slot] = mixed
                part[i] = dot(mixed, wout[n])
            else:
                for block in range(hidden // 256):
                    at = slice(block * 256, block * 256 + 256)
                    pre = dot(x, w1[n, :, at]) + bias_fc1[n : n + 1, at]
                    cdf, pdf = erf_parts(pre)
                    act[slot, :, at] = (pre * cdf).astype(BF16)
                    slope[slot, :, at] = (cdf + pre * pdf).astype(BF16)
                part[i] = dot(act[slot], w2[n])
            for copy in saves(s, slot):
                copy.start()
            ex.after(i)
            return 0

        lax.fori_loop(0, 8, step, 0)
    for g in range(GROUPS):
        produce(stages, g)
    drain(stages - 1)
    ex.end()
    for s in range(stages + 1):
        for g in range(GROUPS):
            save_flow(s, g).wait()


VM = pl.BlockSpec(memory_space=pltpu.VMEM)
HB = pl.BlockSpec(memory_space=pl.ANY)


def sds(shape, dtype):
    return jax.ShapeDtypeStruct(shape, dtype)


def params(n):
    return pltpu.CompilerParams(
        collective_id=n, has_side_effects=True, vmem_limit_bytes=67043328
    )


def forward(patches, keep, counts, gains, shifts, bias_qv, bias_fc1, wqkv, wout, w1, w2):
    width, hidden = wout.shape[1], w1.shape[2]
    heads = width // HEAD
    wide = (8, ROWS, D)
    inner = ((8, ROWS, 3 * width), (8, heads * ROWS, ROWS), (8, ROWS, width))
    mlp = ((8, ROWS, hidden), (8, ROWS, hidden))
    kept = (wide,) + inner + (wide,) + mlp
    steps = (2 * LAYERS + 1, GROUPS, ROWS, D)
    dma = pltpu.SemaphoreType.DMA
    return pl.pallas_call(
        forward_kernel,
        out_shape=(sds(steps, F32),) + tuple(sds((LAYERS,) + k, BF16) for k in kept),
        in_specs=[VM] * 7 + [HB] * 4,
        out_specs=(HB,) * 8,
        scratch_shapes=exchange_scratch()
        + [
            pltpu.VMEM(steps, F32),
            pltpu.VMEM((LAYERS, D, 3 * width), BF16),
            pltpu.VMEM((LAYERS, width, D), BF16),
            pltpu.VMEM((LAYERS, D, hidden), BF16),
            pltpu.VMEM((LAYERS, hidden, D), BF16),
        ]
        + [pltpu.VMEM(k, BF16) for k in inner + mlp]
        + [dma((6 * LAYERS,)), dma((4, 8)), dma((2 * LAYERS + 1, GROUPS))],
        compiler_params=params(1),
    )(patches, keep, counts, gains, shifts, bias_qv, bias_fc1, wqkv, wout, w1, w2)


def column_sums(values):
    return jnp.sum(values, axis=0, keepdims=True)


class Scatter:
    order = (3, 1, 2, 0)

    def __init__(self, made, halves, arrivals, totals, outs, sems):
        self.made, self.halves, self.arrivals = made, halves, arrivals
        self.totals, self.outs = totals, outs
        self.x_sem, self.z_sem, self.out_sem, self.x_free, self.z_free = sems
        me = lax.axis_index("dp")
        self.x, self.z = me % 2, me // 2
        self.across = me + 1 - 2 * self.x
        self.near = self.z + 1 - 2 * (self.z % 2)
        self.far = (self.z + 2) % 4

    def device(self, z):
        return 2 * z + self.x

    def shard(self, k):
        return (self.z, self.near, self.far, (self.near + 2) % 4)[k]

    def number(self, j):
        third = (self.near + 2) % 4
        return jnp.where(
            j < 2, jnp.where(j == 0, third, self.near), jnp.where(j == 2, self.far, self.z)
        )

    def over_x(self, kind, part, j):
        n = self.number(j)
        return to_peer(
            "dp",
            self.made[kind][part].at[1 - self.x, n],
            self.halves[kind][part].at[n],
            self.x_sem.at[kind, part, j, 0],
            self.x_sem.at[kind, part, j, 1],
            self.across,
        )

    def over_z(self, kind, part, k):
        there, slot = {1: (self.near, 0), 3: (self.near, 1), 2: (self.far, 2)}[k]
        return to_peer(
            "dp",
            self.made[kind][part].at[self.x, self.shard(k)],
            self.arrivals[kind][part].at[slot],
            self.z_sem.at[kind, part, slot, 0],
            self.z_sem.at[kind, part, slot, 1],
            self.device(there),
        )

    def ready(self, s, part):
        if s >= 2:
            for j in range(4):
                self.over_x(s % 2, part, j).wait_send()
            for k in (1, 2, 3):
                self.over_z(s % 2, part, k).wait_send()

    def send(self, s, part, j):
        if s >= 2:
            pl.semaphore_wait(self.x_free.at[s % 2, part], 1)
        self.over_x(s % 2, part, j).start()

    def signal(self, sem, device):
        pl.semaphore_signal(
            sem, inc=1, device_id={"dp": device}, device_id_type=pl.DeviceIdType.MESH
        )

    def sum_rows(self, out, terms):
        def one(i, _):
            at = pl.ds(pl.multiple_of(i * COLS, COLS), COLS)
            value = terms[0][at, :].astype(F32)
            for term in terms[1:]:
                value = value + term[at, :].astype(F32)
            out[at, :] = value.astype(out.dtype)
            return 0

        lax.fori_loop(0, out.shape[0] // COLS, one, 0)

    def take(self, s, part, k):
        kind = s % 2
        mine = self.made[kind][part].at[self.x, self.shard(k)]
        terms = [mine, self.halves[kind][part].at[self.shard(k)]]
        self.over_x(kind, part, self.order.index(k)).wait_recv()
        if k == 2:
            self.over_z(kind, part, 3).wait_recv()
            terms.append(self.arrivals[kind][part].at[1])
        if k == 0:
            if s >= 2:
                self.store(s - 2, part, wait=True)
            mine = self.totals[kind][part]
        self.sum_rows(mine, terms)
        if s < 2:
            self.signal(self.x_free.at[kind, part], self.across)
            if k == 2:
                self.signal(self.z_free.at[kind, part, 1], self.device(self.near))
        if k:
            if s >= 2:
                slot = {1: 0, 3: 1, 2: 2}[k]
                pl.semaphore_wait(self.z_free.at[kind, part, slot], 1)
            self.over_z(kind, part, k).start()

    def store(self, s, part, wait=False):
        kind, n = s % 2, LAYERS - 1 - s // 2
        total, out = self.totals[kind][part], self.outs[kind][part]
        if kind == 1 and part == 1:
            width = out.shape[-1]
            pairs = [(total.at[:, pl.ds(c * width, width)], out.at[n, c]) for c in range(3)]
        else:
            pairs = [(total, out.at[n])]
        for c, pair in enumerate(pairs):
            copy = pltpu.make_async_copy(*pair, self.out_sem.at[kind, part, c])
            if wait:
                copy.wait()
            else:
                copy.start()

    def finish(self, s, part):
        kind = s % 2
        total, arrivals = self.totals[kind][part], self.arrivals[kind][part]
        self.over_z(kind, part, 1).wait_recv()
        self.over_z(kind, part, 2).wait_recv()
        self.sum_rows(total, [total, arrivals.at[0], arrivals.at[2]])
        self.store(s, part)
        if s < 2:
            self.signal(self.z_free.at[kind, part, 0], self.device(self.near))
            self.signal(self.z_free.at[kind, part, 2], self.device(self.far))

    def end(self):
        for s in (2, 3):
            for part in range(2):
                self.ready(s, part)
                self.store(s, part, wait=True)


def to_peer(axis, src, dst, send, recv, peer):
    return pltpu.make_async_remote_copy(
        src_ref=src,
        dst_ref=dst,
        send_sem=send,
        recv_sem=recv,
        device_id={axis: peer},
        device_id_type=pl.DeviceIdType.MESH,
    )


class SmallSum:
    def __init__(self, lines, arrived, over_z, out, sem, sc, mine):
        self.lines, self.arrived, self.over_z, self.out = lines, arrived, over_z, out
        self.sem, self.sc, self.mine = sem, sc, mine

    def across(self):
        s = self.sem
        return to_peer("dp", self.lines, self.arrived, s.at[0, 0], s.at[1, 0], self.sc.across)

    def along(self, k):
        part, s = self.over_z.at[self.sc.z], self.sem
        return to_peer("dp", part, part, s.at[0, k], s.at[1, k], self.sc.device((self.sc.z + k) % 4))

    def around(self, k):
        part, s = self.out.at[self.mine], self.sem
        peer = (self.mine + k) % 4
        return to_peer("tensor", part, part, s.at[0, 3 + k], s.at[1, 3 + k], peer)

    def second(self):
        self.across().wait()
        self.over_z[self.sc.z] = self.lines[...] + self.arrived[...]
        for k in range(1, 4):
            self.along(k).start()

    def third(self):
        for k in range(1, 4):
            self.along(k).wait()
        z = self.over_z
        self.out[self.mine] = z[0] + z[1] + z[2] + z[3]
        for k in range(1, 4):
            self.around(k).start()

    def last(self):
        for k in range(1, 4):
            self.around(k).wait()


def backward_kernel(
    fused,
    cot, keep, gains, flow_h, wqkv_h, wout_h, w1_h, w2_h,
    gath_h, qkv_h, prob_h, att_h, gmlp_h, act_h, slope_h,
    patch_grad, small_out, o_fc2, o_fc1, o_out, o_qkv,
    gath, part, out_po, out_pd, out_y, in_po, in_pd, in_y, ex_sem,
    gradient, source, wqkv, wout, w1, w2, qkv, prob, att, norm_a, act, slope, norm_m,
    pre, triple, lines, cols_m, rows_m, cols_a, rows_a, load_sem, *rest,
):
    ex = Exchange(gath, part, (out_po, out_pd, out_y, in_po, in_pd, in_y), ex_sem)
    width, hidden = wout.shape[0], w1.shape[1]
    stages = 2 * LAYERS
    flat = 8 * ROWS
    made = ((cols_m, rows_m), (cols_a, rows_a))
    outs = ((o_fc2, o_fc1), (o_out, o_qkv))
    if fused:
        halves, arrivals, totals = (
            ((rest[4 * n], rest[4 * n + 1]), (rest[4 * n + 2], rest[4 * n + 3])) for n in range(3)
        )
        small_in, small_z, small_sem = rest[12:15]
        sc = Scatter(made, halves, arrivals, totals, outs, rest[15:20])
    else:
        sc = None
        save_sem = rest[0]

    def layer(s):
        return LAYERS - 1 - s // 2

    def loads(s):
        n = layer(s)
        if s % 2 == 0:
            pairs = (
                (w2_h.at[n], w2),
                (slope_h.at[n], slope),
                (w1_h.at[n], w1),
                (act_h.at[n], act),
                (gmlp_h.at[n], norm_m),
                (flow_h.at[2 * n + 1], source.at[0]),
            )
        else:
            pairs = tuple(
                (wqkv_h.at[n, c], wqkv.at[:, pl.ds(c * width, width)]) for c in range(3)
            ) + (
                (wout_h.at[n], wout),
                (qkv_h.at[n], qkv),
                (prob_h.at[n], prob),
                (att_h.at[n], att),
                (gath_h.at[n], norm_a),
                (flow_h.at[2 * n], source.at[1]),
            )
        return [
            pltpu.make_async_copy(*pair, load_sem.at[s % 2, m]) for m, pair in enumerate(pairs)
        ]

    for s in range(2):
        for copy in loads(s):
            copy.start()
    barrier = pltpu.get_barrier_semaphore()
    peers = [{"tensor": ex.mate}, {"tensor": ex.far}]
    if fused:
        peers += [{"tensor": ex.diag}, {"dp": sc.across}]
        peers += [{"dp": sc.device((sc.z + k) % 4)} for k in range(1, 4)]
    for peer in peers:
        pl.semaphore_signal(barrier, inc=1, device_id=peer, device_id_type=pl.DeviceIdType.MESH)
    pl.semaphore_wait(barrier, len(peers))

    def note(at, g, row):
        lines[at : at + 1] = row if g == 0 else lines[at : at + 1] + row

    def produce(s, g):
        if s == 0:
            rounded = cot[g]
            gradient[g] = rounded.astype(F32)
        else:
            n, side = layer(s - 1), s % 2
            gain = gains[n, side].reshape(1, D)
            moved = ex.total(g)
            unit, scale = norm_parts(source[1 - side, g])
            note(2 * n + side, g, column_sums(moved * unit))
            note(4 + 4 * n + side, g, column_sums(moved))
            scaled = moved * gain
            lean = jnp.mean(scaled, axis=-1, keepdims=True)
            tilt = jnp.mean(scaled * unit, axis=-1, keepdims=True)
            grad = gradient[g] + scale * (scaled - lean - unit * tilt)
            rounded = grad.astype(BF16)
            if s < stages:
                gradient[g] = grad
            else:
                pick = picker(keep, g)
                rest_of = (grad - rounded.astype(F32)).astype(BF16)
                patch_grad[g] = dot(pick, rounded) + dot(pick, rest_of)
                return
        if s % 2 == 0:
            note(4 + 4 * layer(s) + 3, g, column_sums(rounded.astype(F32)))
        else:
            note(4 + 4 * layer(s) + 2, g, column_sums(rounded.astype(F32)))
        gath[s % 2, ex.own(g)] = rounded
        ex.share(g)

    def spill(s, part, k):
        return [
            pltpu.make_async_copy(
                made[s % 2][part].at[half, k],
                outs[s % 2][part].at[layer(s), half, k],
                save_sem.at[s % 2, part, k, half],
            )
            for half in range(2)
        ]

    def column_block(s, j):
        n = sc.number(j) if fused else j
        at = pl.ds(pl.multiple_of(n * 256, 256), 256)
        some = gath[s % 2, :, :, at].reshape(flat, 256)
        left = (act, att)[s % 2]
        wide = dot(left[...].reshape(flat, left.shape[-1]), some, 0, 0).astype(BF16)
        out = made[s % 2][0]
        out[0, n] = wide[:, :COLS]
        out[1, n] = wide[:, COLS:]
        if fused:
            if s < stages - 1:
                sc.send(s, 0, j)
        else:
            for copy in spill(s, 0, j):
                copy.start()

    def row_block(s, j):
        n = sc.number(j) if fused else j
        at = pl.ds(pl.multiple_of(n * 256, 256), 256)
        left, right = ((norm_m, pre), (norm_a, triple))[s % 2]
        some = left[:, :, at].reshape(flat, 256)
        tall = dot(some, right[...].reshape(flat, right.shape[-1]), 0, 0).astype(BF16)
        out = made[s % 2][1]
        out[0, n] = tall[:COLS]
        out[1, n] = tall[COLS:]
        if fused:
            if s < stages - 1:
                sc.send(s, 1, j)
        else:
            for copy in spill(s, 1, j):
                copy.start()

    def settle(s, part):
        if fused:
            sc.ready(s, part)
        elif s >= 2:
            for k in range(4):
                for copy in spill(s - 2, part, k):
                    copy.wait()

    def columns(s):
        settle(s, 0)

        def one(j, _):
            column_block(s, j)
            return 0

        lax.fori_loop(0, 4, one, 0)

    def some_rows(s, start, count):
        def one(j, _):
            row_block(s, start + j)
            return 0

        lax.fori_loop(0, count, one, 0)

    def bias_sums(s):
        n = layer(s)
        ones = jnp.ones((8, flat), BF16)
        if s % 2 == 0:
            lines[12 + n : 13 + n] = dot(ones, pre[...].reshape(flat, hidden))[0:1]
        else:
            sums = dot(ones, triple[...].reshape(flat, 3 * width))[0:1]
            at = 2 * n * width
            lines[14:15, at : at + width] = sums[:, :width]
            lines[14:15, at + width : at + 2 * width] = sums[:, 2 * width :]

    def take(*work):
        def run():
            if fused:
                for s, part, k in work:
                    if k == 4:
                        sc.finish(s, part)
                    else:
                        sc.take(s, part, k)

        return run

    lines[15:16] = jnp.zeros((1, D), F32)
    plan = {
        (1, 4): take((0, 0, 3)),
        (1, 6): take((0, 0, 1)),
        (1, 8): take((0, 0, 2)),
        (2, 2): take((0, 0, 0), (0, 1, 3)),
        (2, 4): take((0, 1, 1)),
        (2, 6): take((0, 1, 2)),
        (2, 8): take((0, 1, 0), (0, 0, 4), (1, 0, 3), (1, 0, 1)),
        (3, 2): take((1, 0, 2), (1, 0, 0), (1, 1, 3), (1, 1, 1)),
        (3, 4): take((0, 1, 4), (1, 1, 2)),
        (3, 6): take((1, 0, 4), (1, 1, 0)),
        (3, 8): take((2, 0, 3), (2, 0, 1)),
    }

    for s in range(stages):
        ex.stage = s
        if s:
            columns(s - 1)
        produce(s, 0)
        if s == 0:
            produce(s, 1)
        early = (3, 6)[s % 2]
        for copy in loads(s)[:early]:
            copy.wait()

        def step(i, _, s=s):
            if s:

                @pl.when(i == 2)
                def _():
                    settle(s - 1, 1)

                @pl.when((i == 2) | (i == 4))
                def _():
                    some_rows(s - 1, i - 2, 2)

                @pl.when(i == 2)
                def _():
                    produce(s, 1)

                @pl.when(i == 6)
                def _():
                    bias_sums(s - 1)
                    if s + 1 < stages:
                        for copy in loads(s + 1) if s >= 1 else ():
                            copy.start()

            for (stage, at), task in plan.items():
                if stage == s and at < 8:
                    pl.when(i == at)(task)
            ex.before(i)
            slot = ex.slot(i)
            grad = gath[s % 2, slot]
            if s % 2 == 0:
                for block in range(hidden // 256):
                    at = slice(block * 256, block * 256 + 256)
                    d_act = dot(grad, w2[at, :], 1, 1)
                    pre[slot, :, at] = (d_act * slope[slot, :, at].astype(F32)).astype(BF16)
                part[i] = dot(pre[slot], w1[...], 1, 1)
            else:
                d_att = dot(grad, wout[...], 1, 1).astype(BF16)
                q = qkv[slot, :, 0:width]
                k = qkv[slot, :, width : 2 * width]
                v = qkv[slot, :, 2 * width :]
                d_q = jnp.zeros((ROWS, width), F32)
                d_k = jnp.zeros((ROWS, width), F32)
                d_v = jnp.zeros((ROWS, width), F32)
                for h in range(width // HEAD):
                    mask = head_mask(h, width)
                    d_one = d_att * mask
                    rounded = prob[slot, h * ROWS : (h + 1) * ROWS]
                    weight = rounded.astype(F32)
                    d_prob = dot(d_one, v, 1, 1)
                    centre = jnp.sum(weight * d_prob, axis=-1, keepdims=True)
                    d_scores = (weight * (d_prob - centre)).astype(BF16)
                    d_q = d_q + dot(d_scores, k * mask)
                    d_k = d_k + dot(d_scores, q * mask, 0, 0)
                    d_v = d_v + dot(rounded, d_one, 0, 0)
                triple[slot, :, 0:width] = (d_q * SCALE).astype(BF16)
                triple[slot, :, width : 2 * width] = (d_k * SCALE).astype(BF16)
                triple[slot, :, 2 * width :] = d_v.astype(BF16)
                part[i] = dot(triple[slot], wqkv[...], 1, 1)
            ex.after(i)
            return 0

        lax.fori_loop(0, 8, step, 0)
        for copy in loads(s)[early:]:
            copy.wait()
        if (s, 8) in plan:
            plan[s, 8]()
    last = stages - 1
    columns(last)
    settle(last, 1)
    some_rows(last, 0, 4)
    bias_sums(last)
    take((2, 0, 2), (1, 1, 4))()
    for g in range(GROUPS):
        produce(stages, g)
    if fused:
        tiny = SmallSum(lines, small_in, small_z, small_out, small_sem, sc, ex.me)
        tiny.across().start()
        for side in range(2):
            for j in range(4):
                sc.send(last, side, j)
        take((2, 0, 0), (2, 1, 3), (2, 1, 1), (2, 0, 4), (2, 1, 2), (2, 1, 0))()
        tiny.second()
        take((3, 0, 3), (3, 0, 1), (3, 0, 2), (3, 0, 0))()
        tiny.third()
        take((2, 1, 4), (3, 1, 3), (3, 1, 1), (3, 1, 2), (3, 0, 4), (3, 1, 0), (3, 1, 4))()
        sc.end()
        tiny.last()
    else:
        small_out[...] = lines[...]
        for s in (2, 3):
            for side in range(2):
                for k in range(4):
                    for copy in spill(s, side, k):
                        copy.wait()
    ex.end()


def backward(fused, cot, keep, gains, flow, wqkv, wout, w1, w2, kept):
    width, hidden = wout.shape[1], w1.shape[2]
    heads = width // HEAD
    wide = (8, ROWS, D)
    dma = pltpu.SemaphoreType.DMA
    tall = D // 256
    mine = ((hidden, COLS), (COLS, hidden), (width, COLS), (COLS, 3 * width))
    blocks = [(2, tall) + m for m in mine]
    if fused:
        outs = [
            sds((LAYERS, hidden, COLS), F32),
            sds((LAYERS, COLS, hidden), F32),
            sds((LAYERS, width, COLS), F32),
            sds((LAYERS, 3, COLS, width), F32),
        ]
        small = sds((4, 16, D), F32)
        regular = pltpu.SemaphoreType.REGULAR
        more = (
            [pltpu.VMEM((4,) + m, BF16) for m in mine]
            + [pltpu.VMEM((3,) + m, BF16) for m in mine]
            + [pltpu.VMEM(m, F32) for m in mine]
            + [pltpu.VMEM((16, D), F32), pltpu.VMEM((4, 16, D), F32), dma((2, 7))]
            + [dma((2, 2, 4, 2)), dma((2, 2, 3, 2)), dma((2, 2, 3))]
            + [regular((2, 2)), regular((2, 2, 3))]
        )
    else:
        outs = [sds((LAYERS,) + b, BF16) for b in blocks]
        small = sds((16, D), F32)
        more = [dma((2, 2, 4, 2))]
    kept_shapes = (
        (8, ROWS, 3 * width), (8, heads * ROWS, ROWS), (8, ROWS, width), wide,
        (8, ROWS, hidden), (8, ROWS, hidden), wide, (8, ROWS, hidden), (8, ROWS, 3 * width),
    )
    return pl.pallas_call(
        partial(backward_kernel, fused),
        out_shape=[sds((GROUPS, ROWS, D), F32), small] + outs,
        in_specs=[VM] * 3 + [HB] * 12,
        out_specs=[VM] * 2 + [HB] * 4,
        scratch_shapes=exchange_scratch()
        + [
            pltpu.VMEM((GROUPS, ROWS, D), F32),
            pltpu.VMEM((2, GROUPS, ROWS, D), F32),
            pltpu.VMEM((D, 3 * width), BF16),
            pltpu.VMEM((width, D), BF16),
            pltpu.VMEM((D, hidden), BF16),
            pltpu.VMEM((hidden, D), BF16),
        ]
        + [pltpu.VMEM(k, BF16) for k in kept_shapes]
        + [pltpu.VMEM((16, D), F32)]
        + [pltpu.VMEM(b, BF16) for b in blocks]
        + [dma((2, 9))]
        + more,
        compiler_params=params(2),
    )(cot, keep, gains, flow, wqkv, wout, w1, w2, *kept)


def to_groups(array, dtype):
    images = array.shape[0] // GROUPS
    rows = array.reshape(GROUPS, images * PATCHES, D)
    return jnp.pad(rows, ((0, 0), (0, ROWS - images * PATCHES), (0, 0))).astype(dtype)


def from_groups(array):
    return array[:, :LIVE].reshape(GROUPS * (LIVE // PATCHES), PATCHES, D)


def collect_weight(partial_grad, split_dim):
    return lax.psum_scatter(
        partial_grad, "dp", scatter_dimension=split_dim, tiled=True
    ).astype(F32)


def join_rows(blocks):
    return jnp.transpose(blocks, (1, 0, 2, 3)).reshape(D, -1)


def join_columns(blocks):
    return jnp.transpose(blocks, (2, 1, 0, 3)).reshape(blocks.shape[2], -1)


def local(
    patches,
    keep_index,
    kept_count,
    norm_gain,
    shifts,
    w_qkv,
    bias_qv,
    w_out,
    w_fc1,
    bias_fc1,
    w_fc2,
    cotangent,
):
    width = w_qkv.shape[-1]
    hidden = w_fc1.shape[-1]
    dp_size, ways = lax.axis_size("dp"), lax.axis_size("tensor")
    assert ways == 4
    per = kept_count.shape[0] // GROUPS
    slot_ids = jnp.arange(PATCHES, dtype=jnp.int32)
    counts = kept_count.reshape(GROUPS, per, 1).astype(F32)
    first = LIVE - ROWS + 16
    counts = jnp.broadcast_to(
        jnp.pad(counts, ((0, 0), (first, 16 - first - per), (0, 0))), (GROUPS, 16, 256)
    )
    places = keep_index.reshape(GROUPS, per, PATCHES) + PATCHES * jnp.arange(per)[:, None]
    places = places.reshape(GROUPS, 1, per * PATCHES)
    places = jnp.pad(places, ((0, 0), (0, 0), (0, ROWS - LIVE)), constant_values=-1)
    wqkv = jnp.transpose(w_qkv, (0, 2, 1, 3))
    flow, *kept = forward(
        to_groups(patches, BF16), places, counts, norm_gain, shifts, bias_qv, bias_fc1,
        wqkv, w_out, w_fc1, w_fc2,
    )
    own_mask = (slot_ids[None, :] < kept_count[:, None])[:, :, None]
    layer_out = from_groups(flow[2 * LAYERS]) * own_mask.astype(F32)
    fused = dp_size == 8 and hidden == D and 4 * width == D
    patch_grad, small, g_fc2, g_fc1, g_out, g_qkv = backward(
        fused, to_groups(cotangent * own_mask.astype(BF16), BF16), places, norm_gain, flow,
        wqkv, w_out, w_fc1, w_fc2, kept,
    )
    grad_patches = from_groups(patch_grad)
    if fused:
        grad_qkv, grad_out, grad_fc1, grad_fc2 = g_qkv, g_out, g_fc1, g_fc2
    else:
        grad_qkv, grad_out, grad_fc1, grad_fc2 = (
            jnp.stack([collect_weight(join(array[n]), split) for n in range(LAYERS)])
            for array, join, split in (
                (g_qkv, join_rows, 0),
                (g_out, join_columns, 1),
                (g_fc1, join_rows, 0),
                (g_fc2, join_columns, 1),
            )
        )
        grad_qkv = jnp.transpose(grad_qkv.reshape(LAYERS, -1, 3, width), (0, 2, 1, 3))
        small = lax.all_gather(lax.psum(small, "dp"), "tensor")
    grad_qkv = jnp.transpose(grad_qkv, (0, 2, 1, 3))
    summed = jnp.sum(small[:, :12], axis=0)
    grad_gain = summed[:4].reshape(LAYERS, 2, D)
    grad_shifts = summed[4:].reshape(LAYERS, 4, D)
    grad_bias_fc1 = jnp.transpose(small[:, 12:14], (1, 0, 2)).reshape(LAYERS, ways * hidden)
    quarters = small[:, 14, : 2 * LAYERS * width].reshape(ways, LAYERS, 2, width)
    grad_bias_qv = jnp.transpose(quarters, (1, 2, 0, 3)).reshape(LAYERS, 2, ways * width)
    return (
        layer_out,
        grad_patches,
        grad_gain,
        grad_shifts,
        grad_qkv,
        grad_bias_qv,
        grad_out,
        grad_fc1,
        grad_bias_fc1,
        grad_fc2,
    )


def solution(mesh):
    in_specs = (
        P(("dp", "tensor"), None, None),
        P(("dp", "tensor"), None),
        P(("dp", "tensor")),
        P(),
        P(),
        P(None, None, None, "tensor"),
        P(None, None, "tensor"),
        P(None, "tensor", None),
        P(None, None, "tensor"),
        P(None, "tensor"),
        P(None, "tensor", None),
        P(("dp", "tensor"), None, None),
    )
    out_specs = (
        P(("dp", "tensor"), None, None),
        P(("dp", "tensor"), None, None),
        P(),
        P(),
        P(None, "dp", None, "tensor"),
        P(),
        P(None, "tensor", "dp"),
        P(None, "dp", "tensor"),
        P(),
        P(None, "tensor", "dp"),
    )
    return jax.shard_map(local, mesh=mesh, in_specs=in_specs, out_specs=out_specs, check_vma=False)
```

```python
from functools import partial

import jax
import jax.numpy as jnp
from jax import lax
from jax.experimental import pallas as pl
from jax.experimental.pallas import tpu as pltpu
from jax.sharding import PartitionSpec as P

D = 1024
HEAD = 64
FF = 4096
LAYERS = 2
PATCHES = 50
EPS = 1e-06
HIGHEST = lax.Precision.HIGHEST
F32 = jnp.float32
BF16 = jnp.bfloat16

GROUPS = 2
ROWS = 160
LIVE = 150
COLS = 128
SCALE = HEAD ** (-0.5)


def dot(a, b, lhs=1, rhs=0):
    return lax.dot_general(a, b, (((lhs,), (rhs,)), ((), ())), preferred_element_type=F32)


def remote(src, dst, send, recv, peer):
    return pltpu.make_async_remote_copy(
        src_ref=src,
        dst_ref=dst,
        send_sem=send,
        recv_sem=recv,
        device_id={"tensor": peer},
        device_id_type=pl.DeviceIdType.MESH,
    )


def norm_parts(values):
    average = jnp.mean(values, axis=-1, keepdims=True)
    centred = values - average
    variance = jnp.mean(centred * centred, axis=-1, keepdims=True)
    scale = lax.rsqrt(variance + EPS)
    return centred * scale, scale


def head_mask(h, width):
    lane = lax.broadcasted_iota(jnp.int32, (1, width), 1)
    return (lane // HEAD == h).astype(F32).astype(BF16)


class Exchange:
    def __init__(self, gath, part, bufs, sems):
        self.gath, self.part = gath, part
        self.out_po, self.out_pd, self.out_y, self.in_po, self.in_pd, self.in_y = bufs
        self.sem = sems
        me = lax.axis_index("tensor")
        self.me = me
        self.mate = me + 1 - 2 * (me % 2)
        self.far = (me + 2) % 4
        self.diag = (self.mate + 2) % 4
        self.stage = 0

    def barrier(self):
        sem = pltpu.get_barrier_semaphore()
        for peer in (self.mate, self.far):
            pl.semaphore_signal(
                sem, inc=1, device_id={"tensor": peer}, device_id_type=pl.DeviceIdType.MESH
            )
        pl.semaphore_wait(sem, 2)

    def own(self, g):
        return GROUPS * self.me + g

    def rows(self, slot):
        return self.gath.at[self.stage % 2, slot]

    def copy(self, kind, g):
        s = self.sem
        own, slot = self.rows(self.own(g)), self.rows(GROUPS * self.far + g)
        src, dst, peer = (
            (own, own, self.far),
            (own, own, self.mate),
            (slot, slot, self.mate),
            (self.out_po.at[g], self.in_po.at[g], self.mate),
            (self.out_pd.at[g], self.in_pd.at[g], self.mate),
            (self.out_y.at[g], self.in_y.at[g], self.far),
        )[kind]
        return remote(src, dst, s.at[0, kind, g], s.at[1, kind, g], peer)

    def again(self, kind, g):
        if self.stage:
            self.copy(kind, g).wait_send()

    def send(self, kind, g):
        self.copy(kind, g).start()

    def share(self, g):
        for kind in range(2):
            self.again(kind, g)
            self.send(kind, g)

    def slot(self, i):
        even = i % 2 == 0
        owner = jnp.where(
            i < 4,
            jnp.where(even, self.me, self.mate),
            jnp.where(even, self.far, self.diag),
        )
        return GROUPS * owner + (i // 2) % 2

    def place(self, i):
        return jnp.where(i % 2 == 0, i // 2, 4)

    def before(self, i):
        for g in range(GROUPS):

            @pl.when(i == 1 + 2 * g)
            def _():
                self.copy(1, g).wait_recv()

            @pl.when(i == 4 + 2 * g)
            def _():
                self.copy(0, g).wait_recv()
                self.again(2, g)
                self.send(2, g)

            @pl.when(i == 5 + 2 * g)
            def _():
                self.copy(2, g).wait_recv()

    def after(self, i):
        for g in range(GROUPS):

            @pl.when(i == 1 + 2 * g)
            def _():
                self.again(3, g)
                self.out_po[g] = self.part[4].astype(BF16)
                self.send(3, g)

            @pl.when(i == 5 + 2 * g)
            def _():
                self.again(4, g)
                self.out_pd[g] = self.part[4].astype(BF16)
                self.send(4, g)
                self.copy(4, g).wait_recv()
                self.again(5, g)
                self.out_y[g] = (self.part[2 + g] + self.in_pd[g].astype(F32)).astype(BF16)
                self.send(5, g)

    def total(self, g):
        self.copy(3, g).wait_recv()
        self.copy(5, g).wait_recv()
        return self.part[g] + self.in_po[g].astype(F32) + self.in_y[g].astype(F32)

    def end(self):
        for g in range(GROUPS):
            for kind in range(6):
                self.copy(kind, g).wait_send()


def exchange_scratch():
    return [
        pltpu.VMEM((2, 8, ROWS, D), BF16),
        pltpu.VMEM((5, ROWS, D), F32),
    ] + [pltpu.VMEM((GROUPS, ROWS, D), BF16)] * 6 + [pltpu.SemaphoreType.DMA((2, 6, GROUPS))]


def picker(keep, image):
    patch = lax.broadcasted_iota(jnp.int32, (PATCHES, PATCHES), 0)
    return (keep[image : image + 1] == patch).astype(F32).astype(BF16)


def images_of(g):
    per = LIVE // PATCHES
    return [(g * per + m, m * PATCHES) for m in range(per)]


def live_rows(count, image):
    row = lax.broadcasted_iota(jnp.int32, (PATCHES, D), 0)
    return row < count[image]


def attend(x, q_bias, v_bias, wqkv, wout, counts, keep_parts):
    width = wout.shape[0]
    triple = dot(x, wqkv[...])
    q = (triple[:, :width] + q_bias).astype(BF16)
    k = triple[:, width : 2 * width].astype(BF16)
    v = (triple[:, 2 * width :] + v_bias).astype(BF16)
    keep_parts(0, q, k, v)
    lane = lax.broadcasted_iota(jnp.int32, (1, ROWS), 1)
    image = lane // PATCHES
    count = jnp.where(image == 0, counts[6:7], jnp.where(image == 1, counts[7:8], counts[8:9]))
    fits = (lane - image * PATCHES).astype(F32) < count
    row = lax.broadcasted_iota(jnp.int32, (ROWS, ROWS), 0)
    col = lax.broadcasted_iota(jnp.int32, (ROWS, ROWS), 1)
    same = jnp.minimum(row // PATCHES, 2) == col // PATCHES
    veil = jnp.where(same, 0.0, -1e30) + jnp.where(fits, 0.0, -1e30)
    mixed = jnp.zeros((ROWS, width), F32)
    for h in range(width // HEAD):
        mask = head_mask(h, width)
        scores = dot(q * mask, k, 1, 1) * SCALE + veil
        peak = jnp.max(scores, axis=-1, keepdims=True)
        raised = jnp.exp(scores - peak)
        weight = raised * (1.0 / jnp.sum(raised, axis=-1, keepdims=True))
        rounded = weight.astype(BF16)
        keep_parts(1 + h, rounded)
        mixed = mixed + dot(rounded, v * mask)
    return mixed.astype(BF16)


def erf_parts(pre):
    cdf = 0.5 * (1.0 + lax.erf(pre * (0.5 ** 0.5)))
    pdf = jnp.exp(-0.5 * pre * pre) * 0.3989422804014327
    return cdf, pdf


VM = pl.BlockSpec(memory_space=pltpu.VMEM)
HB = pl.BlockSpec(memory_space=pl.ANY)


def sds(shape, dtype):
    return jax.ShapeDtypeStruct(shape, dtype)


def params(n):
    return pltpu.CompilerParams(
        collective_id=n, has_side_effects=True, vmem_limit_bytes=67043328
    )


def column_sums(values):
    return jnp.sum(values, axis=0, keepdims=True)


class Scatter:
    order = (3, 1, 2, 0)

    def __init__(self, made, halves, arrivals, totals, outs, sems):
        self.made, self.halves, self.arrivals = made, halves, arrivals
        self.totals, self.outs = totals, outs
        self.x_sem, self.z_sem, self.out_sem, self.x_free, self.z_free = sems
        me = lax.axis_index("dp")
        self.x, self.z = me % 2, me // 2
        self.across = me + 1 - 2 * self.x
        self.near = self.z + 1 - 2 * (self.z % 2)
        self.far = (self.z + 2) % 4

    def device(self, z):
        return 2 * z + self.x

    def shard(self, k):
        return (self.z, self.near, self.far, (self.near + 2) % 4)[k]

    def number(self, j):
        third = (self.near + 2) % 4
        return jnp.where(
            j < 2, jnp.where(j == 0, third, self.near), jnp.where(j == 2, self.far, self.z)
        )

    def over_x(self, kind, part, j):
        n = self.number(j)
        return to_peer(
            "dp",
            self.made[kind][part].at[1 - self.x, n],
            self.halves[kind][part].at[n],
            self.x_sem.at[kind, part, j, 0],
            self.x_sem.at[kind, part, j, 1],
            self.across,
        )

    def over_z(self, kind, part, k):
        there, slot = {1: (self.near, 0), 3: (self.near, 1), 2: (self.far, 2)}[k]
        return to_peer(
            "dp",
            self.made[kind][part].at[self.x, self.shard(k)],
            self.arrivals[kind][part].at[slot],
            self.z_sem.at[kind, part, slot, 0],
            self.z_sem.at[kind, part, slot, 1],
            self.device(there),
        )

    def ready(self, s, part):
        if s >= 2:
            for j in range(4):
                self.over_x(s % 2, part, j).wait_send()
            for k in (1, 2, 3):
                self.over_z(s % 2, part, k).wait_send()

    def send(self, s, part, j):
        if s >= 2:
            pl.semaphore_wait(self.x_free.at[s % 2, part], 1)
        self.over_x(s % 2, part, j).start()

    def signal(self, sem, device):
        pl.semaphore_signal(
            sem, inc=1, device_id={"dp": device}, device_id_type=pl.DeviceIdType.MESH
        )

    def sum_rows(self, out, terms):
        def one(i, _):
            at = pl.ds(pl.multiple_of(i * COLS, COLS), COLS)
            value = terms[0][at, :].astype(F32)
            for term in terms[1:]:
                value = value + term[at, :].astype(F32)
            out[at, :] = value.astype(out.dtype)
            return 0

        lax.fori_loop(0, out.shape[0] // COLS, one, 0)

    def take(self, s, part, k):
        kind = s % 2
        mine = self.made[kind][part].at[self.x, self.shard(k)]
        terms = [mine, self.halves[kind][part].at[self.shard(k)]]
        self.over_x(kind, part, self.order.index(k)).wait_recv()
        if k == 2:
            self.over_z(kind, part, 3).wait_recv()
            terms.append(self.arrivals[kind][part].at[1])
        if k == 0:
            if s >= 2:
                self.store(s - 2, part, wait=True)
            mine = self.totals[kind][part]
        self.sum_rows(mine, terms)
        if s < 2:
            self.signal(self.x_free.at[kind, part], self.across)
            if k == 2:
                self.signal(self.z_free.at[kind, part, 1], self.device(self.near))
        if k:
            if s >= 2:
                slot = {1: 0, 3: 1, 2: 2}[k]
                pl.semaphore_wait(self.z_free.at[kind, part, slot], 1)
            self.over_z(kind, part, k).start()

    def store(self, s, part, wait=False):
        kind, n = s % 2, LAYERS - 1 - s // 2
        total, out = self.totals[kind][part], self.outs[kind][part]
        if kind == 1 and part == 1:
            width = out.shape[-1]
            pairs = [(total.at[:, pl.ds(c * width, width)], out.at[n, c]) for c in range(3)]
        else:
            pairs = [(total, out.at[n])]
        for c, pair in enumerate(pairs):
            copy = pltpu.make_async_copy(*pair, self.out_sem.at[kind, part, c])
            if wait:
                copy.wait()
            else:
                copy.start()

    def finish(self, s, part):
        kind = s % 2
        total, arrivals = self.totals[kind][part], self.arrivals[kind][part]
        self.over_z(kind, part, 1).wait_recv()
        self.over_z(kind, part, 2).wait_recv()
        self.sum_rows(total, [total, arrivals.at[0], arrivals.at[2]])
        self.store(s, part)
        if s < 2:
            self.signal(self.z_free.at[kind, part, 0], self.device(self.near))
            self.signal(self.z_free.at[kind, part, 2], self.device(self.far))

    def end(self):
        for s in (2, 3):
            for part in range(2):
                self.ready(s, part)
                self.store(s, part, wait=True)


def to_peer(axis, src, dst, send, recv, peer):
    return pltpu.make_async_remote_copy(
        src_ref=src,
        dst_ref=dst,
        send_sem=send,
        recv_sem=recv,
        device_id={axis: peer},
        device_id_type=pl.DeviceIdType.MESH,
    )


class SmallSum:
    def __init__(self, lines, arrived, over_z, out, sem, sc, mine):
        self.lines, self.arrived, self.over_z, self.out = lines, arrived, over_z, out
        self.sem, self.sc, self.mine = sem, sc, mine

    def across(self):
        s = self.sem
        return to_peer("dp", self.lines, self.arrived, s.at[0, 0], s.at[1, 0], self.sc.across)

    def along(self, k):
        part, s = self.over_z.at[self.sc.z], self.sem
        return to_peer("dp", part, part, s.at[0, k], s.at[1, k], self.sc.device((self.sc.z + k) % 4))

    def around(self, k):
        part, s = self.out.at[self.mine], self.sem
        peer = (self.mine + k) % 4
        return to_peer("tensor", part, part, s.at[0, 3 + k], s.at[1, 3 + k], peer)

    def second(self):
        self.across().wait()
        self.over_z[self.sc.z] = self.lines[...] + self.arrived[...]
        for k in range(1, 4):
            self.along(k).start()

    def third(self):
        for k in range(1, 4):
            self.along(k).wait()
        z = self.over_z
        self.out[self.mine] = z[0] + z[1] + z[2] + z[3]
        for k in range(1, 4):
            self.around(k).start()

    def last(self):
        for k in range(1, 4):
            self.around(k).wait()


def step_kernel(
    fused,
    count, patches, cot, keep, gains, shifts, bias_qv, bias_fc1, wqkv_h, wout_h, w1_h, w2_h,
    layer_h, patch_h, small_out, o_fc2, o_fc1, o_out, o_qkv,
    flow_h, gath_h, qkv_h, prob_h, att_h, gmlp_h, act_h, slope_h,
    gath, part, out_po, out_pd, out_y, in_po, in_pd, in_y, ex_sem,
    gradient, source, final, wqkv, wout, w1, w2,
    qkv, prob, att, norm_a, act, slope, norm_m,
    pre, triple, lines, cols_m, rows_m, cols_a, rows_a, load_sem, keep_sem, flow_sem, *rest,
):
    ex = Exchange(gath, part, (out_po, out_pd, out_y, in_po, in_pd, in_y), ex_sem)
    width, hidden = wout.shape[0], w1.shape[1]
    stages = 2 * LAYERS
    flat = 8 * ROWS
    made = ((cols_m, rows_m), (cols_a, rows_a))
    outs = ((o_fc2, o_fc1), (o_out, o_qkv))
    if fused:
        halves, arrivals, totals = (
            ((rest[4 * n], rest[4 * n + 1]), (rest[4 * n + 2], rest[4 * n + 3])) for n in range(3)
        )
        small_in, small_z, small_sem = rest[12:15]
        sc = Scatter(made, halves, arrivals, totals, outs, rest[15:20])
    else:
        sc = None
        save_sem = rest[0]

    def layer(s):
        return LAYERS - 1 - s // 2

    def loads(s):
        n = layer(s)
        if s < 2:
            return []
        if s % 2 == 0:
            pairs = (
                (w2_h.at[n], w2),
                (slope_h, slope),
                (w1_h.at[n], w1),
                (act_h, act),
                (gmlp_h, norm_m),
                (flow_h.at[1], source.at[0]),
            )
        else:
            pairs = tuple(
                (wqkv_h.at[n, c], wqkv.at[:, pl.ds(c * width, width)]) for c in range(3)
            ) + (
                (wout_h.at[n], wout),
                (qkv_h, qkv),
                (prob_h, prob),
                (att_h, att),
                (gath_h, norm_a),
                (flow_h.at[0], source.at[1]),
            )
        return [
            pltpu.make_async_copy(*pair, load_sem.at[s % 2, m]) for m, pair in enumerate(pairs)
        ]

    def forward_loads(s):
        n = s // 2
        if s % 2 == 0:
            pairs = [
                (wqkv_h.at[n, c], wqkv.at[:, pl.ds(c * width, width)]) for c in range(3)
            ] + [(wout_h.at[n], wout)]
        else:
            pairs = [(w1_h.at[n], w1), (w2_h.at[n], w2)]
        return [
            pltpu.make_async_copy(*pair, load_sem.at[s % 2, m]) for m, pair in enumerate(pairs)
        ]

    for s in range(2):
        for copy in forward_loads(s):
            copy.start()
    barrier = pltpu.get_barrier_semaphore()
    peers = [{"tensor": ex.mate}, {"tensor": ex.far}]
    if fused:
        peers += [{"tensor": ex.diag}, {"dp": sc.across}]
        peers += [{"dp": sc.device((sc.z + k) % 4)} for k in range(1, 4)]
    for peer in peers:
        pl.semaphore_signal(barrier, inc=1, device_id=peer, device_id_type=pl.DeviceIdType.MESH)
    pl.semaphore_wait(barrier, len(peers))

    def hold(s):
        return final if s == stages else source.at[(s + 1) % 2]

    def save_flow(s, g):
        out = layer_h if s == stages else flow_h.at[s]
        return pltpu.make_async_copy(hold(s).at[g], out.at[g], flow_sem.at[s % 2, g])

    def begin(s, g):
        n = s // 2
        held = hold(s)
        if 2 <= s < stages:
            save_flow(s - 2, g).wait()
        if s == 0:
            for image, at in images_of(g):
                held[g, at : at + PATCHES] = dot(picker(keep, image), patches[image], 0, 0)
            held[g, LIVE:] = jnp.zeros((ROWS - LIVE, D), F32)
            value = held[g]
        else:
            shift = shifts[(s - 1) // 2, 2 + (s - 1) % 2].reshape(1, D)
            value = hold(s - 1)[g] + ex.total(g) + shift
            held[g] = value
        if s < 2 or s == stages:
            save_flow(s, g).start()
        if s == stages:
            return
        unit, _ = norm_parts(value)
        gain, shift = gains[n, s % 2].reshape(1, D), shifts[n, s % 2].reshape(1, D)
        own = ex.own(g)
        gath[s % 2, own] = (unit * gain + shift).astype(BF16)
        tail = gath[s % 2, own, ROWS - 16 : ROWS, 0:256].astype(F32)
        row = lax.broadcasted_iota(jnp.int32, (16, 256), 0) - (LIVE - ROWS + 16)
        for m, (image, _) in enumerate(images_of(g)):
            tail = jnp.where(row == m, count[image].astype(F32), tail)
        gath[s % 2, own, ROWS - 16 : ROWS, 0:256] = tail.astype(BF16)
        ex.share(g)

    def saves(s, slot):
        if s == 0:
            pairs = (
                (gath.at[0, slot], gath_h),
                (qkv.at[slot], qkv_h),
                (prob.at[slot], prob_h),
                (att.at[slot], att_h),
            )
        elif s == 1:
            pairs = ((gath.at[1, slot], gmlp_h), (act.at[slot], act_h), (slope.at[slot], slope_h))
        else:
            pairs = ((gath.at[s % 2, slot], (norm_a, norm_m)[s % 2]),)
        return [
            pltpu.make_async_copy(a, b.at[slot], keep_sem.at[m, slot])
            for m, (a, b) in enumerate(pairs)
        ]

    def drain(s):
        def one(slot, _):
            for copy in saves(s, slot):
                copy.wait()
            return 0

        lax.fori_loop(0, 8, one, 0)

    for s in range(stages):
        n = s // 2
        ex.stage = s
        begin(s, 0)
        if s == 0:
            begin(s, 1)
        else:
            drain(s - 1)
        for copy in forward_loads(s):
            copy.wait()
        if 1 <= s < stages - 1:
            for copy in forward_loads(s + 1):
                copy.start()

        def step(i, _, s=s, n=n):
            if s:

                @pl.when(i == 2)
                def _():
                    begin(s, 1)

            ex.before(i)
            slot = ex.slot(i)
            x = gath[s % 2, slot]
            if s % 2 == 0:

                def keep_parts(kind, *values):
                    if kind == 0:
                        for c, value in enumerate(values):
                            qkv[slot, :, c * width : (c + 1) * width] = value
                    else:
                        prob[slot, (kind - 1) * ROWS : kind * ROWS] = values[0]

                tail = gath[0, slot, ROWS - 16 : ROWS, 0:256][:, 0:ROWS].astype(F32)
                mixed = attend(
                    x, bias_qv[n, 0:1], bias_qv[n, 1:2], wqkv, wout, tail, keep_parts
                )
                att[slot] = mixed
                part[ex.place(i)] = dot(mixed, wout[...])
            else:
                for block in range(hidden // 256):
                    at = slice(block * 256, block * 256 + 256)
                    pre_act = dot(x, w1[:, at]) + bias_fc1[n : n + 1, at]
                    cdf, pdf = erf_parts(pre_act)
                    act[slot, :, at] = (pre_act * cdf).astype(BF16)
                    slope[slot, :, at] = (cdf + pre_act * pdf).astype(BF16)
                part[ex.place(i)] = dot(act[slot], w2[...])
            for copy in saves(s, slot):
                copy.start()
            ex.after(i)
            return 0

        lax.fori_loop(0, 8, step, 0)

    def note(at, g, row):
        lines[at : at + 1] = row if g == 0 else lines[at : at + 1] + row

    def produce(s, g):
        if s == 0:
            begin(stages, g)
            gradient[g, LIVE:] = jnp.zeros((ROWS - LIVE, D), F32)
            for image, at in images_of(g):
                piece = jnp.where(live_rows(count, image), cot[image].astype(F32), 0.0)
                gradient[g, at : at + PATCHES] = piece
            rounded = gradient[g].astype(BF16)
        else:
            n, side = layer(s - 1), s % 2
            gain = gains[n, side].reshape(1, D)
            moved = ex.total(g)
            unit, scale = norm_parts(source[1 - side, g])
            note(2 * n + side, g, column_sums(moved * unit))
            note(4 + 4 * n + side, g, column_sums(moved))
            scaled = moved * gain
            lean = jnp.mean(scaled, axis=-1, keepdims=True)
            tilt = jnp.mean(scaled * unit, axis=-1, keepdims=True)
            grad = gradient[g] + scale * (scaled - lean - unit * tilt)
            rounded = grad.astype(BF16)
            if s < stages:
                gradient[g] = grad
            else:
                gradient[g] = grad
                save_flow(stages, g).wait()
                for image, at in images_of(g):
                    exact = gradient[g, at : at + PATCHES]
                    high = exact.astype(BF16)
                    low = (exact - high.astype(F32)).astype(BF16)
                    pick = picker(keep, image)
                    final[g, at : at + PATCHES] = dot(pick, high) + dot(pick, low)
                pltpu.make_async_copy(final.at[g], patch_h.at[g], flow_sem.at[0, g]).start()
                return
        if s % 2 == 0:
            note(4 + 4 * layer(s) + 3, g, column_sums(rounded.astype(F32)))
        else:
            note(4 + 4 * layer(s) + 2, g, column_sums(rounded.astype(F32)))
        gath[s % 2, ex.own(g)] = rounded
        ex.share(g)

    def spill(s, part, k):
        return [
            pltpu.make_async_copy(
                made[s % 2][part].at[half, k],
                outs[s % 2][part].at[layer(s), half, k],
                save_sem.at[s % 2, part, k, half],
            )
            for half in range(2)
        ]

    def column_block(s, j):
        n = sc.number(j) if fused else j
        at = pl.ds(pl.multiple_of(n * 256, 256), 256)
        some = gath[s % 2, :, :, at].reshape(flat, 256)
        left = (act, att)[s % 2]
        wide = dot(left[...].reshape(flat, left.shape[-1]), some, 0, 0).astype(BF16)
        out = made[s % 2][0]
        out[0, n] = wide[:, :COLS]
        out[1, n] = wide[:, COLS:]
        if fused:
            if s < stages - 1:
                sc.send(s, 0, j)
        else:
            for copy in spill(s, 0, j):
                copy.start()

    def row_block(s, j):
        n = sc.number(j) if fused else j
        at = pl.ds(pl.multiple_of(n * 256, 256), 256)
        left, right = ((norm_m, pre), (norm_a, triple))[s % 2]
        some = left[:, :, at].reshape(flat, 256)
        tall = dot(some, right[...].reshape(flat, right.shape[-1]), 0, 0).astype(BF16)
        out = made[s % 2][1]
        out[0, n] = tall[:COLS]
        out[1, n] = tall[COLS:]
        if fused:
            if s < stages - 1:
                sc.send(s, 1, j)
        else:
            for copy in spill(s, 1, j):
                copy.start()

    def settle(s, part):
        if fused:
            sc.ready(s, part)
        elif s >= 2:
            for k in range(4):
                for copy in spill(s - 2, part, k):
                    copy.wait()

    def columns(s):
        settle(s, 0)

        def one(j, _):
            column_block(s, j)
            return 0

        lax.fori_loop(0, 4, one, 0)

    def some_rows(s, start, count):
        def one(j, _):
            row_block(s, start + j)
            return 0

        lax.fori_loop(0, count, one, 0)

    def bias_sums(s):
        n = layer(s)
        ones = jnp.ones((8, flat), BF16)
        if s % 2 == 0:
            lines[12 + n : 13 + n] = dot(ones, pre[...].reshape(flat, hidden))[0:1]
        else:
            sums = dot(ones, triple[...].reshape(flat, 3 * width))[0:1]
            at = 2 * n * width
            lines[14:15, at : at + width] = sums[:, :width]
            lines[14:15, at + width : at + 2 * width] = sums[:, 2 * width :]

    def take(*work):
        def run():
            if fused:
                for s, part, k in work:
                    if k == 4:
                        sc.finish(s, part)
                    else:
                        sc.take(s, part, k)

        return run

    lines[15:16] = jnp.zeros((1, D), F32)
    plan = {
        (1, 4): take((0, 0, 3)),
        (1, 6): take((0, 0, 1)),
        (1, 8): take((0, 0, 2)),
        (2, 2): take((0, 0, 0), (0, 1, 3)),
        (2, 4): take((0, 1, 1)),
        (2, 6): take((0, 1, 2)),
        (2, 8): take((0, 1, 0), (0, 0, 4), (1, 0, 3), (1, 0, 1)),
        (3, 2): take((1, 0, 2), (1, 0, 0), (1, 1, 3), (1, 1, 1)),
        (3, 4): take((0, 1, 4), (1, 1, 2)),
        (3, 6): take((1, 0, 4), (1, 1, 0)),
        (3, 8): take((2, 0, 3), (2, 0, 1)),
    }

    for s in range(stages):
        ex.stage = stages + s
        if s:
            columns(s - 1)
        produce(s, 0)
        if s == 0:
            drain(stages - 1)
        early = (3, 6)[s % 2]
        for copy in loads(s)[:early]:
            copy.wait()

        def step(i, _, s=s):
            if s:

                @pl.when(i == 2)
                def _():
                    settle(s - 1, 1)

                @pl.when((i == 2) | (i == 4))
                def _():
                    some_rows(s - 1, i - 2, 2)

            @pl.when(i == 2)
            def _():
                produce(s, 1)

            if s:

                @pl.when(i == 6)
                def _():
                    bias_sums(s - 1)
                    if s + 1 < stages:
                        for copy in loads(s + 1) if s >= 1 else ():
                            copy.start()

            for (stage, at), task in plan.items():
                if stage == s and at < 8:
                    pl.when(i == at)(task)
            ex.before(i)
            slot = ex.slot(i)
            grad = gath[s % 2, slot]
            if s % 2 == 0:
                for block in range(hidden // 256):
                    at = slice(block * 256, block * 256 + 256)
                    d_act = dot(grad, w2[at, :], 1, 1)
                    pre[slot, :, at] = (d_act * slope[slot, :, at].astype(F32)).astype(BF16)
                part[ex.place(i)] = dot(pre[slot], w1[...], 1, 1)
            else:
                d_att = dot(grad, wout[...], 1, 1).astype(BF16)
                q = qkv[slot, :, 0:width]
                k = qkv[slot, :, width : 2 * width]
                v = qkv[slot, :, 2 * width :]
                d_q = jnp.zeros((ROWS, width), F32)
                d_k = jnp.zeros((ROWS, width), F32)
                d_v = jnp.zeros((ROWS, width), F32)
                for h in range(width // HEAD):
                    mask = head_mask(h, width)
                    d_one = d_att * mask
                    rounded = prob[slot, h * ROWS : (h + 1) * ROWS]
                    weight = rounded.astype(F32)
                    d_prob = dot(d_one, v, 1, 1)
                    centre = jnp.sum(weight * d_prob, axis=-1, keepdims=True)
                    d_scores = (weight * (d_prob - centre)).astype(BF16)
                    d_q = d_q + dot(d_scores, k * mask)
                    d_k = d_k + dot(d_scores, q * mask, 0, 0)
                    d_v = d_v + dot(rounded, d_one, 0, 0)
                triple[slot, :, 0:width] = (d_q * SCALE).astype(BF16)
                triple[slot, :, width : 2 * width] = (d_k * SCALE).astype(BF16)
                triple[slot, :, 2 * width :] = d_v.astype(BF16)
                part[ex.place(i)] = dot(triple[slot], wqkv[...], 1, 1)
            ex.after(i)
            return 0

        lax.fori_loop(0, 8, step, 0)
        for copy in loads(s)[early:]:
            copy.wait()
        if (s, 8) in plan:
            plan[s, 8]()
    last = stages - 1
    columns(last)
    settle(last, 1)
    some_rows(last, 0, 4)
    bias_sums(last)
    take((2, 0, 2), (1, 1, 4))()
    for g in range(GROUPS):
        produce(stages, g)
    if fused:
        tiny = SmallSum(lines, small_in, small_z, small_out, small_sem, sc, ex.me)
        tiny.across().start()
        for side in range(2):
            for j in range(4):
                sc.send(last, side, j)
        take((2, 0, 0), (2, 1, 3), (2, 1, 1), (2, 0, 4), (2, 1, 2), (2, 1, 0))()
        tiny.second()
        take((3, 0, 3), (3, 0, 1), (3, 0, 2), (3, 0, 0))()
        tiny.third()
        take((2, 1, 4), (3, 1, 3), (3, 1, 1), (3, 1, 2), (3, 0, 4), (3, 1, 0), (3, 1, 4))()
        sc.end()
        tiny.last()
    else:
        small_out[...] = lines[...]
        for s in (2, 3):
            for side in range(2):
                for k in range(4):
                    for copy in spill(s, side, k):
                        copy.wait()
    ex.end()
    for g in range(GROUPS):
        pltpu.make_async_copy(final.at[g], patch_h.at[g], flow_sem.at[0, g]).wait()


def run_step(fused, count, patches, cot, keep, gains, shifts, bias_qv, bias_fc1, wqkv, wout, w1, w2):
    width, hidden = wout.shape[1], w1.shape[2]
    heads = width // HEAD
    wide, own = (8, ROWS, D), (GROUPS, ROWS, D)
    dma = pltpu.SemaphoreType.DMA
    tall = D // 256
    mine = ((hidden, COLS), (COLS, hidden), (width, COLS), (COLS, 3 * width))
    blocks = [(2, tall) + m for m in mine]
    if fused:
        outs = [
            sds((LAYERS, hidden, COLS), F32),
            sds((LAYERS, COLS, hidden), F32),
            sds((LAYERS, width, COLS), F32),
            sds((LAYERS, 3, COLS, width), F32),
        ]
        small = sds((4, 16, D), F32)
        regular = pltpu.SemaphoreType.REGULAR
        more = (
            [pltpu.VMEM((4,) + m, BF16) for m in mine]
            + [pltpu.VMEM((3,) + m, BF16) for m in mine]
            + [pltpu.VMEM(m, F32) for m in mine]
            + [pltpu.VMEM((16, D), F32), pltpu.VMEM((4, 16, D), F32), dma((2, 7))]
            + [dma((2, 2, 4, 2)), dma((2, 2, 3, 2)), dma((2, 2, 3))]
            + [regular((2, 2)), regular((2, 2, 3))]
        )
    else:
        outs = [sds((LAYERS,) + b, BF16) for b in blocks]
        small = sds((16, D), F32)
        more = [dma((2, 2, 4, 2))]
    inner = ((8, ROWS, 3 * width), (8, heads * ROWS, ROWS), (8, ROWS, width))
    mlp = ((8, ROWS, hidden), (8, ROWS, hidden))
    saved = (wide,) + inner + (wide,) + mlp
    return pl.pallas_call(
        partial(step_kernel, fused),
        out_shape=[sds(own, F32), sds(own, F32), small]
        + outs
        + [sds((2,) + own, F32)]
        + [sds(k, BF16) for k in saved],
        in_specs=[pl.BlockSpec(memory_space=pltpu.SMEM)] + [VM] * 7 + [HB] * 4,
        out_specs=[HB] * 2 + [VM] + [HB] * 12,
        scratch_shapes=exchange_scratch()
        + [
            pltpu.VMEM(own, F32),
            pltpu.VMEM((2,) + own, F32),
            pltpu.VMEM(own, F32),
            pltpu.VMEM((D, 3 * width), BF16),
            pltpu.VMEM((width, D), BF16),
            pltpu.VMEM((D, hidden), BF16),
            pltpu.VMEM((hidden, D), BF16),
        ]
        + [pltpu.VMEM(k, BF16) for k in inner + (wide,) + mlp + (wide,)]
        + [pltpu.VMEM((8, ROWS, hidden), BF16), pltpu.VMEM((8, ROWS, 3 * width), BF16)]
        + [pltpu.VMEM((16, D), F32)]
        + [pltpu.VMEM(b, BF16) for b in blocks]
        + [dma((2, 9)), dma((4, 8)), dma((2, GROUPS))]
        + more,
        compiler_params=params(1),
    )(count, patches, cot, keep, gains, shifts, bias_qv, bias_fc1, wqkv, wout, w1, w2)[:7]


def deliver_kernel(
    count, layer, patch, small, a_h, b_h, c_h, d_h,
    layer_out, patch_out, gain, shift, qv, fc1, a_out, b_out, c_out, d_out,
    a, b, c, d, sems,
):
    held = ((a_h, a, a_out), (b_h, b, b_out), (c_h, c, c_out), (d_h, d, d_out))

    def inward(n):
        return pltpu.make_async_copy(held[n][0], held[n][1], sems.at[0, n])

    def outward(n):
        return pltpu.make_async_copy(held[n][1], held[n][2], sems.at[1, n])

    for n in range(4):
        inward(n).start()
    for g in range(GROUPS):
        for image, at in images_of(g):
            rows = layer[g, at : at + PATCHES]
            layer_out[image] = jnp.where(live_rows(count, image), rows, 0.0)
            patch_out[image] = patch[g, at : at + PATCHES]
    for n in range(4):
        inward(n).wait()
        outward(n).start()
    summed = small[0, 0:12] + small[1, 0:12] + small[2, 0:12] + small[3, 0:12]
    for n in range(LAYERS):
        gain[n] = summed[2 * n : 2 * n + 2]
        shift[n] = summed[4 + 4 * n : 8 + 4 * n]
        for t in range(4):
            hidden = fc1.shape[1] // 4
            fc1[n : n + 1, t * hidden : (t + 1) * hidden] = small[t, 12 + n : 13 + n]
            width = D // 4
            for side in range(2):
                at = (2 * n + side) * width
                piece = small[t, 14:15, at : at + width]
                qv[n, side : side + 1, t * width : (t + 1) * width] = piece
    for n in range(4):
        outward(n).wait()


def deliver(count, layer, patch, small, grads):
    images = (GROUPS * LIVE // PATCHES, PATCHES, D)
    shapes = [g.shape for g in grads]
    return pl.pallas_call(
        deliver_kernel,
        out_shape=[
            sds(images, F32),
            sds(images, F32),
            sds((LAYERS, 2, D), F32),
            sds((LAYERS, 4, D), F32),
            sds((LAYERS, 2, D), F32),
            sds((LAYERS, FF), F32),
        ]
        + [sds(s, F32) for s in shapes],
        in_specs=[pl.BlockSpec(memory_space=pltpu.SMEM)] + [VM] * 3 + [HB] * 4,
        out_specs=[VM] * 6 + [HB] * 4,
        scratch_shapes=[pltpu.VMEM(s, F32) for s in shapes] + [pltpu.SemaphoreType.DMA((2, 4))],
    )(count, layer, patch, small, *grads)


def from_groups(array):
    return array[:, :LIVE].reshape(GROUPS * (LIVE // PATCHES), PATCHES, D)


def collect_weight(partial_grad, split_dim):
    return lax.psum_scatter(
        partial_grad, "dp", scatter_dimension=split_dim, tiled=True
    ).astype(F32)


def join_rows(blocks):
    return jnp.transpose(blocks, (1, 0, 2, 3)).reshape(D, -1)


def join_columns(blocks):
    return jnp.transpose(blocks, (2, 1, 0, 3)).reshape(blocks.shape[2], -1)


def local(
    patches,
    keep_index,
    kept_count,
    norm_gain,
    shifts,
    w_qkv,
    bias_qv,
    w_out,
    w_fc1,
    bias_fc1,
    w_fc2,
    cotangent,
):
    width = w_qkv.shape[-1]
    hidden = w_fc1.shape[-1]
    dp_size, ways = lax.axis_size("dp"), lax.axis_size("tensor")
    assert ways == 4
    wqkv = jnp.transpose(w_qkv, (0, 2, 1, 3))
    fused = dp_size == 8 and hidden == D and 4 * width == D
    layer, patch, small, g_fc2, g_fc1, g_out, g_qkv = run_step(
        fused, kept_count, patches, cotangent, keep_index, norm_gain, shifts, bias_qv, bias_fc1,
        wqkv, w_out, w_fc1, w_fc2,
    )
    if fused:
        layer_out, grad_patches, gain, shift, qv, fc1, g_fc2, g_fc1, g_out, g_qkv = deliver(
            kept_count, layer, patch, small, (g_fc2, g_fc1, g_out, g_qkv)
        )
        grad_qkv = jnp.transpose(g_qkv, (0, 2, 1, 3))
        return layer_out, grad_patches, gain, shift, grad_qkv, qv, g_out, g_fc1, fc1, g_fc2
    slot_ids = jnp.arange(PATCHES, dtype=jnp.int32)
    own_mask = (slot_ids[None, :] < kept_count[:, None])[:, :, None]
    layer_out = from_groups(layer) * own_mask.astype(F32)
    grad_patches = from_groups(patch)
    grad_qkv, grad_out, grad_fc1, grad_fc2 = (
        jnp.stack([collect_weight(join(array[n]), split) for n in range(LAYERS)])
        for array, join, split in (
            (g_qkv, join_rows, 0),
            (g_out, join_columns, 1),
            (g_fc1, join_rows, 0),
            (g_fc2, join_columns, 1),
        )
    )
    grad_qkv = grad_qkv.reshape(LAYERS, -1, 3, width)
    small = lax.all_gather(lax.psum(small, "dp"), "tensor")
    summed = jnp.sum(small[:, :12], axis=0)
    grad_gain = summed[:4].reshape(LAYERS, 2, D)
    grad_shifts = summed[4:].reshape(LAYERS, 4, D)
    grad_bias_fc1 = jnp.transpose(small[:, 12:14], (1, 0, 2)).reshape(LAYERS, ways * hidden)
    quarters = small[:, 14, : 2 * LAYERS * width].reshape(ways, LAYERS, 2, width)
    grad_bias_qv = jnp.transpose(quarters, (1, 2, 0, 3)).reshape(LAYERS, 2, ways * width)
    return (
        layer_out,
        grad_patches,
        grad_gain,
        grad_shifts,
        grad_qkv,
        grad_bias_qv,
        grad_out,
        grad_fc1,
        grad_bias_fc1,
        grad_fc2,
    )


def solution(mesh):
    in_specs = (
        P(("dp", "tensor"), None, None),
        P(("dp", "tensor"), None),
        P(("dp", "tensor")),
        P(),
        P(),
        P(None, None, None, "tensor"),
        P(None, None, "tensor"),
        P(None, "tensor", None),
        P(None, None, "tensor"),
        P(None, "tensor"),
        P(None, "tensor", None),
        P(("dp", "tensor"), None, None),
    )
    out_specs = (
        P(("dp", "tensor"), None, None),
        P(("dp", "tensor"), None, None),
        P(),
        P(),
        P(None, "dp", None, "tensor"),
        P(),
        P(None, "tensor", "dp"),
        P(None, "dp", "tensor"),
        P(),
        P(None, "tensor", "dp"),
    )
    return jax.shard_map(local, mesh=mesh, in_specs=in_specs, out_specs=out_specs, check_vma=False)
```

```python
from functools import partial

import jax
import jax.numpy as jnp
from jax import lax
from jax.experimental import pallas as pl
from jax.experimental.pallas import tpu as pltpu
from jax.sharding import PartitionSpec as P

D = 1024
HEAD = 64
FF = 4096
LAYERS = 2
PATCHES = 50
EPS = 1e-06
HIGHEST = lax.Precision.HIGHEST
F32 = jnp.float32
BF16 = jnp.bfloat16

GROUPS = 2
ROWS = 160
LIVE = 150
COLS = 128
SCALE = HEAD ** (-0.5)


def dot(a, b, lhs=1, rhs=0):
    return lax.dot_general(a, b, (((lhs,), (rhs,)), ((), ())), preferred_element_type=F32)


def remote(src, dst, send, recv, peer):
    return pltpu.make_async_remote_copy(
        src_ref=src,
        dst_ref=dst,
        send_sem=send,
        recv_sem=recv,
        device_id={"tensor": peer},
        device_id_type=pl.DeviceIdType.MESH,
    )


def norm_parts(values):
    average = jnp.mean(values, axis=-1, keepdims=True)
    centred = values - average
    variance = jnp.mean(centred * centred, axis=-1, keepdims=True)
    scale = lax.rsqrt(variance + EPS)
    return centred * scale, scale


def head_mask(h, width):
    lane = lax.broadcasted_iota(jnp.int32, (1, width), 1)
    return (lane // HEAD == h).astype(F32).astype(BF16)


class Exchange:
    def __init__(self, gath, part, bufs, spare, late_y, sems):
        self.gath, self.part = gath, part
        self.out_po, self.out_pd, self.out_y, self.in_po, self.in_pd, self.in_y = bufs
        self.spare, self.late_y = spare, late_y
        self.sem = sems
        me = lax.axis_index("tensor")
        self.me = me
        self.mate = me + 1 - 2 * (me % 2)
        self.far = (me + 2) % 4
        self.diag = (self.mate + 2) % 4
        self.stage = 0

    def barrier(self):
        sem = pltpu.get_barrier_semaphore()
        for peer in (self.mate, self.far):
            pl.semaphore_signal(
                sem, inc=1, device_id={"tensor": peer}, device_id_type=pl.DeviceIdType.MESH
            )
        pl.semaphore_wait(sem, 2)

    def own(self, g):
        return GROUPS * self.me + g

    def rows(self, slot):
        return self.gath.at[self.stage % 2, slot]

    def copy(self, kind, g):
        s = self.sem
        own, slot = self.rows(self.own(g)), self.rows(GROUPS * self.far + g)
        own_0, slot_0 = self.gath.at[0, self.own(g)], self.gath.at[0, GROUPS * self.far + g]
        spare = self.spare
        src, dst, peer = (
            (own, own, self.far),
            (own, own, self.mate),
            (slot, slot, self.mate),
            (self.out_po.at[g], self.in_po.at[g], self.mate),
            (self.out_pd.at[g], self.in_pd.at[g], self.mate),
            (self.out_y.at[g], self.in_y.at[g], self.far),
            (own_0, own_0, self.far),
            (own_0, own_0, self.mate),
            (slot_0, slot_0, self.mate),
            (spare.at[g], spare.at[2 + g], self.mate),
            (spare.at[4 + g], spare.at[6 + g], self.mate),
            (self.late_y.at[g], self.in_pd.at[g], self.far),
        )[kind]
        return remote(src, dst, s.at[0, kind, g], s.at[1, kind, g], peer)

    def again(self, kind, g):
        if self.stage:
            self.copy(kind, g).wait_send()

    def send(self, kind, g):
        self.copy(kind, g).start()

    def clear(self, g):
        for kind in range(2):
            self.again(kind, g)

    def share(self, g):
        for kind in range(2):
            self.send(kind, g)

    def slot(self, i):
        even = i % 2 == 0
        owner = jnp.where(
            i < 4,
            jnp.where(even, self.me, self.mate),
            jnp.where(even, self.far, self.diag),
        )
        return GROUPS * owner + (i // 2) % 2

    def place(self, i):
        return jnp.where(i % 2 == 0, i // 2, 4)

    def before(self, i):
        for g in range(GROUPS):

            @pl.when(i == 1 + 2 * g)
            def _():
                self.copy(1, g).wait_recv()

            @pl.when(i == 4 + 2 * g)
            def _():
                self.copy(0, g).wait_recv()
                self.send(2, g)

            @pl.when(i == 5 + 2 * g)
            def _():
                self.copy(2, g).wait_recv()

    def after(self, i):
        for g in range(GROUPS):

            @pl.when(i == 1 + 2 * g)
            def _():
                self.again(3, g)
                self.out_po[g] = self.part[4].astype(BF16)
                self.send(3, g)

            @pl.when(i == 5 + 2 * g)
            def _():
                self.again(4, g)
                self.out_pd[g] = self.part[4].astype(BF16)
                self.send(4, g)
                self.copy(4, g).wait_recv()
                self.again(5, g)
                self.out_y[g] = (self.part[2 + g] + self.in_pd[g].astype(F32)).astype(BF16)
                self.copy(2, g).wait_send()
                self.send(5, g)

    def total(self, g):
        self.copy(3, g).wait_recv()
        self.copy(5, g).wait_recv()
        return self.part[g] + self.in_po[g].astype(F32) + self.in_y[g].astype(F32)

    def before_both(self, i):
        self.before(i)
        for g in range(GROUPS):

            @pl.when(i == 1 + 2 * g)
            def _():
                self.copy(7, g).wait_recv()

            @pl.when(i == 4 + 2 * g)
            def _():
                self.copy(6, g).wait_recv()
                self.send(8, g)

            @pl.when(i == 5 + 2 * g)
            def _():
                self.copy(8, g).wait_recv()

    def set_aside(self, i, value, own_total):
        self.part[4] = value
        for g in range(GROUPS):

            @pl.when(i == 2 * g)
            def _():
                own_total(g, self.part[4])

            @pl.when(i == 1 + 2 * g)
            def _():
                self.spare[g] = self.part[4].astype(BF16)
                self.send(9, g)

            @pl.when(i == 4 + 2 * g)
            def _():
                self.late_y[g] = self.part[4].astype(BF16)

            @pl.when(i == 5 + 2 * g)
            def _():
                self.spare[4 + g] = self.part[4].astype(BF16)
                self.send(10, g)
                self.copy(10, g).wait_recv()
                both = self.late_y[g].astype(F32) + self.spare[6 + g].astype(F32)
                self.late_y[g] = both.astype(BF16)

    def end(self):
        for g in range(GROUPS):
            for kind in (0, 1, 3, 4, 5, 11):
                self.copy(kind, g).wait_send()


def exchange_scratch():
    return [
        pltpu.VMEM((2, 8, ROWS, D), BF16),
        pltpu.VMEM((5, ROWS, D), F32),
    ] + [pltpu.VMEM((GROUPS, ROWS, D), BF16)] * 6 + [pltpu.SemaphoreType.DMA((2, 12, GROUPS))]


def picker(keep, image):
    patch = lax.broadcasted_iota(jnp.int32, (PATCHES, PATCHES), 0)
    return (keep[image : image + 1] == patch).astype(F32).astype(BF16)


def images_of(g):
    per = LIVE // PATCHES
    return [(g * per + m, m * PATCHES) for m in range(per)]


def live_rows(count, image):
    row = lax.broadcasted_iota(jnp.int32, (PATCHES, D), 0)
    return row < count[image]


def attend(x, q_bias, v_bias, wqkv, wout, counts, keep_parts):
    width = wout.shape[0]
    triple = dot(x, wqkv[...])
    q = (triple[:, :width] + q_bias).astype(BF16)
    k = triple[:, width : 2 * width].astype(BF16)
    v = (triple[:, 2 * width :] + v_bias).astype(BF16)
    keep_parts(0, q, k, v)
    lane = lax.broadcasted_iota(jnp.int32, (1, ROWS), 1)
    image = lane // PATCHES
    count = jnp.where(image == 0, counts[6:7], jnp.where(image == 1, counts[7:8], counts[8:9]))
    fits = (lane - image * PATCHES).astype(F32) < count
    row = lax.broadcasted_iota(jnp.int32, (ROWS, ROWS), 0)
    col = lax.broadcasted_iota(jnp.int32, (ROWS, ROWS), 1)
    same = jnp.minimum(row // PATCHES, 2) == col // PATCHES
    veil = jnp.where(same, 0.0, -1e30) + jnp.where(fits, 0.0, -1e30)
    mixed = jnp.zeros((ROWS, width), F32)
    for h in range(width // HEAD):
        mask = head_mask(h, width)
        scores = dot(q * mask, k, 1, 1) * SCALE + veil
        peak = jnp.max(scores, axis=-1, keepdims=True)
        raised = jnp.exp(scores - peak)
        weight = raised * (1.0 / jnp.sum(raised, axis=-1, keepdims=True))
        rounded = weight.astype(BF16)
        keep_parts(1 + h, rounded)
        mixed = mixed + dot(rounded, v * mask)
    return mixed.astype(BF16)


def erf_parts(pre):
    cdf = 0.5 * (1.0 + lax.erf(pre * (0.5 ** 0.5)))
    pdf = jnp.exp(-0.5 * pre * pre) * 0.3989422804014327
    return cdf, pdf


VM = pl.BlockSpec(memory_space=pltpu.VMEM)
HB = pl.BlockSpec(memory_space=pl.ANY)


def sds(shape, dtype):
    return jax.ShapeDtypeStruct(shape, dtype)


def params(n):
    return pltpu.CompilerParams(
        collective_id=n, has_side_effects=True, vmem_limit_bytes=67043328
    )


def column_sums(values):
    return jnp.sum(values, axis=0, keepdims=True)


class Scatter:
    order = (3, 1, 2, 0)

    def __init__(self, made, halves, arrivals, totals, outs, sems):
        self.made, self.halves, self.arrivals = made, halves, arrivals
        self.totals, self.outs = totals, outs
        self.x_sem, self.z_sem, self.out_sem, self.x_free, self.z_free = sems
        me = lax.axis_index("dp")
        self.x, self.z = me % 2, me // 2
        self.across = me + 1 - 2 * self.x
        self.near = self.z + 1 - 2 * (self.z % 2)
        self.far = (self.z + 2) % 4

    def device(self, z):
        return 2 * z + self.x

    def shard(self, k):
        return (self.z, self.near, self.far, (self.near + 2) % 4)[k]

    def number(self, j):
        third = (self.near + 2) % 4
        return jnp.where(
            j < 2, jnp.where(j == 0, third, self.near), jnp.where(j == 2, self.far, self.z)
        )

    def over_x(self, kind, part, j):
        n = self.number(j)
        return to_peer(
            "dp",
            self.made[kind][part].at[1 - self.x, n],
            self.halves[kind][part].at[n],
            self.x_sem.at[kind, part, j, 0],
            self.x_sem.at[kind, part, j, 1],
            self.across,
        )

    def over_z(self, kind, part, k):
        there, slot = {1: (self.near, 0), 3: (self.near, 1), 2: (self.far, 2)}[k]
        return to_peer(
            "dp",
            self.made[kind][part].at[self.x, self.shard(k)],
            self.arrivals[kind][part].at[slot],
            self.z_sem.at[kind, part, slot, 0],
            self.z_sem.at[kind, part, slot, 1],
            self.device(there),
        )

    def ready(self, s, part):
        if s >= 2:
            for j in range(4):
                self.over_x(s % 2, part, j).wait_send()
            for k in (1, 2, 3):
                self.over_z(s % 2, part, k).wait_send()

    def send(self, s, part, j):
        if s >= 2:
            pl.semaphore_wait(self.x_free.at[s % 2, part], 1)
        self.over_x(s % 2, part, j).start()

    def signal(self, sem, device):
        pl.semaphore_signal(
            sem, inc=1, device_id={"dp": device}, device_id_type=pl.DeviceIdType.MESH
        )

    def sum_rows(self, out, terms):
        def one(i, _):
            at = pl.ds(pl.multiple_of(i * COLS, COLS), COLS)
            value = terms[0][at, :].astype(F32)
            for term in terms[1:]:
                value = value + term[at, :].astype(F32)
            out[at, :] = value.astype(out.dtype)
            return 0

        lax.fori_loop(0, out.shape[0] // COLS, one, 0)

    def take(self, s, part, k):
        kind = s % 2
        mine = self.made[kind][part].at[self.x, self.shard(k)]
        terms = [mine, self.halves[kind][part].at[self.shard(k)]]
        self.over_x(kind, part, self.order.index(k)).wait_recv()
        if k == 2:
            self.over_z(kind, part, 3).wait_recv()
            terms.append(self.arrivals[kind][part].at[1])
        if k == 0:
            if s >= 2:
                self.store(s - 2, part, wait=True)
            mine = self.totals[kind][part]
        self.sum_rows(mine, terms)
        if s < 2:
            self.signal(self.x_free.at[kind, part], self.across)
            if k == 2:
                self.signal(self.z_free.at[kind, part, 1], self.device(self.near))
        if k:
            if s >= 2:
                slot = {1: 0, 3: 1, 2: 2}[k]
                pl.semaphore_wait(self.z_free.at[kind, part, slot], 1)
            self.over_z(kind, part, k).start()

    def store(self, s, part, wait=False):
        kind, n = s % 2, LAYERS - 1 - s // 2
        total, out = self.totals[kind][part], self.outs[kind][part]
        if kind == 1 and part == 1:
            width = out.shape[-1]
            pairs = [(total.at[:, pl.ds(c * width, width)], out.at[n, c]) for c in range(3)]
        else:
            pairs = [(total, out.at[n])]
        for c, pair in enumerate(pairs):
            copy = pltpu.make_async_copy(*pair, self.out_sem.at[kind, part, c])
            if wait:
                copy.wait()
            else:
                copy.start()

    def finish(self, s, part):
        kind = s % 2
        total, arrivals = self.totals[kind][part], self.arrivals[kind][part]
        self.over_z(kind, part, 1).wait_recv()
        self.over_z(kind, part, 2).wait_recv()
        self.sum_rows(total, [total, arrivals.at[0], arrivals.at[2]])
        self.store(s, part)
        if s < 2:
            self.signal(self.z_free.at[kind, part, 0], self.device(self.near))
            self.signal(self.z_free.at[kind, part, 2], self.device(self.far))

    def end(self):
        for s in (2, 3):
            for part in range(2):
                self.ready(s, part)
                self.store(s, part, wait=True)


def to_peer(axis, src, dst, send, recv, peer):
    return pltpu.make_async_remote_copy(
        src_ref=src,
        dst_ref=dst,
        send_sem=send,
        recv_sem=recv,
        device_id={axis: peer},
        device_id_type=pl.DeviceIdType.MESH,
    )


class SmallSum:
    def __init__(self, lines, arrived, over_z, out, sem, sc, mine):
        self.lines, self.arrived, self.over_z, self.out = lines, arrived, over_z, out
        self.sem, self.sc, self.mine = sem, sc, mine

    def across(self):
        s = self.sem
        return to_peer("dp", self.lines, self.arrived, s.at[0, 0], s.at[1, 0], self.sc.across)

    def along(self, k):
        part, s = self.over_z.at[self.sc.z], self.sem
        return to_peer("dp", part, part, s.at[0, k], s.at[1, k], self.sc.device((self.sc.z + k) % 4))

    def around(self, k):
        part, s = self.out.at[self.mine], self.sem
        peer = (self.mine + k) % 4
        return to_peer("tensor", part, part, s.at[0, 3 + k], s.at[1, 3 + k], peer)

    def second(self):
        self.across().wait()
        self.over_z[self.sc.z] = self.lines[...] + self.arrived[...]
        for k in range(1, 4):
            self.along(k).start()

    def third(self):
        for k in range(1, 4):
            self.along(k).wait()
        z = self.over_z
        self.out[self.mine] = z[0] + z[1] + z[2] + z[3]
        for k in range(1, 4):
            self.around(k).start()

    def last(self):
        for k in range(1, 4):
            self.around(k).wait()


def step_kernel(
    fused,
    count, patches, cot, keep, gains, shifts, bias_qv, bias_fc1, wqkv_h, wout_h, w1_h, w2_h,
    layer_h, patch_h, small_out, o_fc2, o_fc1, o_out, o_qkv,
    flow_h, gath_h, qkv_h, prob_h, att_h, gmlp_h, act_h, slope_h,
    gath, part, out_po, out_pd, out_y, in_po, in_pd, in_y, ex_sem,
    gradient, source, final, late_y, wqkv, wout, w1, w2,
    qkv, prob, att, norm_a, act, slope, norm_m,
    pre, triple, lines, cols_m, rows_m, cols_a, rows_a, load_sem, keep_sem, flow_sem, *rest,
):
    bufs = (out_po, out_pd, out_y, in_po, in_pd, in_y)
    ex = Exchange(gath, part, bufs, slope, late_y, ex_sem)
    width, hidden = wout.shape[0], w1.shape[1]
    stages = 2 * LAYERS
    flat = 8 * ROWS
    made = ((cols_m, rows_m), (cols_a, rows_a))
    outs = ((o_fc2, o_fc1), (o_out, o_qkv))
    if fused:
        halves, arrivals, totals = (
            ((rest[4 * n], rest[4 * n + 1]), (rest[4 * n + 2], rest[4 * n + 3])) for n in range(3)
        )
        small_in, small_z, small_sem = rest[12:15]
        sc = Scatter(made, halves, arrivals, totals, outs, rest[15:20])
    else:
        sc = None
        save_sem = rest[0]

    def layer(s):
        return LAYERS - 1 - s // 2

    def loads(s):
        n = layer(s)
        if s < 2:
            return []
        if s % 2 == 0:
            pairs = (
                (w2_h.at[n], w2),
                (slope_h, slope),
                (w1_h.at[n], w1),
                (act_h, act),
                (gmlp_h, norm_m),
                (flow_h.at[1], source.at[0]),
            )
        else:
            pairs = tuple(
                (wqkv_h.at[n, c], wqkv.at[:, pl.ds(c * width, width)]) for c in range(3)
            ) + (
                (wout_h.at[n], wout),
                (qkv_h, qkv),
                (prob_h, prob),
                (att_h, att),
                (gath_h, norm_a),
                (flow_h.at[0], source.at[1]),
            )
        return [
            pltpu.make_async_copy(*pair, load_sem.at[s % 2, m]) for m, pair in enumerate(pairs)
        ]

    def forward_loads(s):
        n = s // 2
        if s % 2 == 0:
            pairs = [
                (wqkv_h.at[n, c], wqkv.at[:, pl.ds(c * width, width)]) for c in range(3)
            ] + [(wout_h.at[n], wout)]
        else:
            pairs = [(w1_h.at[n], w1), (w2_h.at[n], w2)]
        return [
            pltpu.make_async_copy(*pair, load_sem.at[s % 2, m]) for m, pair in enumerate(pairs)
        ]

    for s in range(2):
        for copy in forward_loads(s):
            copy.start()
    barrier = pltpu.get_barrier_semaphore()
    peers = [{"tensor": ex.mate}, {"tensor": ex.far}]
    if fused:
        peers += [{"tensor": ex.diag}, {"dp": sc.across}]
        peers += [{"dp": sc.device((sc.z + k) % 4)} for k in range(1, 4)]
    for peer in peers:
        pl.semaphore_signal(barrier, inc=1, device_id=peer, device_id_type=pl.DeviceIdType.MESH)
    pl.semaphore_wait(barrier, len(peers))

    def note(at, g, row):
        lines[at : at + 1] = row if g == 0 else lines[at : at + 1] + row

    def hold(s):
        return source.at[(s + 1) % 2]

    def save_flow(s, g):
        return pltpu.make_async_copy(hold(s).at[g], flow_h.at[s, g], flow_sem.at[s, g])

    def begin(s, g):
        n = s // 2
        held = hold(s)
        if s >= 2:
            save_flow(s - 2, g).wait()
        if s == 0:
            for image, at in images_of(g):
                held[g, at : at + PATCHES] = dot(picker(keep, image), patches[image], 0, 0)
            held[g, LIVE:] = jnp.zeros((ROWS - LIVE, D), F32)
            value = held[g]
        else:
            shift = shifts[(s - 1) // 2, 2 + (s - 1) % 2].reshape(1, D)
            value = hold(s - 1)[g] + ex.total(g) + shift
            held[g] = value
        if s < 2:
            save_flow(s, g).start()
        unit, _ = norm_parts(value)
        gain, shift = gains[n, s % 2].reshape(1, D), shifts[n, s % 2].reshape(1, D)
        own = ex.own(g)
        ex.clear(g)
        gath[s % 2, own] = (unit * gain + shift).astype(BF16)
        tail = gath[s % 2, own, ROWS - 16 : ROWS, 0:256].astype(F32)
        row = lax.broadcasted_iota(jnp.int32, (16, 256), 0) - (LIVE - ROWS + 16)
        for m, (image, _) in enumerate(images_of(g)):
            tail = jnp.where(row == m, count[image].astype(F32), tail)
        gath[s % 2, own, ROWS - 16 : ROWS, 0:256] = tail.astype(BF16)
        ex.share(g)
        if s < stages - 1:
            return
        gradient[g, LIVE:] = jnp.zeros((ROWS - LIVE, D), F32)
        for image, at in images_of(g):
            piece = jnp.where(live_rows(count, image), cot[image].astype(F32), 0.0)
            gradient[g, at : at + PATCHES] = piece
        rounded = gradient[g].astype(BF16)
        note(4 + 4 * n + 3, g, column_sums(rounded.astype(F32)))
        gath[0, own] = rounded
        ex.send(6, g)
        ex.send(7, g)

    def saves(s, slot):
        if s == 0:
            pairs = (
                (gath.at[0, slot], gath_h),
                (qkv.at[slot], qkv_h),
                (prob.at[slot], prob_h),
                (att.at[slot], att_h),
            )
        elif s == 1:
            pairs = ((gath.at[1, slot], gmlp_h), (act.at[slot], act_h), (slope.at[slot], slope_h))
        else:
            pairs = ()
        return [
            pltpu.make_async_copy(a, b.at[slot], keep_sem.at[m, slot])
            for m, (a, b) in enumerate(pairs)
        ]

    def drain(s):
        def one(slot, _):
            for copy in saves(s, slot):
                copy.wait()
            return 0

        lax.fori_loop(0, 8, one, 0)

    def own_total(g, value):
        final[g] = source[0, g] + value + shifts[LAYERS - 1, 3].reshape(1, D)

    lines[15:16] = jnp.zeros((1, D), F32)
    for s in range(stages):
        n = s // 2
        ex.stage = s
        begin(s, 0)
        if s == 0:
            begin(s, 1)
        elif s <= 2:
            drain(s - 1)
        for copy in forward_loads(s):
            copy.wait()
        if 1 <= s < stages - 1:
            for copy in forward_loads(s + 1):
                copy.start()

        def step(i, _, s=s, n=n):
            if s:

                @pl.when(i == 2)
                def _():
                    begin(s, 1)

            both = s == stages - 1
            (ex.before_both if both else ex.before)(i)
            slot = ex.slot(i)
            x = gath[s % 2, slot]
            if s >= 2:
                (norm_a, norm_m)[s % 2][slot] = x
            if s % 2 == 0:

                def keep_parts(kind, *values):
                    if kind == 0:
                        for c, value in enumerate(values):
                            qkv[slot, :, c * width : (c + 1) * width] = value
                    else:
                        prob[slot, (kind - 1) * ROWS : kind * ROWS] = values[0]

                tail = gath[0, slot, ROWS - 16 : ROWS, 0:256][:, 0:ROWS].astype(F32)
                mixed = attend(
                    x, bias_qv[n, 0:1], bias_qv[n, 1:2], wqkv, wout, tail, keep_parts
                )
                att[slot] = mixed
                part[ex.place(i)] = dot(mixed, wout[...])
            else:
                for block in range(hidden // 256):
                    at = slice(block * 256, block * 256 + 256)
                    pre_act = dot(x, w1[:, at]) + bias_fc1[n : n + 1, at]
                    cdf, pdf = erf_parts(pre_act)
                    act[slot, :, at] = (pre_act * cdf).astype(BF16)
                    steep = cdf + pre_act * pdf
                    if both:
                        d_act = dot(gath[0, slot], w2[at, :], 1, 1)
                        pre[slot, :, at] = (d_act * steep).astype(BF16)
                    else:
                        slope[slot, :, at] = steep.astype(BF16)
                value = dot(act[slot], w2[...])
                if both:
                    ex.set_aside(i, value, own_total)
                    value = dot(pre[slot], w1[...], 1, 1)
                part[ex.place(i)] = value
            for copy in saves(s, slot):
                copy.start()
            ex.after(i)
            return 0

        lax.fori_loop(0, 8, step, 0)

    for g in range(GROUPS):
        for kind in (6, 7, 8):
            ex.copy(kind, g).wait_send()
        ex.copy(9, g).wait()
        ex.copy(10, g).wait_send()
        final[g] = final[g] + ex.spare[2 + g].astype(F32)

    def produce(s, g):
        n, side = layer(s - 1), s % 2
        gain = gains[n, side].reshape(1, D)
        moved = ex.total(g)
        unit, scale = norm_parts(source[1 - side, g])
        note(2 * n + side, g, column_sums(moved * unit))
        note(4 + 4 * n + side, g, column_sums(moved))
        scaled = moved * gain
        lean = jnp.mean(scaled, axis=-1, keepdims=True)
        tilt = jnp.mean(scaled * unit, axis=-1, keepdims=True)
        grad = gradient[g] + scale * (scaled - lean - unit * tilt)
        rounded = grad.astype(BF16)
        if s < stages:
            gradient[g] = grad
        else:
            gradient[g] = grad
            for image, at in images_of(g):
                exact = gradient[g, at : at + PATCHES]
                high = exact.astype(BF16)
                low = (exact - high.astype(F32)).astype(BF16)
                pick = picker(keep, image)
                source[0, g, at : at + PATCHES] = dot(pick, high) + dot(pick, low)
            pltpu.make_async_copy(source.at[0, g], patch_h.at[g], flow_sem.at[0, g]).start()
            return
        if s % 2 == 0:
            note(4 + 4 * layer(s) + 3, g, column_sums(rounded.astype(F32)))
        else:
            note(4 + 4 * layer(s) + 2, g, column_sums(rounded.astype(F32)))
        ex.clear(g)
        gath[s % 2, ex.own(g)] = rounded
        ex.share(g)

    def spill(s, part, k):
        return [
            pltpu.make_async_copy(
                made[s % 2][part].at[half, k],
                outs[s % 2][part].at[layer(s), half, k],
                save_sem.at[s % 2, part, k, half],
            )
            for half in range(2)
        ]

    def column_block(s, j):
        n = sc.number(j) if fused else j
        at = pl.ds(pl.multiple_of(n * 256, 256), 256)
        some = gath[s % 2, :, :, at].reshape(flat, 256)
        left = (act, att)[s % 2]
        wide = dot(left[...].reshape(flat, left.shape[-1]), some, 0, 0).astype(BF16)
        out = made[s % 2][0]
        out[0, n] = wide[:, :COLS]
        out[1, n] = wide[:, COLS:]
        if fused:
            if s < stages - 1:
                sc.send(s, 0, j)
        else:
            for copy in spill(s, 0, j):
                copy.start()

    def row_block(s, j):
        n = sc.number(j) if fused else j
        at = pl.ds(pl.multiple_of(n * 256, 256), 256)
        left, right = ((norm_m, pre), (norm_a, triple))[s % 2]
        some = left[:, :, at].reshape(flat, 256)
        tall = dot(some, right[...].reshape(flat, right.shape[-1]), 0, 0).astype(BF16)
        out = made[s % 2][1]
        out[0, n] = tall[:COLS]
        out[1, n] = tall[COLS:]
        if fused:
            if s < stages - 1:
                sc.send(s, 1, j)
        else:
            for copy in spill(s, 1, j):
                copy.start()

    def settle(s, part):
        if fused:
            sc.ready(s, part)
        elif s >= 2:
            for k in range(4):
                for copy in spill(s - 2, part, k):
                    copy.wait()

    def columns(s):
        settle(s, 0)

        def one(j, _):
            column_block(s, j)
            return 0

        lax.fori_loop(0, 4, one, 0)

    def some_rows(s, start, count):
        def one(j, _):
            row_block(s, start + j)
            return 0

        lax.fori_loop(0, count, one, 0)

    def bias_sums(s):
        n = layer(s)
        ones = jnp.ones((8, flat), BF16)
        if s % 2 == 0:
            lines[12 + n : 13 + n] = dot(ones, pre[...].reshape(flat, hidden))[0:1]
        else:
            sums = dot(ones, triple[...].reshape(flat, 3 * width))[0:1]
            at = 2 * n * width
            lines[14:15, at : at + width] = sums[:, :width]
            lines[14:15, at + width : at + 2 * width] = sums[:, 2 * width :]

    def take(*work):
        def run():
            if fused:
                for s, part, k in work:
                    if k == 4:
                        sc.finish(s, part)
                    else:
                        sc.take(s, part, k)

        return run

    plan = {
        (1, 4): take((0, 0, 3)),
        (1, 6): take((0, 0, 1)),
        (1, 8): take((0, 0, 2)),
        (2, 2): take((0, 0, 0), (0, 1, 3)),
        (2, 4): take((0, 1, 1)),
        (2, 6): take((0, 1, 2)),
        (2, 8): take((0, 1, 0), (0, 0, 4), (1, 0, 3), (1, 0, 1)),
        (3, 2): take((1, 0, 2), (1, 0, 0), (1, 1, 3), (1, 1, 1)),
        (3, 4): take((0, 1, 4), (1, 1, 2)),
        (3, 6): take((1, 0, 4), (1, 1, 0), (2, 0, 3)),
        (3, 8): take((2, 0, 1), (1, 1, 4)),
    }

    for s in range(1, stages):
        ex.stage = stages + s
        columns(s - 1)
        produce(s, 0)
        early = (3, 6)[s % 2]
        for copy in loads(s)[:early]:
            copy.wait()

        def step(i, _, s=s):
            if s:

                @pl.when(i == 2)
                def _():
                    settle(s - 1, 1)

                @pl.when((i == 2) | (i == 4))
                def _():
                    some_rows(s - 1, i - 2, 2)

            @pl.when(i == 2)
            def _():
                produce(s, 1)

            if s:

                @pl.when(i == 6)
                def _():
                    bias_sums(s - 1)
                    if s + 1 < stages:
                        for copy in loads(s + 1) if s >= 1 else ():
                            copy.start()

            for (stage, at), task in plan.items():
                if stage == s and at < 8:
                    pl.when(i == at)(task)
            ex.before(i)
            slot = ex.slot(i)
            grad = gath[s % 2, slot]
            if s % 2 == 0:
                for block in range(hidden // 256):
                    at = slice(block * 256, block * 256 + 256)
                    d_act = dot(grad, w2[at, :], 1, 1)
                    pre[slot, :, at] = (d_act * slope[slot, :, at].astype(F32)).astype(BF16)
                part[ex.place(i)] = dot(pre[slot], w1[...], 1, 1)
            else:
                d_att = dot(grad, wout[...], 1, 1).astype(BF16)
                q = qkv[slot, :, 0:width]
                k = qkv[slot, :, width : 2 * width]
                v = qkv[slot, :, 2 * width :]
                d_q = jnp.zeros((ROWS, width), F32)
                d_k = jnp.zeros((ROWS, width), F32)
                d_v = jnp.zeros((ROWS, width), F32)
                for h in range(width // HEAD):
                    mask = head_mask(h, width)
                    d_one = d_att * mask
                    rounded = prob[slot, h * ROWS : (h + 1) * ROWS]
                    weight = rounded.astype(F32)
                    d_prob = dot(d_one, v, 1, 1)
                    centre = jnp.sum(weight * d_prob, axis=-1, keepdims=True)
                    d_scores = (weight * (d_prob - centre)).astype(BF16)
                    d_q = d_q + dot(d_scores, k * mask)
                    d_k = d_k + dot(d_scores, q * mask, 0, 0)
                    d_v = d_v + dot(rounded, d_one, 0, 0)
                triple[slot, :, 0:width] = (d_q * SCALE).astype(BF16)
                triple[slot, :, width : 2 * width] = (d_k * SCALE).astype(BF16)
                triple[slot, :, 2 * width :] = d_v.astype(BF16)
                part[ex.place(i)] = dot(triple[slot], wqkv[...], 1, 1)
            ex.after(i)
            return 0

        lax.fori_loop(0, 8, step, 0)
        for copy in loads(s)[early:]:
            copy.wait()
        if (s, 8) in plan:
            plan[s, 8]()
    last = stages - 1
    columns(last)
    settle(last, 1)
    some_rows(last, 0, 4)
    bias_sums(last)
    take((2, 0, 2), (2, 0, 0))()
    for g in range(GROUPS):
        produce(stages, g)
    for g in range(GROUPS):
        ex.send(11, g)
    if fused:
        tiny = SmallSum(lines, small_in, small_z, small_out, small_sem, sc, ex.me)
        tiny.across().start()
        for side in (1, 0):
            for j in range(4):
                sc.send(last, side, j)
        take((2, 1, 3), (2, 1, 1), (2, 0, 4), (2, 1, 2), (2, 1, 0))()
        tiny.second()
        take((2, 1, 4), (3, 1, 3), (3, 1, 1))()
        tiny.third()
        take((3, 1, 2), (3, 1, 0), (3, 0, 3), (3, 0, 1), (3, 0, 2), (3, 1, 4), (3, 0, 0), (3, 0, 4))()
        sc.end()
        tiny.last()
    else:
        small_out[...] = lines[...]
        for s in (2, 3):
            for side in range(2):
                for k in range(4):
                    for copy in spill(s, side, k):
                        copy.wait()
    for g in range(GROUPS):
        ex.copy(11, g).wait_recv()
        final[g] = final[g] + in_pd[g].astype(F32)
        pltpu.make_async_copy(final.at[g], layer_h.at[g], flow_sem.at[1, g]).start()
    ex.end()
    for g in range(GROUPS):
        pltpu.make_async_copy(source.at[0, g], patch_h.at[g], flow_sem.at[0, g]).wait()
        pltpu.make_async_copy(final.at[g], layer_h.at[g], flow_sem.at[1, g]).wait()


def run_step(fused, count, patches, cot, keep, gains, shifts, bias_qv, bias_fc1, wqkv, wout, w1, w2):
    width, hidden = wout.shape[1], w1.shape[2]
    heads = width // HEAD
    wide, own = (8, ROWS, D), (GROUPS, ROWS, D)
    dma = pltpu.SemaphoreType.DMA
    tall = D // 256
    mine = ((hidden, COLS), (COLS, hidden), (width, COLS), (COLS, 3 * width))
    blocks = [(2, tall) + m for m in mine]
    if fused:
        outs = [
            sds((LAYERS, hidden, COLS), F32),
            sds((LAYERS, COLS, hidden), F32),
            sds((LAYERS, width, COLS), F32),
            sds((LAYERS, 3, COLS, width), F32),
        ]
        small = sds((4, 16, D), F32)
        regular = pltpu.SemaphoreType.REGULAR
        more = (
            [pltpu.VMEM((4,) + m, BF16) for m in mine]
            + [pltpu.VMEM((3,) + m, BF16) for m in mine]
            + [pltpu.VMEM(m, F32) for m in mine]
            + [pltpu.VMEM((16, D), F32), pltpu.VMEM((4, 16, D), F32), dma((2, 7))]
            + [dma((2, 2, 4, 2)), dma((2, 2, 3, 2)), dma((2, 2, 3))]
            + [regular((2, 2)), regular((2, 2, 3))]
        )
    else:
        outs = [sds((LAYERS,) + b, BF16) for b in blocks]
        small = sds((16, D), F32)
        more = [dma((2, 2, 4, 2))]
    inner = ((8, ROWS, 3 * width), (8, heads * ROWS, ROWS), (8, ROWS, width))
    mlp = ((8, ROWS, hidden), (8, ROWS, hidden))
    saved = (wide,) + inner + (wide,) + mlp
    return pl.pallas_call(
        partial(step_kernel, fused),
        out_shape=[sds(own, F32), sds(own, F32), small]
        + outs
        + [sds((2,) + own, F32)]
        + [sds(k, BF16) for k in saved],
        in_specs=[pl.BlockSpec(memory_space=pltpu.SMEM)] + [VM] * 7 + [HB] * 4,
        out_specs=[HB] * 2 + [VM] + [HB] * 12,
        scratch_shapes=exchange_scratch()
        + [
            pltpu.VMEM(own, F32),
            pltpu.VMEM((2,) + own, F32),
            pltpu.VMEM(own, F32),
            pltpu.VMEM(own, BF16),
            pltpu.VMEM((D, 3 * width), BF16),
            pltpu.VMEM((width, D), BF16),
            pltpu.VMEM((D, hidden), BF16),
            pltpu.VMEM((hidden, D), BF16),
        ]
        + [pltpu.VMEM(k, BF16) for k in inner + (wide,) + mlp + (wide,)]
        + [pltpu.VMEM((8, ROWS, hidden), BF16), pltpu.VMEM((8, ROWS, 3 * width), BF16)]
        + [pltpu.VMEM((16, D), F32)]
        + [pltpu.VMEM(b, BF16) for b in blocks]
        + [dma((2, 9)), dma((4, 8)), dma((2, GROUPS))]
        + more,
        compiler_params=params(1),
    )(count, patches, cot, keep, gains, shifts, bias_qv, bias_fc1, wqkv, wout, w1, w2)[:7]


def deliver_kernel(
    count, layer, patch, small, a_h, b_h, c_h, d_h,
    layer_out, patch_out, gain, shift, qv, fc1, a_out, b_out, c_out, d_out,
    a, b, c, d, sems,
):
    held = ((a_h, a, a_out), (b_h, b, b_out), (c_h, c, c_out), (d_h, d, d_out))

    def inward(n):
        return pltpu.make_async_copy(held[n][0], held[n][1], sems.at[0, n])

    def outward(n):
        return pltpu.make_async_copy(held[n][1], held[n][2], sems.at[1, n])

    for n in range(4):
        inward(n).start()
    for g in range(GROUPS):
        for image, at in images_of(g):
            rows = layer[g, at : at + PATCHES]
            layer_out[image] = jnp.where(live_rows(count, image), rows, 0.0)
            patch_out[image] = patch[g, at : at + PATCHES]
    for n in range(4):
        inward(n).wait()
        outward(n).start()
    summed = small[0, 0:12] + small[1, 0:12] + small[2, 0:12] + small[3, 0:12]
    for n in range(LAYERS):
        gain[n] = summed[2 * n : 2 * n + 2]
        shift[n] = summed[4 + 4 * n : 8 + 4 * n]
        for t in range(4):
            hidden = fc1.shape[1] // 4
            fc1[n : n + 1, t * hidden : (t + 1) * hidden] = small[t, 12 + n : 13 + n]
            width = D // 4
            for side in range(2):
                at = (2 * n + side) * width
                piece = small[t, 14:15, at : at + width]
                qv[n, side : side + 1, t * width : (t + 1) * width] = piece
    for n in range(4):
        outward(n).wait()


def deliver(count, layer, patch, small, grads):
    images = (GROUPS * LIVE // PATCHES, PATCHES, D)
    shapes = [g.shape for g in grads]
    return pl.pallas_call(
        deliver_kernel,
        out_shape=[
            sds(images, F32),
            sds(images, F32),
            sds((LAYERS, 2, D), F32),
            sds((LAYERS, 4, D), F32),
            sds((LAYERS, 2, D), F32),
            sds((LAYERS, FF), F32),
        ]
        + [sds(s, F32) for s in shapes],
        in_specs=[pl.BlockSpec(memory_space=pltpu.SMEM)] + [VM] * 3 + [HB] * 4,
        out_specs=[VM] * 6 + [HB] * 4,
        scratch_shapes=[pltpu.VMEM(s, F32) for s in shapes] + [pltpu.SemaphoreType.DMA((2, 4))],
    )(count, layer, patch, small, *grads)


def from_groups(array):
    return array[:, :LIVE].reshape(GROUPS * (LIVE // PATCHES), PATCHES, D)


def collect_weight(partial_grad, split_dim):
    return lax.psum_scatter(
        partial_grad, "dp", scatter_dimension=split_dim, tiled=True
    ).astype(F32)


def join_rows(blocks):
    return jnp.transpose(blocks, (1, 0, 2, 3)).reshape(D, -1)


def join_columns(blocks):
    return jnp.transpose(blocks, (2, 1, 0, 3)).reshape(blocks.shape[2], -1)


def local(
    patches,
    keep_index,
    kept_count,
    norm_gain,
    shifts,
    w_qkv,
    bias_qv,
    w_out,
    w_fc1,
    bias_fc1,
    w_fc2,
    cotangent,
):
    width = w_qkv.shape[-1]
    hidden = w_fc1.shape[-1]
    dp_size, ways = lax.axis_size("dp"), lax.axis_size("tensor")
    assert ways == 4
    wqkv = jnp.transpose(w_qkv, (0, 2, 1, 3))
    fused = dp_size == 8 and hidden == D and 4 * width == D
    layer, patch, small, g_fc2, g_fc1, g_out, g_qkv = run_step(
        fused, kept_count, patches, cotangent, keep_index, norm_gain, shifts, bias_qv, bias_fc1,
        wqkv, w_out, w_fc1, w_fc2,
    )
    if fused:
        layer_out, grad_patches, gain, shift, qv, fc1, g_fc2, g_fc1, g_out, g_qkv = deliver(
            kept_count, layer, patch, small, (g_fc2, g_fc1, g_out, g_qkv)
        )
        grad_qkv = jnp.transpose(g_qkv, (0, 2, 1, 3))
        return layer_out, grad_patches, gain, shift, grad_qkv, qv, g_out, g_fc1, fc1, g_fc2
    slot_ids = jnp.arange(PATCHES, dtype=jnp.int32)
    own_mask = (slot_ids[None, :] < kept_count[:, None])[:, :, None]
    layer_out = from_groups(layer) * own_mask.astype(F32)
    grad_patches = from_groups(patch)
    grad_qkv, grad_out, grad_fc1, grad_fc2 = (
        jnp.stack([collect_weight(join(array[n]), split) for n in range(LAYERS)])
        for array, join, split in (
            (g_qkv, join_rows, 0),
            (g_out, join_columns, 1),
            (g_fc1, join_rows, 0),
            (g_fc2, join_columns, 1),
        )
    )
    grad_qkv = grad_qkv.reshape(LAYERS, -1, 3, width)
    small = lax.all_gather(lax.psum(small, "dp"), "tensor")
    summed = jnp.sum(small[:, :12], axis=0)
    grad_gain = summed[:4].reshape(LAYERS, 2, D)
    grad_shifts = summed[4:].reshape(LAYERS, 4, D)
    grad_bias_fc1 = jnp.transpose(small[:, 12:14], (1, 0, 2)).reshape(LAYERS, ways * hidden)
    quarters = small[:, 14, : 2 * LAYERS * width].reshape(ways, LAYERS, 2, width)
    grad_bias_qv = jnp.transpose(quarters, (1, 2, 0, 3)).reshape(LAYERS, 2, ways * width)
    return (
        layer_out,
        grad_patches,
        grad_gain,
        grad_shifts,
        grad_qkv,
        grad_bias_qv,
        grad_out,
        grad_fc1,
        grad_bias_fc1,
        grad_fc2,
    )


def solution(mesh):
    in_specs = (
        P(("dp", "tensor"), None, None),
        P(("dp", "tensor"), None),
        P(("dp", "tensor")),
        P(),
        P(),
        P(None, None, None, "tensor"),
        P(None, None, "tensor"),
        P(None, "tensor", None),
        P(None, None, "tensor"),
        P(None, "tensor"),
        P(None, "tensor", None),
        P(("dp", "tensor"), None, None),
    )
    out_specs = (
        P(("dp", "tensor"), None, None),
        P(("dp", "tensor"), None, None),
        P(),
        P(),
        P(None, "dp", None, "tensor"),
        P(),
        P(None, "tensor", "dp"),
        P(None, "dp", "tensor"),
        P(),
        P(None, "tensor", "dp"),
    )
    return jax.shard_map(local, mesh=mesh, in_specs=in_specs, out_specs=out_specs, check_vma=False)
```

```python
from functools import partial

import jax
import jax.numpy as jnp
from jax import lax
from jax.experimental import pallas as pl
from jax.experimental.pallas import tpu as pltpu
from jax.sharding import PartitionSpec as P

D = 1024
HEAD = 64
FF = 4096
LAYERS = 2
PATCHES = 50
EPS = 1e-06
HIGHEST = lax.Precision.HIGHEST
F32 = jnp.float32
BF16 = jnp.bfloat16

GROUPS = 2
ROWS = 160
LIVE = 150
MOST, EDGE = 144, 152
COLS = 128
SCALE = HEAD ** (-0.5)


def dot(a, b, lhs=1, rhs=0):
    return lax.dot_general(a, b, (((lhs,), (rhs,)), ((), ())), preferred_element_type=F32)


def remote(src, dst, send, recv, peer):
    return pltpu.make_async_remote_copy(
        src_ref=src,
        dst_ref=dst,
        send_sem=send,
        recv_sem=recv,
        device_id={"tensor": peer},
        device_id_type=pl.DeviceIdType.MESH,
    )


def norm_parts(values):
    average = jnp.mean(values, axis=-1, keepdims=True)
    centred = values - average
    variance = jnp.mean(centred * centred, axis=-1, keepdims=True)
    scale = lax.rsqrt(variance + EPS)
    return centred * scale, scale


def head_mask(h, width):
    lane = lax.broadcasted_iota(jnp.int32, (1, width), 1)
    return (lane // HEAD == h).astype(F32).astype(BF16)


class Exchange:
    def __init__(self, gath, part, bufs, spare, late_y, edges, sems):
        self.edge_out, self.edge_in = edges
        self.gath, self.part = gath, part
        self.out_po, self.out_pd, self.out_y, self.in_po, self.in_pd, self.in_y = bufs
        self.spare, self.late_y = spare, late_y
        self.sem = sems
        me = lax.axis_index("tensor")
        self.me = me
        self.mate = me + 1 - 2 * (me % 2)
        self.far = (me + 2) % 4
        self.diag = (self.mate + 2) % 4
        self.stage = 0

    def barrier(self):
        sem = pltpu.get_barrier_semaphore()
        for peer in (self.mate, self.far):
            pl.semaphore_signal(
                sem, inc=1, device_id={"tensor": peer}, device_id_type=pl.DeviceIdType.MESH
            )
        pl.semaphore_wait(sem, 2)

    def own(self, g):
        return GROUPS * self.me + g

    def rows(self, slot):
        return self.gath.at[self.stage % 2, slot]

    def copy(self, kind, g):
        s = self.sem
        own, slot = self.rows(self.own(g)), self.rows(GROUPS * self.far + g)
        most = pl.ds(0, MOST)
        far_own = self.gath.at[self.stage % 2, self.own(g), most]
        far_own_0 = self.gath.at[0, self.own(g), most]
        own_0, slot_0 = self.gath.at[0, self.own(g)], self.gath.at[0, GROUPS * self.far + g]
        spare = self.spare
        src, dst, peer = (
            (far_own, far_own, self.far),
            (own, own, self.mate),
            (slot, slot, self.mate),
            (self.out_po.at[g], self.in_po.at[g], self.mate),
            (self.out_pd.at[g], self.in_pd.at[g], self.mate),
            (self.out_y.at[g, most], self.in_y.at[g, most], self.far),
            (far_own_0, far_own_0, self.far),
            (own_0, own_0, self.mate),
            (slot_0, slot_0, self.mate),
            (spare.at[g], spare.at[2 + g], self.mate),
            (spare.at[4 + g], spare.at[6 + g], self.mate),
            (self.late_y.at[g], self.in_pd.at[g], self.far),
            (self.edge_out.at[0, g], self.edge_in.at[0, g], self.far),
            (self.edge_out.at[1, g], self.edge_in.at[1, g], self.far),
            (self.edge_out.at[2, g], self.edge_in.at[2, g], self.far),
        )[kind]
        return remote(src, dst, s.at[0, kind, g], s.at[1, kind, g], peer)

    def again(self, kind, g):
        if self.stage:
            self.copy(kind, g).wait_send()

    def send(self, kind, g):
        self.copy(kind, g).start()

    def clear(self, g):
        for kind in (0, 1, 12):
            self.again(kind, g)

    def set_edge(self, n, g, rows):
        self.edge_out[n, g] = rows.astype(F32)[0 : EDGE - MOST].astype(BF16)

    def get_edge(self, n, g):
        rows = self.edge_in[n, g].astype(F32)
        return jnp.concatenate([rows, jnp.zeros((ROWS - EDGE, D), F32)]).astype(BF16)

    def share(self, g):
        self.set_edge(0, g, self.gath[self.stage % 2, self.own(g), MOST:ROWS])
        self.send(12, g)
        for kind in range(2):
            self.send(kind, g)

    def slot(self, i):
        even = i % 2 == 0
        owner = jnp.where(
            i < 4,
            jnp.where(even, self.me, self.mate),
            jnp.where(even, self.far, self.diag),
        )
        return GROUPS * owner + (i // 2) % 2

    def place(self, i):
        return jnp.where(i % 2 == 0, i // 2, 4)

    def before(self, i):
        for g in range(GROUPS):

            @pl.when(i == 1 + 2 * g)
            def _():
                self.copy(1, g).wait_recv()

            @pl.when(i == 4 + 2 * g)
            def _():
                self.copy(0, g).wait_recv()
                self.copy(12, g).wait_recv()
                self.gath[self.stage % 2, GROUPS * self.far + g, MOST:ROWS] = self.get_edge(0, g)
                self.send(2, g)

            @pl.when(i == 5 + 2 * g)
            def _():
                self.copy(2, g).wait_recv()

    def after(self, i):
        for g in range(GROUPS):

            @pl.when(i == 1 + 2 * g)
            def _():
                self.again(3, g)
                self.out_po[g] = self.part[4].astype(BF16)
                self.send(3, g)

            @pl.when(i == 5 + 2 * g)
            def _():
                self.again(4, g)
                self.out_pd[g] = self.part[4].astype(BF16)
                self.send(4, g)
                self.copy(4, g).wait_recv()
                self.again(5, g)
                self.out_y[g] = (self.part[2 + g] + self.in_pd[g].astype(F32)).astype(BF16)
                self.again(13, g)
                self.set_edge(1, g, self.out_y[g, MOST:ROWS])
                self.copy(2, g).wait_send()
                self.send(5, g)
                self.send(13, g)

    def total(self, g):
        self.copy(3, g).wait_recv()
        self.copy(5, g).wait_recv()
        self.copy(13, g).wait_recv()
        self.in_y[g, MOST:ROWS] = self.get_edge(1, g)
        return self.part[g] + self.in_po[g].astype(F32) + self.in_y[g].astype(F32)

    def before_both(self, i):
        self.before(i)
        for g in range(GROUPS):

            @pl.when(i == 1 + 2 * g)
            def _():
                self.copy(7, g).wait_recv()

            @pl.when(i == 4 + 2 * g)
            def _():
                self.copy(6, g).wait_recv()
                self.copy(14, g).wait_recv()
                self.gath[0, GROUPS * self.far + g, MOST:ROWS] = self.get_edge(2, g)
                self.send(8, g)

            @pl.when(i == 5 + 2 * g)
            def _():
                self.copy(8, g).wait_recv()

    def set_aside(self, i, value, own_total):
        self.part[4] = value
        for g in range(GROUPS):

            @pl.when(i == 2 * g)
            def _():
                own_total(g, self.part[4])

            @pl.when(i == 1 + 2 * g)
            def _():
                self.spare[g] = self.part[4].astype(BF16)
                self.send(9, g)

            @pl.when(i == 4 + 2 * g)
            def _():
                self.late_y[g] = self.part[4].astype(BF16)

            @pl.when(i == 5 + 2 * g)
            def _():
                self.spare[4 + g] = self.part[4].astype(BF16)
                self.send(10, g)
                self.copy(10, g).wait_recv()
                both = self.late_y[g].astype(F32) + self.spare[6 + g].astype(F32)
                self.late_y[g] = both.astype(BF16)

    def end(self):
        for g in range(GROUPS):
            for kind in (0, 1, 3, 4, 5, 11, 12, 13):
                self.copy(kind, g).wait_send()


def exchange_scratch():
    return [
        pltpu.VMEM((2, 8, ROWS, D), BF16),
        pltpu.VMEM((5, ROWS, D), F32),
    ] + [pltpu.VMEM((GROUPS, ROWS, D), BF16)] * 6 + [pltpu.VMEM((3, GROUPS, EDGE - MOST, D), BF16)] * 2 + [
        pltpu.SemaphoreType.DMA((2, 15, GROUPS))
    ]


def picker(keep, image):
    patch = lax.broadcasted_iota(jnp.int32, (PATCHES, PATCHES), 0)
    return (keep[image : image + 1] == patch).astype(F32).astype(BF16)


def images_of(g):
    per = LIVE // PATCHES
    return [(g * per + m, m * PATCHES) for m in range(per)]


def live_rows(count, image):
    row = lax.broadcasted_iota(jnp.int32, (PATCHES, D), 0)
    return row < count[image]


def attend(x, q_bias, v_bias, wqkv, wout, counts, keep_parts):
    width = wout.shape[0]
    triple = dot(x, wqkv[...])
    q = (triple[:, :width] + q_bias).astype(BF16)
    k = triple[:, width : 2 * width].astype(BF16)
    v = (triple[:, 2 * width :] + v_bias).astype(BF16)
    keep_parts(0, q, k, v)
    lane = lax.broadcasted_iota(jnp.int32, (1, ROWS), 1)
    image = lane // PATCHES
    count = counts[LIVE - ROWS + 16 : LIVE - ROWS + 17]
    fits = (lane - image * PATCHES).astype(F32) < count
    row = lax.broadcasted_iota(jnp.int32, (ROWS, ROWS), 0)
    col = lax.broadcasted_iota(jnp.int32, (ROWS, ROWS), 1)
    same = jnp.minimum(row // PATCHES, 2) == col // PATCHES
    veil = jnp.where(same, 0.0, -1e30) + jnp.where(fits, 0.0, -1e30)
    mixed = jnp.zeros((ROWS, width), F32)
    for h in range(width // HEAD):
        mask = head_mask(h, width)
        scores = dot(q * mask, k, 1, 1) * SCALE + veil
        peak = jnp.max(scores, axis=-1, keepdims=True)
        raised = jnp.exp(scores - peak)
        weight = raised * (1.0 / jnp.sum(raised, axis=-1, keepdims=True))
        rounded = weight.astype(BF16)
        keep_parts(1 + h, rounded)
        mixed = mixed + dot(rounded, v * mask)
    return mixed.astype(BF16)


def erf_parts(pre):
    cdf = 0.5 * (1.0 + lax.erf(pre * (0.5 ** 0.5)))
    pdf = jnp.exp(-0.5 * pre * pre) * 0.3989422804014327
    return cdf, pdf


VM = pl.BlockSpec(memory_space=pltpu.VMEM)
HB = pl.BlockSpec(memory_space=pl.ANY)


def sds(shape, dtype):
    return jax.ShapeDtypeStruct(shape, dtype)


def params(n):
    return pltpu.CompilerParams(
        collective_id=n, has_side_effects=True, vmem_limit_bytes=67043328
    )


def column_sums(values):
    return jnp.sum(values, axis=0, keepdims=True)


class Scatter:
    order = (3, 1, 2, 0)

    def __init__(self, made, halves, arrivals, totals, outs, sems):
        self.made, self.halves, self.arrivals = made, halves, arrivals
        self.totals, self.outs = totals, outs
        self.x_sem, self.z_sem, self.out_sem, self.x_free, self.z_free = sems
        me = lax.axis_index("dp")
        self.x, self.z = me % 2, me // 2
        self.across = me + 1 - 2 * self.x
        self.near = self.z + 1 - 2 * (self.z % 2)
        self.far = (self.z + 2) % 4

    def device(self, z):
        return 2 * z + self.x

    def shard(self, k):
        return (self.z, self.near, self.far, (self.near + 2) % 4)[k]

    def number(self, j):
        third = (self.near + 2) % 4
        return jnp.where(
            j < 2, jnp.where(j == 0, third, self.near), jnp.where(j == 2, self.far, self.z)
        )

    def over_x(self, kind, part, j):
        n = self.number(j)
        return to_peer(
            "dp",
            self.made[kind][part].at[1 - self.x, n],
            self.halves[kind][part].at[n],
            self.x_sem.at[kind, part, j, 0],
            self.x_sem.at[kind, part, j, 1],
            self.across,
        )

    def over_z(self, kind, part, k):
        there, slot = {1: (self.near, 0), 3: (self.near, 1), 2: (self.far, 2)}[k]
        return to_peer(
            "dp",
            self.made[kind][part].at[self.x, self.shard(k)],
            self.arrivals[kind][part].at[slot],
            self.z_sem.at[kind, part, slot, 0],
            self.z_sem.at[kind, part, slot, 1],
            self.device(there),
        )

    def ready(self, s, part):
        if s >= 2:
            for j in range(4):
                self.over_x(s % 2, part, j).wait_send()
            for k in (1, 2, 3):
                self.over_z(s % 2, part, k).wait_send()

    def send(self, s, part, j):
        if s >= 2:
            pl.semaphore_wait(self.x_free.at[s % 2, part], 1)
        self.over_x(s % 2, part, j).start()

    def signal(self, sem, device):
        pl.semaphore_signal(
            sem, inc=1, device_id={"dp": device}, device_id_type=pl.DeviceIdType.MESH
        )

    def sum_rows(self, out, terms):
        def one(i, _):
            at = pl.ds(pl.multiple_of(i * COLS, COLS), COLS)
            value = terms[0][at, :].astype(F32)
            for term in terms[1:]:
                value = value + term[at, :].astype(F32)
            out[at, :] = value.astype(out.dtype)
            return 0

        lax.fori_loop(0, out.shape[0] // COLS, one, 0)

    def take(self, s, part, k):
        kind = s % 2
        mine = self.made[kind][part].at[self.x, self.shard(k)]
        terms = [mine, self.halves[kind][part].at[self.shard(k)]]
        self.over_x(kind, part, self.order.index(k)).wait_recv()
        if k == 2:
            self.over_z(kind, part, 3).wait_recv()
            terms.append(self.arrivals[kind][part].at[1])
        if k == 0:
            if s >= 2:
                self.store(s - 2, part, wait=True)
            mine = self.totals[kind][part]
        self.sum_rows(mine, terms)
        if s < 2:
            self.signal(self.x_free.at[kind, part], self.across)
            if k == 2:
                self.signal(self.z_free.at[kind, part, 1], self.device(self.near))
        if k:
            if s >= 2:
                slot = {1: 0, 3: 1, 2: 2}[k]
                pl.semaphore_wait(self.z_free.at[kind, part, slot], 1)
            self.over_z(kind, part, k).start()

    def store(self, s, part, wait=False):
        kind, n = s % 2, LAYERS - 1 - s // 2
        total, out = self.totals[kind][part], self.outs[kind][part]
        if kind == 1 and part == 1:
            width = out.shape[-1]
            pairs = [(total.at[:, pl.ds(c * width, width)], out.at[n, c]) for c in range(3)]
        else:
            pairs = [(total, out.at[n])]
        for c, pair in enumerate(pairs):
            copy = pltpu.make_async_copy(*pair, self.out_sem.at[kind, part, c])
            if wait:
                copy.wait()
            else:
                copy.start()

    def finish(self, s, part):
        kind = s % 2
        total, arrivals = self.totals[kind][part], self.arrivals[kind][part]
        self.over_z(kind, part, 1).wait_recv()
        self.over_z(kind, part, 2).wait_recv()
        self.sum_rows(total, [total, arrivals.at[0], arrivals.at[2]])
        self.store(s, part)
        if s < 2:
            self.signal(self.z_free.at[kind, part, 0], self.device(self.near))
            self.signal(self.z_free.at[kind, part, 2], self.device(self.far))

    def end(self):
        for s in (2, 3):
            for part in range(2):
                self.ready(s, part)
                self.store(s, part, wait=True)


def to_peer(axis, src, dst, send, recv, peer):
    return pltpu.make_async_remote_copy(
        src_ref=src,
        dst_ref=dst,
        send_sem=send,
        recv_sem=recv,
        device_id={axis: peer},
        device_id_type=pl.DeviceIdType.MESH,
    )


class SmallSum:
    def __init__(self, lines, arrived, over_z, out, sem, sc, mine):
        self.lines, self.arrived, self.over_z, self.out = lines, arrived, over_z, out
        self.sem, self.sc, self.mine = sem, sc, mine

    def across(self):
        s = self.sem
        return to_peer("dp", self.lines, self.arrived, s.at[0, 0], s.at[1, 0], self.sc.across)

    def along(self, k):
        part, s = self.over_z.at[self.sc.z], self.sem
        return to_peer("dp", part, part, s.at[0, k], s.at[1, k], self.sc.device((self.sc.z + k) % 4))

    def around(self, k):
        part, s = self.out.at[self.mine], self.sem
        peer = (self.mine + k) % 4
        return to_peer("tensor", part, part, s.at[0, 3 + k], s.at[1, 3 + k], peer)

    def second(self):
        self.across().wait()
        self.over_z[self.sc.z] = self.lines[...] + self.arrived[...]
        for k in range(1, 4):
            self.along(k).start()

    def third(self):
        for k in range(1, 4):
            self.along(k).wait()
        z = self.over_z
        self.out[self.mine] = z[0] + z[1] + z[2] + z[3]
        for k in range(1, 4):
            self.around(k).start()

    def last(self):
        for k in range(1, 4):
            self.around(k).wait()


def step_kernel(
    fused,
    count, patches, cot, keep, gains, shifts, bias_qv, bias_fc1, wqkv_h, wout_h, w1_h, w2_h,
    layer_h, patch_h, small_out, o_fc2, o_fc1, o_out, o_qkv,
    flow_h, gath_h, qkv_h, prob_h, att_h, gmlp_h, act_h, slope_h,
    gath, part, out_po, out_pd, out_y, in_po, in_pd, in_y, edge_out, edge_in, ex_sem,
    gradient, source, final, late_y, wqkv, wout, w1, w2,
    qkv, prob, att, norm_a, act, slope, norm_m,
    pre, triple, lines, cols_m, rows_m, cols_a, rows_a, load_sem, keep_sem, flow_sem, *rest,
):
    bufs = (out_po, out_pd, out_y, in_po, in_pd, in_y)
    ex = Exchange(gath, part, bufs, slope, late_y, (edge_out, edge_in), ex_sem)
    width, hidden = wout.shape[0], w1.shape[1]
    stages = 2 * LAYERS
    flat = 8 * ROWS
    made = ((cols_m, rows_m), (cols_a, rows_a))
    outs = ((o_fc2, o_fc1), (o_out, o_qkv))
    if fused:
        halves, arrivals, totals = (
            ((rest[4 * n], rest[4 * n + 1]), (rest[4 * n + 2], rest[4 * n + 3])) for n in range(3)
        )
        small_in, small_z, small_sem = rest[12:15]
        sc = Scatter(made, halves, arrivals, totals, outs, rest[15:20])
    else:
        sc = None
        save_sem = rest[0]

    def layer(s):
        return LAYERS - 1 - s // 2

    def loads(s):
        n = layer(s)
        if s < 2:
            return []
        if s % 2 == 0:
            pairs = (
                (w2_h.at[n], w2),
                (slope_h, slope),
                (w1_h.at[n], w1),
                (act_h, act),
                (gmlp_h, norm_m),
                (flow_h.at[1], source.at[0]),
            )
        else:
            pairs = tuple(
                (wqkv_h.at[n, c], wqkv.at[:, pl.ds(c * width, width)]) for c in range(3)
            ) + (
                (wout_h.at[n], wout),
                (qkv_h, qkv),
                (prob_h, prob),
                (att_h, att),
                (gath_h, norm_a),
                (flow_h.at[0], source.at[1]),
            )
        return [
            pltpu.make_async_copy(*pair, load_sem.at[s % 2, m]) for m, pair in enumerate(pairs)
        ]

    def forward_loads(s):
        n = s // 2
        if s % 2 == 0:
            pairs = [
                (wqkv_h.at[n, c], wqkv.at[:, pl.ds(c * width, width)]) for c in range(3)
            ] + [(wout_h.at[n], wout)]
        else:
            pairs = [(w1_h.at[n], w1), (w2_h.at[n], w2)]
        return [
            pltpu.make_async_copy(*pair, load_sem.at[s % 2, m]) for m, pair in enumerate(pairs)
        ]

    for s in range(2):
        for copy in forward_loads(s):
            copy.start()
    barrier = pltpu.get_barrier_semaphore()
    peers = [{"tensor": ex.mate}, {"tensor": ex.far}]
    if fused:
        peers += [{"tensor": ex.diag}, {"dp": sc.across}]
        peers += [{"dp": sc.device((sc.z + k) % 4)} for k in range(1, 4)]
    for peer in peers:
        pl.semaphore_signal(barrier, inc=1, device_id=peer, device_id_type=pl.DeviceIdType.MESH)

    def note(at, g, row):
        lines[at : at + 1] = row if g == 0 else lines[at : at + 1] + row

    def hold(s):
        return source.at[(s + 1) % 2]

    def save_flow(s, g):
        return pltpu.make_async_copy(hold(s).at[g], flow_h.at[s, g], flow_sem.at[s, g])

    def begin(s, g):
        n = s // 2
        held = hold(s)
        if s >= 2:
            save_flow(s - 2, g).wait()
        if s == 0:
            for image, at in images_of(g):
                held[g, at : at + PATCHES] = dot(picker(keep, image), patches[image], 0, 0)
            held[g, LIVE:] = jnp.zeros((ROWS - LIVE, D), F32)
            value = held[g]
        else:
            shift = shifts[(s - 1) // 2, 2 + (s - 1) % 2].reshape(1, D)
            value = hold(s - 1)[g] + ex.total(g) + shift
            held[g] = value
        if s < 2:
            save_flow(s, g).start()
        unit, _ = norm_parts(value)
        gain, shift = gains[n, s % 2].reshape(1, D), shifts[n, s % 2].reshape(1, D)
        own = ex.own(g)
        ex.clear(g)
        gath[s % 2, own] = (unit * gain + shift).astype(BF16)
        tail = gath[s % 2, own, ROWS - 16 : ROWS, 0:256].astype(F32)
        row = lax.broadcasted_iota(jnp.int32, (16, 256), 0)
        lane = lax.broadcasted_iota(jnp.int32, (16, 256), 1)
        for image, at in images_of(g):
            here = (row == LIVE - ROWS + 16) & (lane >= at)
            tail = jnp.where(here, count[image].astype(F32), tail)
        gath[s % 2, own, ROWS - 16 : ROWS, 0:256] = tail.astype(BF16)
        if s == 0 and g == 0:
            pl.semaphore_wait(barrier, len(peers))
        ex.share(g)
        if s < stages - 1:
            return
        gradient[g, LIVE:] = jnp.zeros((ROWS - LIVE, D), F32)
        for image, at in images_of(g):
            piece = jnp.where(live_rows(count, image), cot[image].astype(F32), 0.0)
            gradient[g, at : at + PATCHES] = piece
        rounded = gradient[g].astype(BF16)
        note(4 + 4 * n + 3, g, column_sums(rounded.astype(F32)))
        gath[0, own] = rounded
        ex.set_edge(2, g, gath[0, own, MOST:ROWS])
        ex.send(14, g)
        ex.send(6, g)
        ex.send(7, g)

    def saves(s, slot):
        if s == 0:
            pairs = (
                (gath.at[0, slot], gath_h),
                (qkv.at[slot], qkv_h),
                (prob.at[slot], prob_h),
                (att.at[slot], att_h),
            )
        elif s == 1:
            pairs = ((gath.at[1, slot], gmlp_h), (act.at[slot], act_h), (slope.at[slot], slope_h))
        else:
            pairs = ()
        return [
            pltpu.make_async_copy(a, b.at[slot], keep_sem.at[m, slot])
            for m, (a, b) in enumerate(pairs)
        ]

    def drain(s):
        def one(slot, _):
            for copy in saves(s, slot):
                copy.wait()
            return 0

        lax.fori_loop(0, 8, one, 0)

    def own_total(g, value):
        final[g] = source[0, g] + value + shifts[LAYERS - 1, 3].reshape(1, D)

    lines[15:16] = jnp.zeros((1, D), F32)
    for s in range(stages):
        n = s // 2
        ex.stage = s
        begin(s, 0)
        if s == 0:
            begin(s, 1)
        elif s <= 2:
            drain(s - 1)
        for copy in forward_loads(s):
            copy.wait()
        if 1 <= s < stages - 1:
            for copy in forward_loads(s + 1):
                copy.start()

        def step(i, _, s=s, n=n):
            if s:

                @pl.when(i == 2)
                def _():
                    begin(s, 1)

            both = s == stages - 1
            (ex.before_both if both else ex.before)(i)
            slot = ex.slot(i)
            x = gath[s % 2, slot]
            if s >= 2:
                (norm_a, norm_m)[s % 2][slot] = x
            if s % 2 == 0:

                def keep_parts(kind, *values):
                    if kind == 0:
                        for c, value in enumerate(values):
                            qkv[slot, :, c * width : (c + 1) * width] = value
                    else:
                        prob[slot, (kind - 1) * ROWS : kind * ROWS] = values[0]

                tail = gath[0, slot, ROWS - 16 : ROWS, 0:256][:, 0:ROWS].astype(F32)
                mixed = attend(
                    x, bias_qv[n, 0:1], bias_qv[n, 1:2], wqkv, wout, tail, keep_parts
                )
                att[slot] = mixed
                part[ex.place(i)] = dot(mixed, wout[...])
            else:
                for block in range(hidden // 256):
                    at = slice(block * 256, block * 256 + 256)
                    pre_act = dot(x, w1[:, at]) + bias_fc1[n : n + 1, at]
                    cdf, pdf = erf_parts(pre_act)
                    act[slot, :, at] = (pre_act * cdf).astype(BF16)
                    steep = cdf + pre_act * pdf
                    if both:
                        d_act = dot(gath[0, slot], w2[at, :], 1, 1)
                        pre[slot, :, at] = (d_act * steep).astype(BF16)
                    else:
                        slope[slot, :, at] = steep.astype(BF16)
                value = dot(act[slot], w2[...])
                if both:
                    ex.set_aside(i, value, own_total)
                    value = dot(pre[slot], w1[...], 1, 1)
                part[ex.place(i)] = value
            for copy in saves(s, slot):
                copy.start()
            ex.after(i)
            return 0

        lax.fori_loop(0, 8, step, 0)

    def complete_output():
        for g in range(GROUPS):
            ex.copy(11, g).wait_recv()
            final[g] = final[g] + in_pd[g].astype(F32)
            pltpu.make_async_copy(final.at[g], layer_h.at[g], flow_sem.at[1, g]).start()

    def produce(s, g):
        n, side = layer(s - 1), s % 2
        gain = gains[n, side].reshape(1, D)
        moved = ex.total(g)
        unit, scale = norm_parts(source[1 - side, g])
        note(2 * n + side, g, column_sums(moved * unit))
        note(4 + 4 * n + side, g, column_sums(moved))
        scaled = moved * gain
        lean = jnp.mean(scaled, axis=-1, keepdims=True)
        tilt = jnp.mean(scaled * unit, axis=-1, keepdims=True)
        grad = gradient[g] + scale * (scaled - lean - unit * tilt)
        rounded = grad.astype(BF16)
        if s < stages:
            gradient[g] = grad
        else:
            gradient[g] = grad
            for image, at in images_of(g):
                exact = gradient[g, at : at + PATCHES]
                high = exact.astype(BF16)
                low = (exact - high.astype(F32)).astype(BF16)
                pick = picker(keep, image)
                source[0, g, at : at + PATCHES] = dot(pick, high) + dot(pick, low)
            pltpu.make_async_copy(source.at[0, g], patch_h.at[g], flow_sem.at[0, g]).start()
            return
        if s % 2 == 0:
            note(4 + 4 * layer(s) + 3, g, column_sums(rounded.astype(F32)))
        else:
            note(4 + 4 * layer(s) + 2, g, column_sums(rounded.astype(F32)))
        ex.clear(g)
        gath[s % 2, ex.own(g)] = rounded
        ex.share(g)

    def spill(s, part, k):
        return [
            pltpu.make_async_copy(
                made[s % 2][part].at[half, k],
                outs[s % 2][part].at[layer(s), half, k],
                save_sem.at[s % 2, part, k, half],
            )
            for half in range(2)
        ]

    def column_block(s, j):
        n = sc.number(j) if fused else j
        at = pl.ds(pl.multiple_of(n * 256, 256), 256)
        some = gath[s % 2, :, :, at].reshape(flat, 256)
        left = (act, att)[s % 2]
        wide = dot(left[...].reshape(flat, left.shape[-1]), some, 0, 0).astype(BF16)
        out = made[s % 2][0]
        out[0, n] = wide[:, :COLS]
        out[1, n] = wide[:, COLS:]
        if fused:
            if s < stages - 1:
                sc.send(s, 0, j)
        else:
            for copy in spill(s, 0, j):
                copy.start()

    def row_block(s, j):
        n = sc.number(j) if fused else j
        at = pl.ds(pl.multiple_of(n * 256, 256), 256)
        left, right = ((norm_m, pre), (norm_a, triple))[s % 2]
        some = left[:, :, at].reshape(flat, 256)
        tall = dot(some, right[...].reshape(flat, right.shape[-1]), 0, 0).astype(BF16)
        out = made[s % 2][1]
        out[0, n] = tall[:COLS]
        out[1, n] = tall[COLS:]
        if fused:
            if s < stages - 1:
                sc.send(s, 1, j)
        else:
            for copy in spill(s, 1, j):
                copy.start()

    def settle(s, part):
        if fused:
            sc.ready(s, part)
        elif s >= 2:
            for k in range(4):
                for copy in spill(s - 2, part, k):
                    copy.wait()

    def columns(s):
        settle(s, 0)

        def one(j, _):
            column_block(s, j)
            return 0

        lax.fori_loop(0, 4, one, 0)

    def some_rows(s, start, count):
        def one(j, _):
            row_block(s, start + j)
            return 0

        lax.fori_loop(0, count, one, 0)

    def bias_sums(s):
        n = layer(s)
        ones = jnp.ones((8, flat), BF16)
        if s % 2 == 0:
            lines[12 + n : 13 + n] = dot(ones, pre[...].reshape(flat, hidden))[0:1]
        else:
            sums = dot(ones, triple[...].reshape(flat, 3 * width))[0:1]
            at = 2 * n * width
            lines[14:15, at : at + width] = sums[:, :width]
            lines[14:15, at + width : at + 2 * width] = sums[:, 2 * width :]

    def take(*work):
        def run():
            if fused:
                for s, part, k in work:
                    if k == 4:
                        sc.finish(s, part)
                    else:
                        sc.take(s, part, k)

        return run

    plan = {
        (1, 4): take((0, 0, 3)),
        (1, 6): take((0, 0, 1)),
        (1, 8): take((0, 0, 2)),
        (2, 2): take((0, 0, 0), (0, 1, 3)),
        (2, 4): take((0, 1, 1)),
        (2, 6): take((0, 1, 2)),
        (2, 8): take((0, 1, 0), (0, 0, 4), (1, 0, 3), (1, 0, 1)),
        (3, 2): take((1, 0, 2), (1, 0, 0), (1, 1, 3), (1, 1, 1)),
        (3, 4): take((0, 1, 4), (1, 1, 2)),
        (3, 6): take((1, 0, 4), (1, 1, 0), (2, 0, 3)),
        (3, 8): take((2, 0, 1), (1, 1, 4)),
    }

    for s in range(1, stages):
        ex.stage = stages + s
        columns(s - 1)
        if s == 1:
            for g in range(GROUPS):
                for kind in (6, 7, 8, 14):
                    ex.copy(kind, g).wait_send()
                ex.copy(9, g).wait()
                ex.copy(10, g).wait_send()
                final[g] = final[g] + ex.spare[2 + g].astype(F32)
        produce(s, 0)
        early = (3, 6)[s % 2]
        for copy in loads(s)[:early]:
            copy.wait()

        def step(i, _, s=s):
            if s:

                @pl.when(i == 2)
                def _():
                    settle(s - 1, 1)

                @pl.when((i == 2) | (i == 4))
                def _():
                    some_rows(s - 1, i - 2, 2)

            @pl.when(i == 2)
            def _():
                produce(s, 1)

            if s:

                @pl.when(i == 6)
                def _():
                    bias_sums(s - 1)
                    if s + 1 < stages:
                        for copy in loads(s + 1) if s >= 1 else ():
                            copy.start()

            for (stage, at), task in plan.items():
                if stage == s and at < 8:
                    pl.when(i == at)(task)
            ex.before(i)
            slot = ex.slot(i)
            grad = gath[s % 2, slot]
            if s % 2 == 0:
                for block in range(hidden // 256):
                    at = slice(block * 256, block * 256 + 256)
                    d_act = dot(grad, w2[at, :], 1, 1)
                    pre[slot, :, at] = (d_act * slope[slot, :, at].astype(F32)).astype(BF16)
                part[ex.place(i)] = dot(pre[slot], w1[...], 1, 1)
            else:
                d_att = dot(grad, wout[...], 1, 1).astype(BF16)
                q = qkv[slot, :, 0:width]
                k = qkv[slot, :, width : 2 * width]
                v = qkv[slot, :, 2 * width :]
                d_q = jnp.zeros((ROWS, width), F32)
                d_k = jnp.zeros((ROWS, width), F32)
                d_v = jnp.zeros((ROWS, width), F32)
                for h in range(width // HEAD):
                    mask = head_mask(h, width)
                    d_one = d_att * mask
                    rounded = prob[slot, h * ROWS : (h + 1) * ROWS]
                    weight = rounded.astype(F32)
                    d_prob = dot(d_one, v, 1, 1)
                    centre = jnp.sum(weight * d_prob, axis=-1, keepdims=True)
                    d_scores = (weight * (d_prob - centre)).astype(BF16)
                    d_q = d_q + dot(d_scores, k * mask)
                    d_k = d_k + dot(d_scores, q * mask, 0, 0)
                    d_v = d_v + dot(rounded, d_one, 0, 0)
                triple[slot, :, 0:width] = (d_q * SCALE).astype(BF16)
                triple[slot, :, width : 2 * width] = (d_k * SCALE).astype(BF16)
                triple[slot, :, 2 * width :] = d_v.astype(BF16)
                part[ex.place(i)] = dot(triple[slot], wqkv[...], 1, 1)
            ex.after(i)
            return 0

        lax.fori_loop(0, 8, step, 0)
        for copy in loads(s)[early:]:
            copy.wait()
        if (s, 8) in plan:
            plan[s, 8]()
    last = stages - 1
    columns(last)
    settle(last, 1)
    some_rows(last, 0, 4)
    bias_sums(last)
    take((2, 0, 2), (2, 0, 0))()
    for g in range(GROUPS):
        produce(stages, g)
    for g in range(GROUPS):
        ex.send(11, g)
    if fused:
        tiny = SmallSum(lines, small_in, small_z, small_out, small_sem, sc, ex.me)
        tiny.across().start()
        for side in (1, 0):
            for j in range(4):
                sc.send(last, side, j)
        take((2, 1, 3), (2, 1, 1), (2, 0, 4), (2, 1, 2), (2, 1, 0))()
        complete_output()
        tiny.second()
        take((2, 1, 4), (3, 1, 3), (3, 1, 1))()
        tiny.third()
        take((3, 1, 2), (3, 1, 0), (3, 0, 3), (3, 0, 1), (3, 0, 2), (3, 1, 4), (3, 0, 0), (3, 0, 4))()
        sc.end()
        tiny.last()
    else:
        complete_output()
        small_out[...] = lines[...]
        for s in (2, 3):
            for side in range(2):
                for k in range(4):
                    for copy in spill(s, side, k):
                        copy.wait()
    ex.end()
    for g in range(GROUPS):
        pltpu.make_async_copy(source.at[0, g], patch_h.at[g], flow_sem.at[0, g]).wait()
        pltpu.make_async_copy(final.at[g], layer_h.at[g], flow_sem.at[1, g]).wait()


def run_step(fused, count, patches, cot, keep, gains, shifts, bias_qv, bias_fc1, wqkv, wout, w1, w2):
    width, hidden = wout.shape[1], w1.shape[2]
    heads = width // HEAD
    wide, own = (8, ROWS, D), (GROUPS, ROWS, D)
    dma = pltpu.SemaphoreType.DMA
    tall = D // 256
    mine = ((hidden, COLS), (COLS, hidden), (width, COLS), (COLS, 3 * width))
    blocks = [(2, tall) + m for m in mine]
    if fused:
        outs = [
            sds((LAYERS, hidden, COLS), F32),
            sds((LAYERS, COLS, hidden), F32),
            sds((LAYERS, width, COLS), F32),
            sds((LAYERS, 3, COLS, width), F32),
        ]
        small = sds((4, 16, D), F32)
        regular = pltpu.SemaphoreType.REGULAR
        more = (
            [pltpu.VMEM((4,) + m, BF16) for m in mine]
            + [pltpu.VMEM((3,) + m, BF16) for m in mine]
            + [pltpu.VMEM(m, F32) for m in mine]
            + [pltpu.VMEM((16, D), F32), pltpu.VMEM((4, 16, D), F32), dma((2, 7))]
            + [dma((2, 2, 4, 2)), dma((2, 2, 3, 2)), dma((2, 2, 3))]
            + [regular((2, 2)), regular((2, 2, 3))]
        )
    else:
        outs = [sds((LAYERS,) + b, BF16) for b in blocks]
        small = sds((16, D), F32)
        more = [dma((2, 2, 4, 2))]
    inner = ((8, ROWS, 3 * width), (8, heads * ROWS, ROWS), (8, ROWS, width))
    mlp = ((8, ROWS, hidden), (8, ROWS, hidden))
    saved = (wide,) + inner + (wide,) + mlp
    return pl.pallas_call(
        partial(step_kernel, fused),
        out_shape=[sds(own, F32), sds(own, F32), small]
        + outs
        + [sds((2,) + own, F32)]
        + [sds(k, BF16) for k in saved],
        in_specs=[pl.BlockSpec(memory_space=pltpu.SMEM)] + [VM] * 7 + [HB] * 4,
        out_specs=[HB] * 2 + [VM] + [HB] * 12,
        scratch_shapes=exchange_scratch()
        + [
            pltpu.VMEM(own, F32),
            pltpu.VMEM((2,) + own, F32),
            pltpu.VMEM(own, F32),
            pltpu.VMEM(own, BF16),
            pltpu.VMEM((D, 3 * width), BF16),
            pltpu.VMEM((width, D), BF16),
            pltpu.VMEM((D, hidden), BF16),
            pltpu.VMEM((hidden, D), BF16),
        ]
        + [pltpu.VMEM(k, BF16) for k in inner + (wide,) + mlp + (wide,)]
        + [pltpu.VMEM((8, ROWS, hidden), BF16), pltpu.VMEM((8, ROWS, 3 * width), BF16)]
        + [pltpu.VMEM((16, D), F32)]
        + [pltpu.VMEM(b, BF16) for b in blocks]
        + [dma((2, 9)), dma((4, 8)), dma((2, GROUPS))]
        + more,
        compiler_params=params(1),
    )(count, patches, cot, keep, gains, shifts, bias_qv, bias_fc1, wqkv, wout, w1, w2)[:7]


def deliver_kernel(
    count, layer, patch, small, a_h, b_h, c_h, d_h,
    layer_out, patch_out, gain, shift, qv, fc1, a_out, b_out, c_out, d_out,
    a, b, c, d, sems,
):
    held = ((a_h, a, a_out), (b_h, b, b_out), (c_h, c, c_out), (d_h, d, d_out))

    def inward(n):
        return pltpu.make_async_copy(held[n][0], held[n][1], sems.at[0, n])

    def outward(n):
        return pltpu.make_async_copy(held[n][1], held[n][2], sems.at[1, n])

    for n in range(4):
        inward(n).start()
    for g in range(GROUPS):
        for image, at in images_of(g):
            rows = layer[g, at : at + PATCHES]
            layer_out[image] = jnp.where(live_rows(count, image), rows, 0.0)
            patch_out[image] = patch[g, at : at + PATCHES]
    for n in range(4):
        inward(n).wait()
        outward(n).start()
    summed = small[0, 0:12] + small[1, 0:12] + small[2, 0:12] + small[3, 0:12]
    for n in range(LAYERS):
        gain[n] = summed[2 * n : 2 * n + 2]
        shift[n] = summed[4 + 4 * n : 8 + 4 * n]
        for t in range(4):
            hidden = fc1.shape[1] // 4
            fc1[n : n + 1, t * hidden : (t + 1) * hidden] = small[t, 12 + n : 13 + n]
            width = D // 4
            for side in range(2):
                at = (2 * n + side) * width
                piece = small[t, 14:15, at : at + width]
                qv[n, side : side + 1, t * width : (t + 1) * width] = piece
    for n in range(4):
        outward(n).wait()


def deliver(count, layer, patch, small, grads):
    images = (GROUPS * LIVE // PATCHES, PATCHES, D)
    shapes = [g.shape for g in grads]
    return pl.pallas_call(
        deliver_kernel,
        out_shape=[
            sds(images, F32),
            sds(images, F32),
            sds((LAYERS, 2, D), F32),
            sds((LAYERS, 4, D), F32),
            sds((LAYERS, 2, D), F32),
            sds((LAYERS, FF), F32),
        ]
        + [sds(s, F32) for s in shapes],
        in_specs=[pl.BlockSpec(memory_space=pltpu.SMEM)] + [VM] * 3 + [HB] * 4,
        out_specs=[VM] * 6 + [HB] * 4,
        scratch_shapes=[pltpu.VMEM(s, F32) for s in shapes] + [pltpu.SemaphoreType.DMA((2, 4))],
    )(count, layer, patch, small, *grads)


def from_groups(array):
    return array[:, :LIVE].reshape(GROUPS * (LIVE // PATCHES), PATCHES, D)


def collect_weight(partial_grad, split_dim):
    return lax.psum_scatter(
        partial_grad, "dp", scatter_dimension=split_dim, tiled=True
    ).astype(F32)


def join_rows(blocks):
    return jnp.transpose(blocks, (1, 0, 2, 3)).reshape(D, -1)


def join_columns(blocks):
    return jnp.transpose(blocks, (2, 1, 0, 3)).reshape(blocks.shape[2], -1)


def local(
    patches,
    keep_index,
    kept_count,
    norm_gain,
    shifts,
    w_qkv,
    bias_qv,
    w_out,
    w_fc1,
    bias_fc1,
    w_fc2,
    cotangent,
):
    width = w_qkv.shape[-1]
    hidden = w_fc1.shape[-1]
    dp_size, ways = lax.axis_size("dp"), lax.axis_size("tensor")
    assert ways == 4
    wqkv = jnp.transpose(w_qkv, (0, 2, 1, 3))
    fused = dp_size == 8 and hidden == D and 4 * width == D
    layer, patch, small, g_fc2, g_fc1, g_out, g_qkv = run_step(
        fused, kept_count, patches, cotangent, keep_index, norm_gain, shifts, bias_qv, bias_fc1,
        wqkv, w_out, w_fc1, w_fc2,
    )
    if fused:
        layer_out, grad_patches, gain, shift, qv, fc1, g_fc2, g_fc1, g_out, g_qkv = deliver(
            kept_count, layer, patch, small, (g_fc2, g_fc1, g_out, g_qkv)
        )
        grad_qkv = jnp.transpose(g_qkv, (0, 2, 1, 3))
        return layer_out, grad_patches, gain, shift, grad_qkv, qv, g_out, g_fc1, fc1, g_fc2
    slot_ids = jnp.arange(PATCHES, dtype=jnp.int32)
    own_mask = (slot_ids[None, :] < kept_count[:, None])[:, :, None]
    layer_out = from_groups(layer) * own_mask.astype(F32)
    grad_patches = from_groups(patch)
    grad_qkv, grad_out, grad_fc1, grad_fc2 = (
        jnp.stack([collect_weight(join(array[n]), split) for n in range(LAYERS)])
        for array, join, split in (
            (g_qkv, join_rows, 0),
            (g_out, join_columns, 1),
            (g_fc1, join_rows, 0),
            (g_fc2, join_columns, 1),
        )
    )
    grad_qkv = grad_qkv.reshape(LAYERS, -1, 3, width)
    small = lax.all_gather(lax.psum(small, "dp"), "tensor")
    summed = jnp.sum(small[:, :12], axis=0)
    grad_gain = summed[:4].reshape(LAYERS, 2, D)
    grad_shifts = summed[4:].reshape(LAYERS, 4, D)
    grad_bias_fc1 = jnp.transpose(small[:, 12:14], (1, 0, 2)).reshape(LAYERS, ways * hidden)
    quarters = small[:, 14, : 2 * LAYERS * width].reshape(ways, LAYERS, 2, width)
    grad_bias_qv = jnp.transpose(quarters, (1, 2, 0, 3)).reshape(LAYERS, 2, ways * width)
    return (
        layer_out,
        grad_patches,
        grad_gain,
        grad_shifts,
        grad_qkv,
        grad_bias_qv,
        grad_out,
        grad_fc1,
        grad_bias_fc1,
        grad_fc2,
    )


def solution(mesh):
    in_specs = (
        P(("dp", "tensor"), None, None),
        P(("dp", "tensor"), None),
        P(("dp", "tensor")),
        P(),
        P(),
        P(None, None, None, "tensor"),
        P(None, None, "tensor"),
        P(None, "tensor", None),
        P(None, None, "tensor"),
        P(None, "tensor"),
        P(None, "tensor", None),
        P(("dp", "tensor"), None, None),
    )
    out_specs = (
        P(("dp", "tensor"), None, None),
        P(("dp", "tensor"), None, None),
        P(),
        P(),
        P(None, "dp", None, "tensor"),
        P(),
        P(None, "tensor", "dp"),
        P(None, "dp", "tensor"),
        P(),
        P(None, "tensor", "dp"),
    )
    return jax.shard_map(local, mesh=mesh, in_specs=in_specs, out_specs=out_specs, check_vma=False)
```

```python
from functools import partial

import jax
import jax.numpy as jnp
from jax import lax
from jax.experimental import pallas as pl
from jax.experimental.pallas import tpu as pltpu
from jax.sharding import PartitionSpec as P

D = 1024
HEAD = 64
FF = 4096
LAYERS = 2
PATCHES = 50
EPS = 1e-06
HIGHEST = lax.Precision.HIGHEST
F32 = jnp.float32
BF16 = jnp.bfloat16

GROUPS = 2
ROWS = 160
LIVE = 150
MOST, EDGE = 144, 152
COLS = 128
SCALE = HEAD ** (-0.5)


def dot(a, b, lhs=1, rhs=0):
    return lax.dot_general(a, b, (((lhs,), (rhs,)), ((), ())), preferred_element_type=F32)


def remote(src, dst, send, recv, peer):
    return pltpu.make_async_remote_copy(
        src_ref=src,
        dst_ref=dst,
        send_sem=send,
        recv_sem=recv,
        device_id={"tensor": peer},
        device_id_type=pl.DeviceIdType.MESH,
    )


def norm_parts(values):
    average = jnp.mean(values, axis=-1, keepdims=True)
    centred = values - average
    variance = jnp.mean(centred * centred, axis=-1, keepdims=True)
    scale = lax.rsqrt(variance + EPS)
    return centred * scale, scale


def head_mask(h, width):
    lane = lax.broadcasted_iota(jnp.int32, (1, width), 1)
    return (lane // HEAD == h).astype(F32).astype(BF16)


class Exchange:
    def __init__(self, gath, part, bufs, spare, late_y, edges, sems):
        self.edge_out, self.edge_in = edges
        self.gath, self.part = gath, part
        self.out_po, self.out_pd, self.out_y, self.in_po, self.in_pd, self.in_y = bufs
        self.spare, self.late_y = spare, late_y
        self.sem = sems
        me = lax.axis_index("tensor")
        self.me = me
        self.mate = me + 1 - 2 * (me % 2)
        self.far = (me + 2) % 4
        self.diag = (self.mate + 2) % 4
        self.stage = 0

    def barrier(self):
        sem = pltpu.get_barrier_semaphore()
        for peer in (self.mate, self.far):
            pl.semaphore_signal(
                sem, inc=1, device_id={"tensor": peer}, device_id_type=pl.DeviceIdType.MESH
            )
        pl.semaphore_wait(sem, 2)

    def own(self, g):
        return GROUPS * self.me + g

    def rows(self, slot):
        return self.gath.at[self.stage % 2, slot]

    def copy(self, kind, g):
        s = self.sem
        own, slot = self.rows(self.own(g)), self.rows(GROUPS * self.far + g)
        most = pl.ds(0, MOST)
        far_own = self.gath.at[self.stage % 2, self.own(g), most]
        far_own_0 = self.gath.at[0, self.own(g), most]
        own_0, slot_0 = self.gath.at[0, self.own(g)], self.gath.at[0, GROUPS * self.far + g]
        spare = self.spare
        src, dst, peer = (
            (far_own, far_own, self.far),
            (own, own, self.mate),
            (slot, slot, self.mate),
            (self.out_po.at[g], self.in_po.at[g], self.mate),
            (self.out_pd.at[g], self.in_pd.at[g], self.mate),
            (self.out_y.at[g, most], self.in_y.at[g, most], self.far),
            (far_own_0, far_own_0, self.far),
            (own_0, own_0, self.mate),
            (slot_0, slot_0, self.mate),
            (spare.at[g], spare.at[2 + g], self.mate),
            (spare.at[4 + g], spare.at[6 + g], self.mate),
            (self.late_y.at[g], self.in_pd.at[g], self.far),
            (self.edge_out.at[0, g], self.edge_in.at[0, g], self.far),
            (self.edge_out.at[1, g], self.edge_in.at[1, g], self.far),
            (self.edge_out.at[2, g], self.edge_in.at[2, g], self.far),
        )[kind]
        return remote(src, dst, s.at[0, kind, g], s.at[1, kind, g], peer)

    def again(self, kind, g):
        if self.stage:
            self.copy(kind, g).wait_send()

    def send(self, kind, g):
        self.copy(kind, g).start()

    def clear(self, g):
        for kind in (0, 1, 12):
            self.again(kind, g)

    def set_edge(self, n, g, rows):
        self.edge_out[n, g] = rows.astype(F32)[0 : EDGE - MOST].astype(BF16)

    def get_edge(self, n, g):
        rows = self.edge_in[n, g].astype(F32)
        return jnp.concatenate([rows, jnp.zeros((ROWS - EDGE, D), F32)]).astype(BF16)

    def share(self, g):
        self.set_edge(0, g, self.gath[self.stage % 2, self.own(g), MOST:ROWS])
        self.send(12, g)
        for kind in range(2):
            self.send(kind, g)

    def slot(self, i):
        even = i % 2 == 0
        owner = jnp.where(
            i < 4,
            jnp.where(even, self.me, self.mate),
            jnp.where(even, self.far, self.diag),
        )
        return GROUPS * owner + (i // 2) % 2

    def place(self, i):
        return jnp.where(i % 2 == 0, i // 2, 4)

    def before(self, i):
        for g in range(GROUPS):

            @pl.when(i == 1 + 2 * g)
            def _():
                self.copy(1, g).wait_recv()

            @pl.when(i == 4 + 2 * g)
            def _():
                self.copy(0, g).wait_recv()
                self.copy(12, g).wait_recv()
                self.gath[self.stage % 2, GROUPS * self.far + g, MOST:ROWS] = self.get_edge(0, g)
                self.send(2, g)

            @pl.when(i == 5 + 2 * g)
            def _():
                self.copy(2, g).wait_recv()

    def after(self, i):
        for g in range(GROUPS):

            @pl.when(i == 1 + 2 * g)
            def _():
                self.again(3, g)
                self.out_po[g] = self.part[4].astype(BF16)
                self.send(3, g)

            @pl.when(i == 5 + 2 * g)
            def _():
                self.again(4, g)
                self.out_pd[g] = self.part[4].astype(BF16)
                self.send(4, g)
                self.copy(4, g).wait_recv()
                self.again(5, g)
                self.out_y[g] = (self.part[2 + g] + self.in_pd[g].astype(F32)).astype(BF16)
                self.again(13, g)
                self.set_edge(1, g, self.out_y[g, MOST:ROWS])
                self.copy(2, g).wait_send()
                self.send(5, g)
                self.send(13, g)

    def total(self, g):
        self.copy(3, g).wait_recv()
        self.copy(5, g).wait_recv()
        self.copy(13, g).wait_recv()
        self.in_y[g, MOST:ROWS] = self.get_edge(1, g)
        return self.part[g] + self.in_po[g].astype(F32) + self.in_y[g].astype(F32)

    def before_both(self, i):
        self.before(i)
        for g in range(GROUPS):

            @pl.when(i == 1 + 2 * g)
            def _():
                self.copy(7, g).wait_recv()

            @pl.when(i == 4 + 2 * g)
            def _():
                self.copy(6, g).wait_recv()
                self.copy(14, g).wait_recv()
                self.gath[0, GROUPS * self.far + g, MOST:ROWS] = self.get_edge(2, g)
                self.send(8, g)

            @pl.when(i == 5 + 2 * g)
            def _():
                self.copy(8, g).wait_recv()

    def set_aside(self, i, value, own_total):
        self.part[4] = value
        for g in range(GROUPS):

            @pl.when(i == 2 * g)
            def _():
                own_total(g, self.part[4])

            @pl.when(i == 1 + 2 * g)
            def _():
                self.spare[g] = self.part[4].astype(BF16)
                self.send(9, g)

            @pl.when(i == 4 + 2 * g)
            def _():
                self.late_y[g] = self.part[4].astype(BF16)

            @pl.when(i == 5 + 2 * g)
            def _():
                self.spare[4 + g] = self.part[4].astype(BF16)
                self.send(10, g)
                self.copy(10, g).wait_recv()
                both = self.late_y[g].astype(F32) + self.spare[6 + g].astype(F32)
                self.late_y[g] = both.astype(BF16)

    def end(self):
        for g in range(GROUPS):
            for kind in (0, 1, 3, 4, 5, 11, 12, 13):
                self.copy(kind, g).wait_send()


def exchange_scratch():
    return [
        pltpu.VMEM((2, 8, ROWS, D), BF16),
        pltpu.VMEM((5, ROWS, D), F32),
    ] + [pltpu.VMEM((GROUPS, ROWS, D), BF16)] * 6 + [pltpu.VMEM((3, GROUPS, EDGE - MOST, D), BF16)] * 2 + [
        pltpu.SemaphoreType.DMA((2, 15, GROUPS))
    ]


def picker(keep, image):
    patch = lax.broadcasted_iota(jnp.int32, (PATCHES, PATCHES), 0)
    return (keep[image : image + 1] == patch).astype(F32).astype(BF16)


def images_of(g):
    per = LIVE // PATCHES
    return [(g * per + m, m * PATCHES) for m in range(per)]


def live_rows(count, image):
    row = lax.broadcasted_iota(jnp.int32, (PATCHES, D), 0)
    return row < count[image]


def attend(x, q_bias, v_bias, wqkv, wout, counts, keep_parts):
    width = wout.shape[0]
    triple = dot(x, wqkv[...])
    q = (triple[:, :width] + q_bias).astype(BF16)
    k = triple[:, width : 2 * width].astype(BF16)
    v = (triple[:, 2 * width :] + v_bias).astype(BF16)
    keep_parts(0, q, k, v)
    lane = lax.broadcasted_iota(jnp.int32, (1, ROWS), 1)
    image = lane // PATCHES
    count = counts[LIVE - ROWS + 16 : LIVE - ROWS + 17]
    fits = (lane - image * PATCHES).astype(F32) < count
    row = lax.broadcasted_iota(jnp.int32, (ROWS, ROWS), 0)
    col = lax.broadcasted_iota(jnp.int32, (ROWS, ROWS), 1)
    same = jnp.minimum(row // PATCHES, 2) == col // PATCHES
    veil = jnp.where(same, 0.0, -1e30) + jnp.where(fits, 0.0, -1e30)
    mixed = jnp.zeros((ROWS, width), F32)
    for h in range(width // HEAD):
        mask = head_mask(h, width)
        scores = dot(q * mask, k, 1, 1) * SCALE + veil
        peak = jnp.max(scores, axis=-1, keepdims=True)
        raised = jnp.exp(scores - peak)
        weight = raised * (1.0 / jnp.sum(raised, axis=-1, keepdims=True))
        rounded = weight.astype(BF16)
        keep_parts(1 + h, rounded)
        mixed = mixed + dot(rounded, v * mask)
    return mixed.astype(BF16)


def erf_parts(pre):
    cdf = 0.5 * (1.0 + lax.erf(pre * (0.5 ** 0.5)))
    pdf = jnp.exp(-0.5 * pre * pre) * 0.3989422804014327
    return cdf, pdf


VM = pl.BlockSpec(memory_space=pltpu.VMEM)
HB = pl.BlockSpec(memory_space=pl.ANY)


def sds(shape, dtype):
    return jax.ShapeDtypeStruct(shape, dtype)


def params(n):
    return pltpu.CompilerParams(
        collective_id=n, has_side_effects=True, vmem_limit_bytes=67043328
    )


def column_sums(values):
    return jnp.sum(values, axis=0, keepdims=True)


class Scatter:
    order = (3, 1, 2, 0)

    def __init__(self, made, halves, arrivals, totals, outs, sems):
        self.made, self.halves, self.arrivals = made, halves, arrivals
        self.totals, self.outs = totals, outs
        self.x_sem, self.z_sem, self.out_sem, self.x_free, self.z_free = sems
        me = lax.axis_index("dp")
        self.x, self.z = me % 2, me // 2
        self.across = me + 1 - 2 * self.x
        self.near = self.z + 1 - 2 * (self.z % 2)
        self.far = (self.z + 2) % 4

    def device(self, z):
        return 2 * z + self.x

    def shard(self, k):
        return (self.z, self.near, self.far, (self.near + 2) % 4)[k]

    def number(self, j):
        third = (self.near + 2) % 4
        return jnp.where(
            j < 2, jnp.where(j == 0, third, self.near), jnp.where(j == 2, self.far, self.z)
        )

    def over_x(self, kind, part, j):
        n = self.number(j)
        return to_peer(
            "dp",
            self.made[kind][part].at[1 - self.x, n],
            self.halves[kind][part].at[n],
            self.x_sem.at[kind, part, j, 0],
            self.x_sem.at[kind, part, j, 1],
            self.across,
        )

    def over_z(self, kind, part, k):
        there, slot = {1: (self.near, 0), 3: (self.near, 1), 2: (self.far, 2)}[k]
        return to_peer(
            "dp",
            self.made[kind][part].at[self.x, self.shard(k)],
            self.arrivals[kind][part].at[slot],
            self.z_sem.at[kind, part, slot, 0],
            self.z_sem.at[kind, part, slot, 1],
            self.device(there),
        )

    def ready(self, s, part):
        if s >= 2:
            for j in range(4):
                self.over_x(s % 2, part, j).wait_send()
            for k in (1, 2, 3):
                self.over_z(s % 2, part, k).wait_send()

    def send(self, s, part, j):
        if s >= 2:
            pl.semaphore_wait(self.x_free.at[s % 2, part], 1)
        self.over_x(s % 2, part, j).start()

    def signal(self, sem, device):
        pl.semaphore_signal(
            sem, inc=1, device_id={"dp": device}, device_id_type=pl.DeviceIdType.MESH
        )

    def sum_rows(self, out, terms):
        def one(i, _):
            at = pl.ds(pl.multiple_of(i * COLS, COLS), COLS)
            value = terms[0][at, :].astype(F32)
            for term in terms[1:]:
                value = value + term[at, :].astype(F32)
            out[at, :] = value.astype(out.dtype)
            return 0

        lax.fori_loop(0, out.shape[0] // COLS, one, 0)

    def take(self, s, part, k):
        kind = s % 2
        mine = self.made[kind][part].at[self.x, self.shard(k)]
        terms = [mine, self.halves[kind][part].at[self.shard(k)]]
        self.over_x(kind, part, self.order.index(k)).wait_recv()
        if k == 2:
            self.over_z(kind, part, 3).wait_recv()
            terms.append(self.arrivals[kind][part].at[1])
        if k == 0:
            if s >= 2:
                self.store(s - 2, part, wait=True)
            mine = self.totals[kind][part]
        self.sum_rows(mine, terms)
        if s < 2:
            self.signal(self.x_free.at[kind, part], self.across)
            if k == 2:
                self.signal(self.z_free.at[kind, part, 1], self.device(self.near))
        if k:
            if s >= 2:
                slot = {1: 0, 3: 1, 2: 2}[k]
                pl.semaphore_wait(self.z_free.at[kind, part, slot], 1)
            self.over_z(kind, part, k).start()

    def store(self, s, part, wait=False):
        kind, n = s % 2, LAYERS - 1 - s // 2
        total, out = self.totals[kind][part], self.outs[kind][part]
        if kind == 1 and part == 1:
            width = out.shape[-1]
            pairs = [(total.at[:, pl.ds(c * width, width)], out.at[n, c]) for c in range(3)]
        else:
            pairs = [(total, out.at[n])]
        for c, pair in enumerate(pairs):
            copy = pltpu.make_async_copy(*pair, self.out_sem.at[kind, part, c])
            if wait:
                copy.wait()
            else:
                copy.start()

    def finish(self, s, part):
        kind = s % 2
        total, arrivals = self.totals[kind][part], self.arrivals[kind][part]
        self.over_z(kind, part, 1).wait_recv()
        self.over_z(kind, part, 2).wait_recv()
        self.sum_rows(total, [total, arrivals.at[0], arrivals.at[2]])
        self.store(s, part)
        if s < 2:
            self.signal(self.z_free.at[kind, part, 0], self.device(self.near))
            self.signal(self.z_free.at[kind, part, 2], self.device(self.far))

    def end(self):
        for s in (2, 3):
            for part in range(2):
                self.ready(s, part)
                self.store(s, part, wait=True)


def to_peer(axis, src, dst, send, recv, peer):
    return pltpu.make_async_remote_copy(
        src_ref=src,
        dst_ref=dst,
        send_sem=send,
        recv_sem=recv,
        device_id={axis: peer},
        device_id_type=pl.DeviceIdType.MESH,
    )


class SmallSum:
    def __init__(self, lines, arrived, over_z, out, sem, sc, mine):
        self.lines, self.arrived, self.over_z, self.out = lines, arrived, over_z, out
        self.sem, self.sc, self.mine = sem, sc, mine

    def across(self):
        s = self.sem
        return to_peer("dp", self.lines, self.arrived, s.at[0, 0], s.at[1, 0], self.sc.across)

    def along(self, k):
        part, s = self.over_z.at[self.sc.z], self.sem
        return to_peer("dp", part, part, s.at[0, k], s.at[1, k], self.sc.device((self.sc.z + k) % 4))

    def around(self, k):
        part, s = self.out.at[self.mine], self.sem
        peer = (self.mine + k) % 4
        return to_peer("tensor", part, part, s.at[0, 3 + k], s.at[1, 3 + k], peer)

    def second(self):
        self.across().wait()
        self.over_z[self.sc.z] = self.lines[...] + self.arrived[...]
        for k in range(1, 4):
            self.along(k).start()

    def third(self):
        for k in range(1, 4):
            self.along(k).wait()
        z = self.over_z
        self.out[self.mine] = z[0] + z[1] + z[2] + z[3]
        for k in range(1, 4):
            self.around(k).start()

    def last(self):
        for k in range(1, 4):
            self.around(k).wait()


def step_kernel(
    fused,
    count, patches, cot, keep, gains, shifts, bias_qv, bias_fc1, wqkv_h, wout_h, w1_h, w2_h,
    layer_h, patch_h, small_out, o_fc2, o_fc1, o_out, o_qkv,
    flow_h, gath_h, qkv_h, prob_h, att_h, gmlp_h, act_h, slope_h,
    gath, part, out_po, out_pd, out_y, in_po, in_pd, in_y, edge_out, edge_in, ex_sem,
    gradient, source, final, late_y, wqkv, wout, w1, w2,
    qkv, prob, att, norm_a, act, slope, norm_m,
    pre, triple, lines, cols_m, rows_m, cols_a, rows_a, load_sem, keep_sem, flow_sem, *rest,
):
    bufs = (out_po, out_pd, out_y, in_po, in_pd, in_y)
    ex = Exchange(gath, part, bufs, slope, late_y, (edge_out, edge_in), ex_sem)
    width, hidden = wout.shape[0], w1.shape[1]
    stages = 2 * LAYERS
    flat = 8 * ROWS
    made = ((cols_m, rows_m), (cols_a, rows_a))
    outs = ((o_fc2, o_fc1), (o_out, o_qkv))
    if fused:
        halves, arrivals, totals = (
            ((rest[4 * n], rest[4 * n + 1]), (rest[4 * n + 2], rest[4 * n + 3])) for n in range(3)
        )
        small_in, small_z, small_sem = rest[12:15]
        sc = Scatter(made, halves, arrivals, totals, outs, rest[15:20])
    else:
        sc = None
        save_sem = rest[0]

    def layer(s):
        return LAYERS - 1 - s // 2

    def loads(s):
        n = layer(s)
        if s < 2:
            return []
        if s % 2 == 0:
            pairs = (
                (w2_h.at[n], w2),
                (slope_h, slope),
                (w1_h.at[n], w1),
                (act_h, act),
                (gmlp_h, norm_m),
                (flow_h.at[1], source.at[0]),
            )
        else:
            pairs = tuple(
                (wqkv_h.at[n, c], wqkv.at[:, pl.ds(c * width, width)]) for c in range(3)
            ) + (
                (wout_h.at[n], wout),
                (qkv_h, qkv),
                (prob_h, prob),
                (att_h, att),
                (gath_h, norm_a),
                (flow_h.at[0], source.at[1]),
            )
        return [
            pltpu.make_async_copy(*pair, load_sem.at[s % 2, m]) for m, pair in enumerate(pairs)
        ]

    def forward_loads(s):
        n = s // 2
        if s % 2 == 0:
            pairs = [
                (wqkv_h.at[n, c], wqkv.at[:, pl.ds(c * width, width)]) for c in range(3)
            ] + [(wout_h.at[n], wout)]
        else:
            pairs = [(w1_h.at[n], w1), (w2_h.at[n], w2)]
        return [
            pltpu.make_async_copy(*pair, load_sem.at[s % 2, m]) for m, pair in enumerate(pairs)
        ]

    for s in range(2):
        for copy in forward_loads(s):
            copy.start()
    barrier = pltpu.get_barrier_semaphore()
    peers = [{"tensor": ex.mate}, {"tensor": ex.far}]
    if fused:
        peers += [{"tensor": ex.diag}, {"dp": sc.across}]
        peers += [{"dp": sc.device((sc.z + k) % 4)} for k in range(1, 4)]
    for peer in peers:
        pl.semaphore_signal(barrier, inc=1, device_id=peer, device_id_type=pl.DeviceIdType.MESH)

    def note(at, g, row):
        lines[at : at + 1] = row if g == 0 else lines[at : at + 1] + row

    def hold(s):
        return source.at[(s + 1) % 2]

    def save_flow(s, g):
        return pltpu.make_async_copy(hold(s).at[g], flow_h.at[s, g], flow_sem.at[s, g])

    def begin(s, g):
        n = s // 2
        held = hold(s)
        if s >= 2:
            save_flow(s - 2, g).wait()
        if s == 0:
            for image, at in images_of(g):
                held[g, at : at + PATCHES] = dot(picker(keep, image), patches[image], 0, 0)
            held[g, LIVE:] = jnp.zeros((ROWS - LIVE, D), F32)
            value = held[g]
        else:
            shift = shifts[(s - 1) // 2, 2 + (s - 1) % 2].reshape(1, D)
            value = hold(s - 1)[g] + ex.total(g) + shift
            held[g] = value
        if s < 2:
            save_flow(s, g).start()
        unit, _ = norm_parts(value)
        gain, shift = gains[n, s % 2].reshape(1, D), shifts[n, s % 2].reshape(1, D)
        own = ex.own(g)
        ex.clear(g)
        gath[s % 2, own] = (unit * gain + shift).astype(BF16)
        tail = gath[s % 2, own, ROWS - 16 : ROWS, 0:256].astype(F32)
        row = lax.broadcasted_iota(jnp.int32, (16, 256), 0)
        lane = lax.broadcasted_iota(jnp.int32, (16, 256), 1)
        for image, at in images_of(g):
            here = (row == LIVE - ROWS + 16) & (lane >= at)
            tail = jnp.where(here, count[image].astype(F32), tail)
        gath[s % 2, own, ROWS - 16 : ROWS, 0:256] = tail.astype(BF16)
        if s == 0 and g == 0:
            pl.semaphore_wait(barrier, len(peers))
        ex.share(g)
        if s < stages - 1:
            return
        gradient[g, LIVE:] = jnp.zeros((ROWS - LIVE, D), F32)
        for image, at in images_of(g):
            piece = jnp.where(live_rows(count, image), cot[image].astype(F32), 0.0)
            gradient[g, at : at + PATCHES] = piece
        rounded = gradient[g].astype(BF16)
        note(4 + 4 * n + 3, g, column_sums(rounded.astype(F32)))
        gath[0, own] = rounded
        ex.set_edge(2, g, gath[0, own, MOST:ROWS])
        ex.send(14, g)
        ex.send(6, g)
        ex.send(7, g)

    def saves(s, slot):
        if s == 0:
            pairs = (
                (gath.at[0, slot], gath_h),
                (qkv.at[slot], qkv_h),
                (prob.at[slot], prob_h),
                (att.at[slot], att_h),
            )
        elif s == 1:
            pairs = ((gath.at[1, slot], gmlp_h), (act.at[slot], act_h), (slope.at[slot], slope_h))
        else:
            pairs = ()
        return [
            pltpu.make_async_copy(a, b.at[slot], keep_sem.at[m, slot])
            for m, (a, b) in enumerate(pairs)
        ]

    def drain(s):
        def one(slot, _):
            for copy in saves(s, slot):
                copy.wait()
            return 0

        lax.fori_loop(0, 8, one, 0)

    def own_total(g, value):
        final[g] = source[0, g] + value + shifts[LAYERS - 1, 3].reshape(1, D)

    lines[15:16] = jnp.zeros((1, D), F32)
    for s in range(stages):
        n = s // 2
        ex.stage = s
        begin(s, 0)
        if s == 0:
            begin(s, 1)
        elif s <= 2:
            drain(s - 1)
        for copy in forward_loads(s):
            copy.wait()
        if 1 <= s < stages - 1:
            for copy in forward_loads(s + 1):
                copy.start()

        def step(i, _, s=s, n=n):
            if s:

                @pl.when(i == 2)
                def _():
                    begin(s, 1)

            both = s == stages - 1
            (ex.before_both if both else ex.before)(i)
            slot = ex.slot(i)
            x = gath[s % 2, slot]
            if s >= 2:
                (norm_a, norm_m)[s % 2][slot] = x
            if s % 2 == 0:

                def keep_parts(kind, *values):
                    if kind == 0:
                        for c, value in enumerate(values):
                            qkv[slot, :, c * width : (c + 1) * width] = value
                    else:
                        prob[slot, (kind - 1) * ROWS : kind * ROWS] = values[0]

                tail = gath[0, slot, ROWS - 16 : ROWS, 0:256][:, 0:ROWS].astype(F32)
                mixed = attend(
                    x, bias_qv[n, 0:1], bias_qv[n, 1:2], wqkv, wout, tail, keep_parts
                )
                att[slot] = mixed
                part[ex.place(i)] = dot(mixed, wout[...])
            else:
                for block in range(hidden // 256):
                    at = slice(block * 256, block * 256 + 256)
                    pre_act = dot(x, w1[:, at]) + bias_fc1[n : n + 1, at]
                    cdf, pdf = erf_parts(pre_act)
                    act[slot, :, at] = (pre_act * cdf).astype(BF16)
                    steep = cdf + pre_act * pdf
                    if both:
                        d_act = dot(gath[0, slot], w2[at, :], 1, 1)
                        pre[slot, :, at] = (d_act * steep).astype(BF16)
                    else:
                        slope[slot, :, at] = steep.astype(BF16)
                value = dot(act[slot], w2[...])
                if both:
                    ex.set_aside(i, value, own_total)
                    value = dot(pre[slot], w1[...], 1, 1)
                part[ex.place(i)] = value
            for copy in saves(s, slot):
                copy.start()
            ex.after(i)
            return 0

        lax.fori_loop(0, 8, step, 0)

    def complete_output():
        for g in range(GROUPS):
            ex.copy(11, g).wait_recv()
            final[g] = final[g] + in_pd[g].astype(F32)
            pltpu.make_async_copy(final.at[g], layer_h.at[g], flow_sem.at[1, g]).start()

    def produce(s, g):
        n, side = layer(s - 1), s % 2
        gain = gains[n, side].reshape(1, D)
        moved = ex.total(g)
        unit, scale = norm_parts(source[1 - side, g])
        note(2 * n + side, g, column_sums(moved * unit))
        note(4 + 4 * n + side, g, column_sums(moved))
        scaled = moved * gain
        lean = jnp.mean(scaled, axis=-1, keepdims=True)
        tilt = jnp.mean(scaled * unit, axis=-1, keepdims=True)
        grad = gradient[g] + scale * (scaled - lean - unit * tilt)
        rounded = grad.astype(BF16)
        if s < stages:
            gradient[g] = grad
        else:
            gradient[g] = grad
            for image, at in images_of(g):
                exact = gradient[g, at : at + PATCHES]
                high = exact.astype(BF16)
                low = (exact - high.astype(F32)).astype(BF16)
                pick = picker(keep, image)
                source[0, g, at : at + PATCHES] = dot(pick, high) + dot(pick, low)
            pltpu.make_async_copy(source.at[0, g], patch_h.at[g], flow_sem.at[0, g]).start()
            return
        if s % 2 == 0:
            note(4 + 4 * layer(s) + 3, g, column_sums(rounded.astype(F32)))
        else:
            note(4 + 4 * layer(s) + 2, g, column_sums(rounded.astype(F32)))
        ex.clear(g)
        gath[s % 2, ex.own(g)] = rounded
        ex.share(g)

    def spill(s, part, k):
        return [
            pltpu.make_async_copy(
                made[s % 2][part].at[half, k],
                outs[s % 2][part].at[layer(s), half, k],
                save_sem.at[s % 2, part, k, half],
            )
            for half in range(2)
        ]

    def column_block(s, j):
        n = sc.number(j) if fused else j
        at = pl.ds(pl.multiple_of(n * 256, 256), 256)
        some = gath[s % 2, :, :, at].reshape(flat, 256)
        left = (act, att)[s % 2]
        wide = dot(left[...].reshape(flat, left.shape[-1]), some, 0, 0).astype(BF16)
        out = made[s % 2][0]
        out[0, n] = wide[:, :COLS]
        out[1, n] = wide[:, COLS:]
        if fused:
            if s < stages - 1:
                sc.send(s, 0, j)
        else:
            for copy in spill(s, 0, j):
                copy.start()

    def row_block(s, j):
        n = sc.number(j) if fused else j
        at = pl.ds(pl.multiple_of(n * 256, 256), 256)
        left, right = ((norm_m, pre), (norm_a, triple))[s % 2]
        some = left[:, :, at].reshape(flat, 256)
        tall = dot(some, right[...].reshape(flat, right.shape[-1]), 0, 0).astype(BF16)
        out = made[s % 2][1]
        out[0, n] = tall[:COLS]
        out[1, n] = tall[COLS:]
        if fused:
            if s < stages - 1:
                sc.send(s, 1, j)
        else:
            for copy in spill(s, 1, j):
                copy.start()

    def settle(s, part):
        if fused:
            sc.ready(s, part)
        elif s >= 2:
            for k in range(4):
                for copy in spill(s - 2, part, k):
                    copy.wait()

    def columns(s):
        settle(s, 0)

        def one(j, _):
            column_block(s, j)
            return 0

        lax.fori_loop(0, 4, one, 0)

    def some_rows(s, start, count):
        def one(j, _):
            row_block(s, start + j)
            return 0

        lax.fori_loop(0, count, one, 0)

    def bias_sums(s):
        n = layer(s)
        ones = jnp.ones((8, flat), BF16)
        if s % 2 == 0:
            lines[12 + n : 13 + n] = dot(ones, pre[...].reshape(flat, hidden))[0:1]
        else:
            sums = dot(ones, triple[...].reshape(flat, 3 * width))[0:1]
            at = 2 * n * width
            lines[14:15, at : at + width] = sums[:, :width]
            lines[14:15, at + width : at + 2 * width] = sums[:, 2 * width :]

    def take(*work):
        def run():
            if fused:
                for s, part, k in work:
                    if k == 4:
                        sc.finish(s, part)
                    else:
                        sc.take(s, part, k)

        return run

    plan = {
        (1, 4): take((0, 0, 3)),
        (1, 6): take((0, 0, 1)),
        (1, 8): take((0, 0, 2)),
        (2, 2): take((0, 0, 0), (0, 1, 3)),
        (2, 4): take((0, 1, 1)),
        (2, 6): take((0, 1, 2)),
        (2, 8): take((0, 1, 0), (0, 0, 4), (1, 0, 3), (1, 0, 1)),
        (3, 2): take((1, 0, 2), (1, 0, 0), (1, 1, 3), (1, 1, 1)),
        (3, 4): take((0, 1, 4), (1, 1, 2)),
        (3, 6): take((1, 1, 0), (2, 0, 3), (2, 0, 1)),
        (3, 8): take((2, 0, 2), (1, 0, 4), (1, 1, 4)),
    }

    for s in range(1, stages):
        ex.stage = stages + s
        columns(s - 1)
        if s == 1:
            for g in range(GROUPS):
                for kind in (6, 7, 8, 14):
                    ex.copy(kind, g).wait_send()
                ex.copy(9, g).wait()
                ex.copy(10, g).wait_send()
                final[g] = final[g] + ex.spare[2 + g].astype(F32)
        produce(s, 0)
        early = (3, 6)[s % 2]
        for copy in loads(s)[:early]:
            copy.wait()

        def step(i, _, s=s):
            if s:

                @pl.when(i == 2)
                def _():
                    settle(s - 1, 1)

                @pl.when(i == 2)
                def _():
                    some_rows(s - 1, 0, 4)

            @pl.when(i == 2)
            def _():
                produce(s, 1)

            if s:

                @pl.when(i == 6)
                def _():
                    bias_sums(s - 1)
                    if s + 1 < stages:
                        for copy in loads(s + 1) if s >= 1 else ():
                            copy.start()

            for (stage, at), task in plan.items():
                if stage == s and at < 8:
                    pl.when(i == at)(task)
            ex.before(i)
            slot = ex.slot(i)
            grad = gath[s % 2, slot]
            if s % 2 == 0:
                for block in range(hidden // 256):
                    at = slice(block * 256, block * 256 + 256)
                    d_act = dot(grad, w2[at, :], 1, 1)
                    pre[slot, :, at] = (d_act * slope[slot, :, at].astype(F32)).astype(BF16)
                part[ex.place(i)] = dot(pre[slot], w1[...], 1, 1)
            else:
                d_att = dot(grad, wout[...], 1, 1).astype(BF16)
                q = qkv[slot, :, 0:width]
                k = qkv[slot, :, width : 2 * width]
                v = qkv[slot, :, 2 * width :]
                d_q = jnp.zeros((ROWS, width), F32)
                d_k = jnp.zeros((ROWS, width), F32)
                d_v = jnp.zeros((ROWS, width), F32)
                for h in range(width // HEAD):
                    mask = head_mask(h, width)
                    d_one = d_att * mask
                    rounded = prob[slot, h * ROWS : (h + 1) * ROWS]
                    weight = rounded.astype(F32)
                    d_prob = dot(d_one, v, 1, 1)
                    centre = jnp.sum(weight * d_prob, axis=-1, keepdims=True)
                    d_scores = (weight * (d_prob - centre)).astype(BF16)
                    d_q = d_q + dot(d_scores, k * mask)
                    d_k = d_k + dot(d_scores, q * mask, 0, 0)
                    d_v = d_v + dot(rounded, d_one, 0, 0)
                triple[slot, :, 0:width] = (d_q * SCALE).astype(BF16)
                triple[slot, :, width : 2 * width] = (d_k * SCALE).astype(BF16)
                triple[slot, :, 2 * width :] = d_v.astype(BF16)
                part[ex.place(i)] = dot(triple[slot], wqkv[...], 1, 1)
            ex.after(i)
            return 0

        lax.fori_loop(0, 8, step, 0)
        for copy in loads(s)[early:]:
            copy.wait()
        if (s, 8) in plan:
            plan[s, 8]()
    last = stages - 1
    columns(last)
    settle(last, 1)
    some_rows(last, 0, 4)
    bias_sums(last)
    take((2, 0, 0), (2, 1, 3))()
    for g in range(GROUPS):
        produce(stages, g)
    for g in range(GROUPS):
        ex.send(11, g)
    if fused:
        tiny = SmallSum(lines, small_in, small_z, small_out, small_sem, sc, ex.me)
        tiny.across().start()
        for side in (1, 0):
            for j in range(4):
                sc.send(last, side, j)
        take((2, 1, 1), (2, 0, 4), (2, 1, 2), (2, 1, 0))()
        complete_output()
        tiny.second()
        take((2, 1, 4), (3, 1, 3), (3, 1, 1))()
        tiny.third()
        take((3, 1, 2), (3, 1, 0), (3, 0, 3), (3, 0, 1), (3, 0, 2), (3, 1, 4), (3, 0, 0), (3, 0, 4))()
        sc.end()
        tiny.last()
    else:
        complete_output()
        small_out[...] = lines[...]
        for s in (2, 3):
            for side in range(2):
                for k in range(4):
                    for copy in spill(s, side, k):
                        copy.wait()
    ex.end()
    for g in range(GROUPS):
        pltpu.make_async_copy(source.at[0, g], patch_h.at[g], flow_sem.at[0, g]).wait()
        pltpu.make_async_copy(final.at[g], layer_h.at[g], flow_sem.at[1, g]).wait()


def run_step(fused, count, patches, cot, keep, gains, shifts, bias_qv, bias_fc1, wqkv, wout, w1, w2):
    width, hidden = wout.shape[1], w1.shape[2]
    heads = width // HEAD
    wide, own = (8, ROWS, D), (GROUPS, ROWS, D)
    dma = pltpu.SemaphoreType.DMA
    tall = D // 256
    mine = ((hidden, COLS), (COLS, hidden), (width, COLS), (COLS, 3 * width))
    blocks = [(2, tall) + m for m in mine]
    if fused:
        outs = [
            sds((LAYERS, hidden, COLS), F32),
            sds((LAYERS, COLS, hidden), F32),
            sds((LAYERS, width, COLS), F32),
            sds((LAYERS, 3, COLS, width), F32),
        ]
        small = sds((4, 16, D), F32)
        regular = pltpu.SemaphoreType.REGULAR
        more = (
            [pltpu.VMEM((4,) + m, BF16) for m in mine]
            + [pltpu.VMEM((3,) + m, BF16) for m in mine]
            + [pltpu.VMEM(m, F32) for m in mine]
            + [pltpu.VMEM((16, D), F32), pltpu.VMEM((4, 16, D), F32), dma((2, 7))]
            + [dma((2, 2, 4, 2)), dma((2, 2, 3, 2)), dma((2, 2, 3))]
            + [regular((2, 2)), regular((2, 2, 3))]
        )
    else:
        outs = [sds((LAYERS,) + b, BF16) for b in blocks]
        small = sds((16, D), F32)
        more = [dma((2, 2, 4, 2))]
    inner = ((8, ROWS, 3 * width), (8, heads * ROWS, ROWS), (8, ROWS, width))
    mlp = ((8, ROWS, hidden), (8, ROWS, hidden))
    saved = (wide,) + inner + (wide,) + mlp
    return pl.pallas_call(
        partial(step_kernel, fused),
        out_shape=[sds(own, F32), sds(own, F32), small]
        + outs
        + [sds((2,) + own, F32)]
        + [sds(k, BF16) for k in saved],
        in_specs=[pl.BlockSpec(memory_space=pltpu.SMEM)] + [VM] * 7 + [HB] * 4,
        out_specs=[HB] * 2 + [VM] + [HB] * 12,
        scratch_shapes=exchange_scratch()
        + [
            pltpu.VMEM(own, F32),
            pltpu.VMEM((2,) + own, F32),
            pltpu.VMEM(own, F32),
            pltpu.VMEM(own, BF16),
            pltpu.VMEM((D, 3 * width), BF16),
            pltpu.VMEM((width, D), BF16),
            pltpu.VMEM((D, hidden), BF16),
            pltpu.VMEM((hidden, D), BF16),
        ]
        + [pltpu.VMEM(k, BF16) for k in inner + (wide,) + mlp + (wide,)]
        + [pltpu.VMEM((8, ROWS, hidden), BF16), pltpu.VMEM((8, ROWS, 3 * width), BF16)]
        + [pltpu.VMEM((16, D), F32)]
        + [pltpu.VMEM(b, BF16) for b in blocks]
        + [dma((2, 9)), dma((4, 8)), dma((2, GROUPS))]
        + more,
        compiler_params=params(1),
    )(count, patches, cot, keep, gains, shifts, bias_qv, bias_fc1, wqkv, wout, w1, w2)[:7]


def deliver_kernel(
    count, layer, patch, small, a_h, b_h, c_h, d_h,
    layer_out, patch_out, gain, shift, qv, fc1, a_out, b_out, c_out, d_out,
    a, b, c, d, sems,
):
    held = ((a_h, a, a_out), (b_h, b, b_out), (c_h, c, c_out), (d_h, d, d_out))

    def inward(n):
        return pltpu.make_async_copy(held[n][0], held[n][1], sems.at[0, n])

    def outward(n):
        return pltpu.make_async_copy(held[n][1], held[n][2], sems.at[1, n])

    for n in range(4):
        inward(n).start()
    for g in range(GROUPS):
        for image, at in images_of(g):
            rows = layer[g, at : at + PATCHES]
            layer_out[image] = jnp.where(live_rows(count, image), rows, 0.0)
            patch_out[image] = patch[g, at : at + PATCHES]
    for n in range(4):
        inward(n).wait()
        outward(n).start()
    summed = small[0, 0:12] + small[1, 0:12] + small[2, 0:12] + small[3, 0:12]
    for n in range(LAYERS):
        gain[n] = summed[2 * n : 2 * n + 2]
        shift[n] = summed[4 + 4 * n : 8 + 4 * n]
        for t in range(4):
            hidden = fc1.shape[1] // 4
            fc1[n : n + 1, t * hidden : (t + 1) * hidden] = small[t, 12 + n : 13 + n]
            width = D // 4
            for side in range(2):
                at = (2 * n + side) * width
                piece = small[t, 14:15, at : at + width]
                qv[n, side : side + 1, t * width : (t + 1) * width] = piece
    for n in range(4):
        outward(n).wait()


def deliver(count, layer, patch, small, grads):
    images = (GROUPS * LIVE // PATCHES, PATCHES, D)
    shapes = [g.shape for g in grads]
    return pl.pallas_call(
        deliver_kernel,
        out_shape=[
            sds(images, F32),
            sds(images, F32),
            sds((LAYERS, 2, D), F32),
            sds((LAYERS, 4, D), F32),
            sds((LAYERS, 2, D), F32),
            sds((LAYERS, FF), F32),
        ]
        + [sds(s, F32) for s in shapes],
        in_specs=[pl.BlockSpec(memory_space=pltpu.SMEM)] + [VM] * 3 + [HB] * 4,
        out_specs=[VM] * 6 + [HB] * 4,
        scratch_shapes=[pltpu.VMEM(s, F32) for s in shapes] + [pltpu.SemaphoreType.DMA((2, 4))],
    )(count, layer, patch, small, *grads)


def from_groups(array):
    return array[:, :LIVE].reshape(GROUPS * (LIVE // PATCHES), PATCHES, D)


def collect_weight(partial_grad, split_dim):
    return lax.psum_scatter(
        partial_grad, "dp", scatter_dimension=split_dim, tiled=True
    ).astype(F32)


def join_rows(blocks):
    return jnp.transpose(blocks, (1, 0, 2, 3)).reshape(D, -1)


def join_columns(blocks):
    return jnp.transpose(blocks, (2, 1, 0, 3)).reshape(blocks.shape[2], -1)


def local(
    patches,
    keep_index,
    kept_count,
    norm_gain,
    shifts,
    w_qkv,
    bias_qv,
    w_out,
    w_fc1,
    bias_fc1,
    w_fc2,
    cotangent,
):
    width = w_qkv.shape[-1]
    hidden = w_fc1.shape[-1]
    dp_size, ways = lax.axis_size("dp"), lax.axis_size("tensor")
    assert ways == 4
    wqkv = jnp.transpose(w_qkv, (0, 2, 1, 3))
    fused = dp_size == 8 and hidden == D and 4 * width == D
    layer, patch, small, g_fc2, g_fc1, g_out, g_qkv = run_step(
        fused, kept_count, patches, cotangent, keep_index, norm_gain, shifts, bias_qv, bias_fc1,
        wqkv, w_out, w_fc1, w_fc2,
    )
    if fused:
        layer_out, grad_patches, gain, shift, qv, fc1, g_fc2, g_fc1, g_out, g_qkv = deliver(
            kept_count, layer, patch, small, (g_fc2, g_fc1, g_out, g_qkv)
        )
        grad_qkv = jnp.transpose(g_qkv, (0, 2, 1, 3))
        return layer_out, grad_patches, gain, shift, grad_qkv, qv, g_out, g_fc1, fc1, g_fc2
    slot_ids = jnp.arange(PATCHES, dtype=jnp.int32)
    own_mask = (slot_ids[None, :] < kept_count[:, None])[:, :, None]
    layer_out = from_groups(layer) * own_mask.astype(F32)
    grad_patches = from_groups(patch)
    grad_qkv, grad_out, grad_fc1, grad_fc2 = (
        jnp.stack([collect_weight(join(array[n]), split) for n in range(LAYERS)])
        for array, join, split in (
            (g_qkv, join_rows, 0),
            (g_out, join_columns, 1),
            (g_fc1, join_rows, 0),
            (g_fc2, join_columns, 1),
        )
    )
    grad_qkv = grad_qkv.reshape(LAYERS, -1, 3, width)
    small = lax.all_gather(lax.psum(small, "dp"), "tensor")
    summed = jnp.sum(small[:, :12], axis=0)
    grad_gain = summed[:4].reshape(LAYERS, 2, D)
    grad_shifts = summed[4:].reshape(LAYERS, 4, D)
    grad_bias_fc1 = jnp.transpose(small[:, 12:14], (1, 0, 2)).reshape(LAYERS, ways * hidden)
    quarters = small[:, 14, : 2 * LAYERS * width].reshape(ways, LAYERS, 2, width)
    grad_bias_qv = jnp.transpose(quarters, (1, 2, 0, 3)).reshape(LAYERS, 2, ways * width)
    return (
        layer_out,
        grad_patches,
        grad_gain,
        grad_shifts,
        grad_qkv,
        grad_bias_qv,
        grad_out,
        grad_fc1,
        grad_bias_fc1,
        grad_fc2,
    )


def solution(mesh):
    in_specs = (
        P(("dp", "tensor"), None, None),
        P(("dp", "tensor"), None),
        P(("dp", "tensor")),
        P(),
        P(),
        P(None, None, None, "tensor"),
        P(None, None, "tensor"),
        P(None, "tensor", None),
        P(None, None, "tensor"),
        P(None, "tensor"),
        P(None, "tensor", None),
        P(("dp", "tensor"), None, None),
    )
    out_specs = (
        P(("dp", "tensor"), None, None),
        P(("dp", "tensor"), None, None),
        P(),
        P(),
        P(None, "dp", None, "tensor"),
        P(),
        P(None, "tensor", "dp"),
        P(None, "dp", "tensor"),
        P(),
        P(None, "tensor", "dp"),
    )
    return jax.shard_map(local, mesh=mesh, in_specs=in_specs, out_specs=out_specs, check_vma=False)
```
